32 devices in a mesh: lvl: 2 (over x), lat: 4 (over z), lon: 4 (over y, core).
Axes of the slice: x: 2, y: 2, z: 4, core: 2. Of those that a mesh axis runs over, the one named last changes fastest.
Arguments:
- patches: bfloat16 [2, 2, 24, 48, 1000], P('lvl', None, 'lat', 'lon'), may hold values from -6 to 6
- level_embed: float32 [2, 512], P('lvl'), may hold values from -6 to 6
- embed_weight: bfloat16 [1000, 512], replicated, may hold values from -0.1875 to 0.1875
- block_ids: int32 [2, 2, 4, 4, 3], P('lvl', None, 'lat', 'lon'), may hold values from -1 to 5, as said below
- latent_queries: bfloat16 [4, 512], replicated, may hold values from -6 to 6
- cross_gain: float32 [512], replicated, may hold values from 0.1 to 1.9
- cross_query: bfloat16 [512, 512], replicated, may hold values from -0.25 to 0.25
- cross_kv: bfloat16 [512, 1024], replicated, may hold values from -0.25 to 0.25
- cross_out: bfloat16 [512, 512], replicated, may hold values from -0.25 to 0.25
- region_ids: int32 [48, 48], P(('lvl', 'lat'), 'lon'), may hold values from 0 to 2
- swin_gain: float32 [512], replicated, may hold values from 0.1 to 1.9
- swin_qkv: bfloat16 [512, 1536], replicated, may hold values from -0.25 to 0.25
- swin_out: bfloat16 [512, 512], replicated, may hold values from -0.25 to 0.25
- mlp_gain: float32 [512], replicated, may hold values from 0.1 to 1.9
- mlp_up: bfloat16 [512, 2048], replicated, may hold values from -0.25 to 0.25
- mlp_down: bfloat16 [2048, 512], replicated, may hold values from -0.125 to 0.125
Outputs:
- latents: float32 [4, 48, 48, 512], P(None, ('lvl', 'lat'), 'lon')
The draws below stay inside these ranges and needn't reach their ends.
Inputs may be any that keep to these rules, and one draw needn't show every extreme that they name: block_ids[l, m, a, o, :] lists the column blocks b (longitude column (m * 4 + a) * 6 + b, latitude rows o * 12 to o * 12 + 11) at which level l is present: distinct numbers in its first slots, -1 in the remaining slots. Every column block is named by the list of at least one level. For every band and tile, the list of some level fills all 3 slots.
All inputs are finite; a program needn't handle non-finite values.
Results may differ from the reference program's by a relative error of at most 0.005.
Values may be sent and summed in bfloat16 or wider, within the bound.
A program may use at most 64 MiB of HBM per device.

```python
import math
import jax
import jax.numpy as jnp
from jax import lax

D = 512
HEADS = 16
MLP = 2048
PF = 1000
LATENT = 4
WIN_LV = 2
WIN_LAT = 6
WIN_LON = 12
SH = 6
SW = 12
LEVELS = 2
BANDS = 2
LAT_TILES = 4
LON_TILES = 4
CAP = 3
NH = 48
NW = 48


def draw_block_ids(key, part):
    key_shuffle = jax.random.fold_in(key, 11)
    key_count = jax.random.fold_in(key, 12)
    key_full = jax.random.fold_in(key, 13)
    key_pick = jax.random.fold_in(key, 14)
    groups = (BANDS, LAT_TILES, LON_TILES)
    block_index = jnp.arange(SH, dtype=jnp.int32)
    shuffle = jax.random.randint(key_shuffle, groups + (SH,), 0, 1 << 20) * SH + block_index
    permuted = jnp.argsort(shuffle, axis=-1)
    position = jnp.argsort(permuted, axis=-1)
    duty_level = position % LEVELS
    level_index = jnp.arange(LEVELS, dtype=jnp.int32)
    required = (duty_level[None] == level_index[:, None, None, None, None]).astype(jnp.int32)
    need_count = jnp.sum(required, axis=-1)
    slot_count = jax.random.randint(key_count, need_count.shape, need_count, CAP + 1)
    full_level = jax.random.randint(key_full, groups, 0, LEVELS)
    slot_count = jnp.where(level_index[:, None, None, None] == full_level[None], CAP, slot_count)
    priority = jax.random.randint(key_pick, required.shape, 0, 1 << 20) * SH + block_index + required * (1 << 27)
    chosen = jnp.argsort(-priority, axis=-1)[..., :CAP].astype(jnp.int32)
    slot_index = jnp.arange(CAP, dtype=jnp.int32)
    return jnp.where(slot_index < slot_count[..., None], chosen, -1).astype(jnp.int32)


def plant(array, key, low, high):
    dims = array.shape
    place = [jax.random.randint(jax.random.fold_in(key, axis), (), 0, dims[axis]) for axis in range(len(dims))]
    array = array.at[tuple(place)].set(low)
    longest = dims.index(max(dims))
    place[longest] = (place[longest] + 1) % dims[longest]
    return array.at[tuple(place)].set(high)


def shard_levels(own_key, dims, cuts, smallest, high):
    loudness, own = 1.0, jax.random.fold_in(own_key, 6)
    for dim, blocks in cuts:
        draws = jnp.exp(jax.random.uniform(jax.random.fold_in(own, dim), (blocks,), jnp.float32, smallest / len(cuts), high / len(cuts)))
        loudness = loudness * jnp.repeat(draws, dims[dim] // blocks).reshape([-1 if axis == dim else 1 for axis in range(len(dims))])
    return loudness


def scatter_about(stream_key, dims, width, reach, split=(), kind=jnp.bfloat16):
    gain = shard_levels(stream_key, dims, split, -0.22, 0.18) if split else 1.0
    values = jax.random.normal(stream_key, dims, jnp.float32) * width * gain
    return jnp.minimum(jnp.maximum(values, -reach), reach).astype(kind)


def setup_inputs(seed: int = 0) -> dict:
    splits = jax.random.split(jax.random.key(seed), 17)
    return {
        "patches": scatter_about(splits[0], (LEVELS, BANDS, LAT_TILES * SH, NW, PF), 1.0, 6.0, ((0, 2), (2, 4), (3, 4))),
        "level_embed": scatter_about(splits[1], (LEVELS, D), 1.0, 6.0, ((0, 2),), jnp.float32),
        "embed_weight": scatter_about(splits[2], (PF, D), PF ** -0.5, 0.1875),
        "block_ids": draw_block_ids(jax.random.fold_in(splits[16], 71), 0),
        "latent_queries": scatter_about(splits[4], (LATENT, D), 1.0, 6.0),
        "cross_gain": jnp.clip(1.0 + 0.18 * jax.random.normal(splits[5], (D,), jnp.float32), 0.1, 1.9),
        "cross_query": scatter_about(splits[6], (D, D), D ** -0.5, 0.25),
        "cross_kv": scatter_about(splits[7], (D, 2 * D), D ** -0.5, 0.25),
        "cross_out": scatter_about(splits[8], (D, D), D ** -0.5, 0.25),
        "region_ids": plant(jax.random.randint(splits[9], (NH, NW), 0, 3), jax.random.fold_in(splits[9], 1), 0, 2).astype(jnp.int32),
        "swin_gain": jnp.clip(1.0 + 0.18 * jax.random.normal(splits[10], (D,), jnp.float32), 0.1, 1.9),
        "swin_qkv": scatter_about(splits[11], (D, 3 * D), D ** -0.5, 0.25),
        "swin_out": scatter_about(splits[12], (D, D), D ** -0.5, 0.25),
        "mlp_gain": jnp.clip(1.0 + 0.18 * jax.random.normal(splits[13], (D,), jnp.float32), 0.1, 1.9),
        "mlp_up": scatter_about(splits[14], (D, MLP), D ** -0.5, 0.25),
        "mlp_down": scatter_about(splits[15], (MLP, D), MLP ** -0.5, 0.125),
    }


def layer_norm(tensor, gain_vec):
    average = lax.optimization_barrier(jnp.mean(tensor, axis=-1, keepdims=True))
    centred = tensor - average
    spread = lax.optimization_barrier(jnp.mean(centred * centred, axis=-1, keepdims=True))
    return centred * lax.rsqrt(spread + 1e-05) * gain_vec

def to_windows(tensor, spans):
    trailing = tensor.shape[3:]
    level_span, row_span, col_span = tensor.shape[:3]
    first, second, third = spans
    shaped = tensor.reshape((level_span // first, first, row_span // second, second, col_span // third, third) + trailing)
    axes_order = (0, 2, 4, 1, 3, 5) + tuple(range(6, 6 + len(trailing)))
    return shaped.transpose(axes_order).reshape((level_span // first, row_span // second, col_span // third, first * second * third) + trailing)

def from_windows(tensor, extents, spans):
    trailing = tensor.shape[4:]
    level_span, row_span, col_span = extents
    first, second, third = spans
    shaped = tensor.reshape((level_span // first, row_span // second, col_span // third, first, second, third) + trailing)
    axes_order = (0, 3, 1, 4, 2, 5) + tuple(range(6, 6 + len(trailing)))
    return shaped.transpose(axes_order).reshape((level_span, row_span, col_span) + trailing)

def label_windows(labels, spans):
    row_span, col_span = labels.shape
    second, third = spans
    shaped = labels.reshape(row_span // second, second, col_span // third, third).transpose(0, 2, 1, 3)
    shaped = shaped.reshape(row_span // second, col_span // third, second * third)
    return jnp.concatenate([shaped] * WIN_LV, axis=-1)

def window_attend(queries, key_rows, value_rows, usable, labels):
    window_size = queries.shape[3]
    scores = jnp.einsum('abcqhe,abckhe->abchqk', queries.astype(jnp.float32), key_rows.astype(jnp.float32))
    same_label = labels[:, :, :, None] == labels[:, :, None, :]
    allowed = usable[:, :, :, None, None, :] & same_label[None, :, :, None, :, :]
    allowed = allowed | jnp.eye(window_size, dtype=jnp.bool_)
    exponent = jnp.where(allowed, jnp.exp(scores), jnp.zeros_like(scores))
    weights = (exponent / lax.optimization_barrier(jnp.sum(exponent, axis=-1, keepdims=True))).astype(jnp.bfloat16)
    mixture = jnp.einsum('abchqk,abckhe->abcqhe', weights.astype(jnp.float32), value_rows.astype(jnp.float32))
    return mixture.astype(jnp.bfloat16)

def reference(patches, level_embed, embed_weight, block_ids, latent_queries, cross_gain, cross_query, cross_kv, cross_out, region_ids, swin_gain, swin_qkv, swin_out, mlp_gain, mlp_up, mlp_down):
    head_dim = D // HEADS
    inv_root = 1.0 / math.sqrt(head_dim)
    band_rows = LAT_TILES * SH
    matches = jnp.any(block_ids[..., None] == jnp.arange(SH, dtype=jnp.int32), axis=4)
    matches = jnp.transpose(matches, (0, 1, 2, 4, 3)).reshape(LEVELS, BANDS, band_rows, LON_TILES)
    presence = jnp.repeat(matches.astype(jnp.float32), SW, axis=3)
    cross_queries = jnp.dot(latent_queries, cross_query, preferred_element_type=jnp.float32) * inv_root
    cross_queries = cross_queries.astype(jnp.bfloat16).reshape(LATENT, HEADS, head_dim)

    def one_band(inputs):
        band_patches, band_presence = inputs
        embedded = jnp.dot(band_patches.reshape(-1, PF), embed_weight, preferred_element_type=jnp.float32)
        embedded = embedded.reshape(LEVELS, band_rows, NW, D) + level_embed[:, None, None, :]
        embedded = embedded.astype(jnp.bfloat16)
        keys_in = layer_norm(embedded.astype(jnp.float32), cross_gain).astype(jnp.bfloat16)
        key_value = jnp.dot(keys_in.reshape(-1, D), cross_kv, preferred_element_type=jnp.float32).astype(jnp.bfloat16)
        key_value = key_value.reshape(LEVELS, band_rows, NW, 2, HEADS, head_dim)
        scores = jnp.einsum('qhe,lrche->qhlrc', cross_queries.astype(jnp.float32), key_value[:, :, :, 0].astype(jnp.float32))
        exponent = jnp.exp(scores) * band_presence[None, None]
        weights = (exponent / lax.optimization_barrier(jnp.sum(exponent, axis=2, keepdims=True))).astype(jnp.bfloat16)
        mixture = jnp.einsum('qhlrc,lrche->qrche', weights.astype(jnp.float32), key_value[:, :, :, 1].astype(jnp.float32))
        mixture = mixture.astype(jnp.bfloat16).reshape(-1, D)
        projected = jnp.dot(mixture, cross_out, preferred_element_type=jnp.float32).reshape(LATENT, band_rows, NW, D)
        return latent_queries.astype(jnp.float32)[:, None, None, :] + projected
    starts = lax.map(one_band, (jnp.moveaxis(patches, 1, 0), jnp.moveaxis(presence, 1, 0)))
    latent_start = jnp.moveaxis(starts, 0, 1).reshape(LATENT, NH, NW, D)
    normed = layer_norm(latent_start, swin_gain).astype(jnp.bfloat16)
    projected = jnp.dot(normed.reshape(-1, D), swin_qkv, preferred_element_type=jnp.float32)
    projected = projected.reshape(LATENT, NH, NW, 3, HEADS, head_dim)
    queries = (projected[:, :, :, 0] * inv_root).astype(jnp.bfloat16)
    key_rows = projected[:, :, :, 1].astype(jnp.bfloat16)
    value_rows = projected[:, :, :, 2].astype(jnp.bfloat16)
    level_pad = WIN_LV // 2
    col_margin = WIN_LAT // 2
    spans = (WIN_LV, WIN_LON, WIN_LAT)
    widths = ((level_pad, level_pad), (0, 0), (col_margin, col_margin), (0, 0), (0, 0))
    usable = jnp.pad(jnp.ones((LATENT, NH, NW), jnp.bool_), widths[:3])
    labels = jnp.pad(region_ids, ((0, 0), (col_margin, col_margin)))
    window_labels = label_windows(labels, (WIN_LON, WIN_LAT))
    inputs = (jnp.moveaxis(to_windows(jnp.pad(queries, widths), spans), 1, 0), jnp.moveaxis(to_windows(jnp.pad(key_rows, widths), spans), 1, 0), jnp.moveaxis(to_windows(jnp.pad(value_rows, widths), spans), 1, 0), jnp.moveaxis(to_windows(usable, spans), 1, 0), window_labels)

    def one_row(pieces):
        q_part, k_part, v_part, u_part, l_part = pieces
        return window_attend(q_part[:, None], k_part[:, None], v_part[:, None], u_part[:, None], l_part[None])[:, 0]
    mixture = jnp.moveaxis(lax.map(one_row, inputs), 0, 1)
    mixture = from_windows(mixture, (LATENT + 2 * level_pad, NH, NW + 2 * col_margin), spans)
    mixture = mixture[level_pad:level_pad + LATENT, :, col_margin:col_margin + NW]
    mixture = mixture.reshape(-1, D)
    attended = latent_start + jnp.dot(mixture, swin_out, preferred_element_type=jnp.float32).reshape(LATENT, NH, NW, D)
    mlp_in = layer_norm(attended, mlp_gain).astype(jnp.bfloat16).reshape(-1, D)
    hidden = jnp.dot(mlp_in, mlp_up, preferred_element_type=jnp.float32)
    activated = jax.nn.gelu(hidden, approximate=False).astype(jnp.bfloat16)
    lowered = jnp.dot(activated, mlp_down, preferred_element_type=jnp.float32).reshape(LATENT, NH, NW, D)
    return attended + lowered
```

```python
import functools
import math

import jax
import jax.numpy as jnp
import numpy as np
from jax import lax
from jax.experimental import pallas as pl
from jax.experimental.pallas import tpu as pltpu
from jax.sharding import PartitionSpec as P

HEADS = 16
WIN_LAT = 6
BLOCK = 16
CODE = 64
VMEM = 63700000
MESH = pl.DeviceIdType.MESH
F32 = jnp.float32
BF16 = jnp.bfloat16


def layer_norm(tensor, gain_vec):
    average = jnp.mean(tensor, axis=-1, keepdims=True)
    centred = tensor - average
    spread = jnp.mean(centred * centred, axis=-1, keepdims=True)
    return centred * lax.rsqrt(spread + 1e-05) * gain_vec


def mm(a, b):
    return jnp.dot(a, b, preferred_element_type=F32)


def mm_nt(a, b):
    return lax.dot_general(a, b, (((1,), (1,)), ((), ())), preferred_element_type=F32)


class Plan:
    def __init__(self, rows, cols, cap):
        self.rows, self.cols, self.cap = rows, cols, cap
        self.margin = WIN_LAT // 2
        per = (BLOCK - 1) // cap
        assert per >= self.margin and rows < CODE and rows * cols <= 128
        self.blocks = max(2, -(-cols // per))
        spread = [min(per, cols)]
        middle = cols - 2 * per
        assert middle >= 0
        groups = [list(range(per))]
        groups += [list(range(c, min(c + per, cols - per))) for c in range(per, cols - per, per)]
        groups += [list(range(cols - per, cols))]
        self.blocks = len(groups)
        self.tile_rows = self.blocks * BLOCK
        col_of = np.full((self.blocks, BLOCK), -1)
        for b, group in enumerate(groups):
            for k, c in enumerate(group):
                col_of[b, k * cap : (k + 1) * cap] = c
        self.col_of = col_of.reshape(-1)
        self.tiles = [(0, self.tile_rows), (self.tile_rows, self.tile_rows)]
        self.tiles += [(2 * self.tile_rows + k * BLOCK, BLOCK) for k in range(4)]
        self.wide_rows = 2 * self.tile_rows + 4 * BLOCK
        first, last = self.col_of[:BLOCK], self.col_of[-BLOCK:]
        parts = [self.col_of, self.col_of, last, last, first, first]
        row_code = np.concatenate(
            [np.where(p >= 0, (t * cols + p) * CODE, -100000) for t, p in enumerate(parts)]
        )
        lanes = -(-self.wide_rows // 128) * 128
        self.lanes = lanes
        self.row_code = np.full((8, lanes), -100000, np.int32)
        self.row_code[:, : self.wide_rows] = row_code
        m = self.margin
        spans = [range(cols), range(cols), range(cols - m, cols), range(cols - m, cols), range(m), range(m)]
        offset = [0, 0, -cols, -cols, cols, cols]
        cells = [(t, i, j, (j + offset[t] + m) // WIN_LAT) for t in range(6) for i in range(rows) for j in spans[t]]
        self.cells = np.array(cells)
        self.count = len(cells)
        self.own = rows * cols
        self.info = np.zeros((self.count, 128), np.int32)
        t, i, j, win = self.cells.T
        self.info[:, 0] = (t * cols + j) * CODE + i
        self.info[:, 1] = i * cols + j
        self.info[:, 2] = t
        self.win = (win[: self.own, None] == win[None, :]).astype(np.float32)


def send_kernel(plan, names, sizes, patches, level_embed, weight, ids, labels, *rest):
    big = rest[:7]
    out = rest[7]
    fast = rest[8:15]
    wbuf, buf, wsem, send, recv, local, fsem = rest[15:]
    rows, cols, cap = plan.rows, plan.cols, plan.cap
    levels, lat_count, lon_count = sizes
    width = weight.shape[1]
    load = pltpu.make_async_copy(weight, wbuf, wsem)
    load.start()
    fetch = [pltpu.make_async_copy(a, b, fsem.at[k]) for k, (a, b) in enumerate(zip(big, fast))]
    me_l, me_a, me_o = (lax.axis_index(name) for name in names)
    low_bit = lax.rem(me_a, 2)
    partner = me_a + 1 - 2 * low_bit
    lats = (me_a, partner)
    lons = {
        0: me_o,
        1: lax.rem(me_o + 1, lon_count),
        -1: lax.rem(me_o + lon_count - 1, lon_count),
    }
    moves = [
        (dm, da, do)
        for dm in range(levels)
        for da in (0, 1)
        for do in (0, -1, 1)
        if (dm, da, do) != (0, 0, 0)
    ]
    band_of = [lax.rem(me_l + dm, levels) for dm in range(levels)]
    barrier = pltpu.get_barrier_semaphore()
    for dm, da, do in moves:
        pl.semaphore_signal(
            barrier, inc=1, device_id=(band_of[dm], lats[da], lons[do]), device_id_type=MESH
        )

    tile_rows = plan.tile_rows
    row = lax.broadcasted_iota(jnp.int32, (tile_rows, 1), 0)
    col_of = jnp.full((tile_rows, 1), -1, jnp.int32)
    slot_of = jnp.full((tile_rows, 1), -1, jnp.int32)
    for r in range(tile_rows):
        pass
    in_block = jnp.bitwise_and(row, BLOCK - 1)
    base = jnp.zeros((tile_rows, 1), jnp.int32)
    for b in range(plan.blocks):
        start = int(plan.col_of[b * BLOCK])
        base = jnp.where((row >= b * BLOCK) & (row < (b + 1) * BLOCK), start, base)
    col_step = jnp.zeros((tile_rows, 1), jnp.int32)
    for k in range(1, BLOCK // cap + 1):
        col_step = col_step + (in_block >= k * cap).astype(jnp.int32)
    slot_of = in_block - col_step * cap
    col_of = base + col_step
    used = jnp.zeros((tile_rows, 1), jnp.bool_)
    for b in range(plan.blocks):
        n = int((plan.col_of[b * BLOCK : (b + 1) * BLOCK] >= 0).sum())
        used = used | ((row >= b * BLOCK) & (row < b * BLOCK + n))
    cell = lax.broadcasted_iota(jnp.int32, (128, 1), 0)
    cell_i = jnp.zeros((128, 1), jnp.int32)
    for k in range(1, rows):
        cell_i = cell_i + (cell >= k * cols).astype(jnp.int32)
    cell_j = cell - cell_i * cols
    lab = labels[...].astype(F32)
    col_lab = jnp.zeros((128, cols), F32)
    for k in range(rows):
        col_lab = jnp.where(cell_i == k, lab[k : k + 1, :], col_lab)
    picked_j = lax.broadcasted_iota(jnp.int32, (128, cols), 1) == cell_j
    lab_col = jnp.sum(jnp.where(picked_j, col_lab, 0.0), axis=1, keepdims=True)
    eye = lax.broadcasted_iota(jnp.int32, (128, 128), 0) == lax.broadcasted_iota(jnp.int32, (128, 128), 1)
    lab_row = jnp.sum(jnp.where(eye, lab_col, 0.0), axis=0, keepdims=True)
    lane = lax.broadcasted_iota(jnp.int32, (1, plan.lanes), 1)
    lane_in = jnp.bitwise_and(lane, BLOCK - 1)
    lane_step = jnp.zeros_like(lane)
    for k in range(1, BLOCK // cap + 1):
        lane_step = lane_step + (lane_in >= k * cap).astype(jnp.int32)
    lane_slot = lane_in - lane_step * cap

    id_cols, metas = [], []
    for band in range(levels):
        id_col = jnp.full((tile_rows, 1), -1, jnp.int32)
        id_row = jnp.full((1, plan.lanes), -1, jnp.int32)
        for s in range(cap):
            number = ids[0, band, 0, 0, s]
            id_col = jnp.where(slot_of == s, number, id_col)
            id_row = jnp.where(lane_slot == s, number, id_row)
        id_cols.append(jnp.where(used, id_col, -1))
        pad = jnp.zeros((1, width - plan.lanes - 128), F32)
        metas.append(jnp.concatenate([id_row.astype(F32), lab_row, pad], axis=1))
    wanted = jnp.concatenate([col_of * levels + band for band in range(levels)], axis=0)
    source = lax.broadcasted_iota(jnp.int32, (levels * tile_rows, cols * levels), 1)
    same_col = source == wanted
    id_all = jnp.concatenate(id_cols, axis=0)
    stacked = jnp.zeros((levels * tile_rows, patches.shape[-1]), F32)
    for i in range(rows):
        chosen = jnp.where(same_col & (id_all == i), 1.0, 0.0).astype(BF16)
        stacked = stacked + mm(chosen, patches[i].reshape(cols * levels, patches.shape[-1]))
    stacked = stacked.astype(BF16)
    load.wait()
    for f in fetch:
        f.start()
    embedded = mm(stacked, wbuf[...]) + level_embed[...]
    for band in range(levels):
        part = embedded[band * tile_rows : (band + 1) * tile_rows]
        buf[band] = jnp.where(in_block == BLOCK - 1, metas[band], part).astype(BF16)
    pl.semaphore_wait(barrier, len(moves))
    copies = []
    for k, (dm, da, do) in enumerate(moves):
        if do == 0:
            source, target, count = 0, plan.tiles[da][0], tile_rows
        elif do == 1:
            source, target, count = tile_rows - BLOCK, plan.tiles[2 + da][0], BLOCK
        else:
            source, target, count = 0, plan.tiles[4 + da][0], BLOCK
        copies.append(
            pltpu.make_async_remote_copy(
                src_ref=buf.at[band_of[dm], pl.ds(source, count)],
                dst_ref=out.at[me_l, pl.ds(target, count)],
                send_sem=send.at[k],
                recv_sem=recv.at[k],
                device_id=(band_of[dm], lats[da], lons[do]),
                device_id_type=MESH,
            )
        )
    for copy in copies[::-1]:
        copy.start()
    own = pltpu.make_async_copy(buf.at[me_l], out.at[me_l, pl.ds(0, tile_rows)], local)
    own.start()
    own.wait()
    for copy in copies:
        copy.wait()
    for f in fetch:
        f.wait()


def main_kernel(
    plan, names, sizes, wide, info, row_code, win, hm, lq, cross_gain, swin_gain, mlp_gain,
    cross_kv, cross_query, cross_out, swin_qkv, swin_out, mlp_up, mlp_down,
    out, start,
):
    levels, _, lon_count = sizes
    b_kv, b_query, b_out, b_qkv, b_so, b_up, b_down = cross_kv, cross_query, cross_out, swin_qkv, swin_out, mlp_up, mlp_down
    me_l, me_o = lax.axis_index(names[0]), lax.axis_index(names[2])
    width = lq.shape[1]
    head_dim = width // HEADS
    inv_root = 1.0 / math.sqrt(head_dim)
    latents = lq.shape[0]
    own, count = plan.own, plan.count
    lanes = plan.lanes
    code_c = info[:, 0:1]
    pos_c = info[:, 1:2]
    tile_c = info[:, 2:3]
    lane = lax.broadcasted_iota(jnp.int32, (1, lanes), 1)
    meta_rows = [first + BLOCK - 1 for first, _ in plan.tiles]

    lq_f = lq[...].astype(F32)
    cq = (mm(lq[...], b_query[...]) * inv_root).astype(BF16).astype(F32)
    hm_f = hm[...].astype(F32)
    masked = jnp.concatenate([cq[q : q + 1] * hm_f for q in range(latents)], axis=0).astype(BF16)

    keys, values, presence = [], [], []
    for level in range(levels):
        tokens = wide[level].astype(F32)
        keys_in = layer_norm(tokens, cross_gain[...]).astype(BF16)
        pair = mm(keys_in, b_kv[...]).astype(BF16)
        id_row = tokens[meta_rows[0] : meta_rows[0] + 1, :lanes]
        for t in range(1, 6):
            first, _ = plan.tiles[t]
            id_row = jnp.where(lane >= first, tokens[meta_rows[t] : meta_rows[t] + 1, :lanes], id_row)
        code_r = (row_code[0:1, :] + id_row.astype(jnp.int32))[:, : plan.wide_rows]
        scatter = jnp.where(
            (code_c == code_r) & (id_row.astype(jnp.int32)[:, : plan.wide_rows] >= 0), 1.0, 0.0
        )
        presence.append(jnp.sum(scatter, axis=1, keepdims=True))
        spread = mm(scatter.astype(BF16), pair)
        keys.append(spread[:, :width].astype(BF16))
        values.append(spread[:, width:])
    lab_src = wide[me_l].astype(F32)
    seg = jnp.zeros((count, 128), F32)
    for t in range(6):
        seg = jnp.where(tile_c == t, lab_src[meta_rows[t] : meta_rows[t] + 1, lanes : lanes + 128], seg)
    at_pos = lax.broadcasted_iota(jnp.int32, (count, 128), 1) == pos_c
    lab_col = jnp.sum(jnp.where(at_pos, seg, 0.0), axis=1, keepdims=True)
    eye = lax.broadcasted_iota(jnp.int32, (count, count), 0) == lax.broadcasted_iota(
        jnp.int32, (count, count), 1
    )
    lab_row = jnp.sum(jnp.where(eye, lab_col, 0.0), axis=0, keepdims=True)
    cell_lane = lax.broadcasted_iota(jnp.int32, (1, count), 1)
    halo = (count - 2 * own) // 2
    bad = ((cell_lane >= 2 * own) & (cell_lane < 2 * own + halo) & (me_o == 0)) | (
        (cell_lane >= 2 * own + halo) & (me_o == lon_count - 1)
    )
    lab_row = jnp.where(bad, -1.0, lab_row)
    allowed = jnp.where(lab_col[:own] == lab_row, win[...], 0.0)
    group = 128 // head_dim
    allowed = jnp.concatenate([allowed] * group, axis=0) > 0.5

    exps = [jnp.exp(mm_nt(keys[l], masked)) * presence[l] for l in range(levels)]
    norm = exps[0]
    for e in exps[1:]:
        norm = norm + e
    weights = [(e / norm).astype(BF16) for e in exps]
    hm_all = jnp.concatenate([hm_f] * latents, axis=0)
    hm_row = lax.broadcasted_iota(jnp.int32, hm_all.shape, 0)
    queries, wkeys, wvalues = [], [], []
    for q in range(latents):
        expand = jnp.where(
            (hm_row >= q * HEADS) & (hm_row < (q + 1) * HEADS), hm_all, 0.0
        ).astype(BF16)
        mix = mm(weights[0], expand) * values[0]
        for l in range(1, levels):
            mix = mix + mm(weights[l], expand) * values[l]
        latent = mm(mix.astype(BF16), b_out[...]) + lq_f[q : q + 1]
        start[q * own : (q + 1) * own] = latent[:own]
        normed_f = layer_norm(latent, swin_gain[...])
        normed = normed_f.astype(BF16)
        kv = mm(normed, b_qkv[:, width:]).astype(BF16)
        wkeys.append(kv[:, :width])
        wvalues.append(kv[:, width:])
        queries.append(normed_f[:own])
    q_all = mm(jnp.concatenate(queries, axis=0).astype(BF16), b_qkv[:, :width]) * inv_root
    lane_head = [
        (lax.broadcasted_iota(jnp.int32, (1, 128), 1) >= h * head_dim)
        & (lax.broadcasted_iota(jnp.int32, (1, 128), 1) < (h + 1) * head_dim)
        for h in range(group)
    ]
    mixes = []
    for p in range(latents):
        partners = [k for k in range(latents) if (k + 1) // 2 == (p + 1) // 2]
        pieces = []
        for g in range(width // 128):
            cut = slice(g * 128, (g + 1) * 128)
            part = q_all[p * own : (p + 1) * own, cut]
            stack = jnp.concatenate([jnp.where(h, part, 0.0) for h in lane_head], axis=0).astype(BF16)
            raised = [
                jnp.where(allowed, jnp.exp(mm_nt(stack, wkeys[k][:, cut])), 0.0) for k in partners
            ]
            norm = jnp.sum(raised[0], axis=1, keepdims=True)
            for e in raised[1:]:
                norm = norm + jnp.sum(e, axis=1, keepdims=True)
            inverse = 1.0 / norm
            total = mm((raised[0] * inverse).astype(BF16), wvalues[partners[0]][:, cut])
            for e, k in zip(raised[1:], partners[1:]):
                total = total + mm((e * inverse).astype(BF16), wvalues[k][:, cut])
            piece = jnp.zeros((own, 128), F32)
            for h in range(group):
                piece = jnp.where(lane_head[h], total[h * own : (h + 1) * own], piece)
            pieces.append(piece)
        mixes.append(jnp.concatenate(pieces, axis=1))
    attended = start[...] + mm(jnp.concatenate(mixes, axis=0).astype(BF16), b_so[...])
    mlp_in = layer_norm(attended, mlp_gain[...]).astype(BF16)
    hidden = mlp_up.shape[1]
    result = attended
    step = 512
    for c in range(0, hidden, step):
        up = mm(mlp_in, b_up[:, c : c + step])
        act = (up * (1.0 + lax.erf(up * math.sqrt(0.5))) * 0.5).astype(BF16)
        result = result + mm(act, b_down[c : c + step, :])
    for p in range(latents):
        out[:, p, :] = result[p * own : (p + 1) * own]


def shards(
    sizes, names,
    patches, level_embed, embed_weight, block_ids, latent_queries, cross_gain, cross_query, cross_kv,
    cross_out, region_ids, swin_gain, swin_qkv, swin_out, mlp_gain, mlp_up, mlp_down,
):
    levels = sizes[0]
    _, bands, rows, cols, _ = patches.shape
    width = embed_weight.shape[1]
    plan = Plan(rows, cols, block_ids.shape[-1])
    vmem = pl.BlockSpec(memory_space=pltpu.VMEM)
    hbm = pl.BlockSpec(memory_space=pl.ANY)
    moves = 6 * levels - 1
    latents = latent_queries.shape[0]
    weights = (cross_kv, cross_query, cross_out, swin_qkv, swin_out, mlp_up, mlp_down)
    handed = 2 * (levels * plan.wide_rows * width + sum(w.size for w in weights))
    wide, *weights = pl.pallas_call(
        functools.partial(send_kernel, plan, names, sizes),
        out_shape=[pltpu.VMEM((levels, plan.wide_rows, width), BF16)] + [pltpu.VMEM(w.shape, BF16) for w in weights],
        in_specs=[vmem, vmem, hbm, pl.BlockSpec(memory_space=pltpu.SMEM), vmem] + [hbm] * 7,
        out_specs=[vmem] * 8,
        scratch_shapes=[
            pltpu.VMEM(embed_weight.shape, BF16),
            pltpu.VMEM((bands, plan.tile_rows, width), BF16),
            pltpu.SemaphoreType.DMA,
            pltpu.SemaphoreType.DMA((moves,)),
            pltpu.SemaphoreType.DMA((moves,)),
            pltpu.SemaphoreType.DMA,
            pltpu.SemaphoreType.DMA((7,)),
        ],
        compiler_params=pltpu.CompilerParams(collective_id=0, has_side_effects=True, vmem_limit_bytes=VMEM - handed),
        name="send",
    )(patches[0].transpose(1, 2, 0, 3), level_embed, embed_weight, block_ids, region_ids, *weights)
    head_mask = (np.arange(width)[None, :] // (width // HEADS) == np.arange(HEADS)[:, None])
    weights = [pltpu.with_memory_space_constraint(w, pltpu.VMEM) for w in weights]
    tokens = pl.pallas_call(
        functools.partial(main_kernel, plan, names, sizes),
        out_shape=jax.ShapeDtypeStruct((plan.own, latents, width), F32),
        in_specs=[vmem] * 16,
        out_specs=vmem,
        scratch_shapes=[pltpu.VMEM((latents * plan.own, width), F32)],
        compiler_params=pltpu.CompilerParams(vmem_limit_bytes=40 << 20),
        name="main",
    )(
        pltpu.with_memory_space_constraint(wide, pltpu.VMEM), jnp.asarray(plan.info), jnp.asarray(plan.row_code), jnp.asarray(plan.win),
        jnp.asarray(head_mask, BF16), latent_queries, cross_gain.reshape(1, -1),
        swin_gain.reshape(1, -1), mlp_gain.reshape(1, -1), *weights,
    )
    return tokens.reshape(rows, cols, latents, width).transpose(2, 0, 1, 3)


def solution(mesh):
    names = ("lvl", "lat", "lon")
    sizes = tuple(mesh.shape[name] for name in names)
    tiled = P("lvl", None, "lat", "lon", None)
    return jax.shard_map(
        functools.partial(shards, sizes, names),
        mesh=mesh,
        in_specs=(
            tiled, P("lvl", None), P(), tiled, P(), P(), P(), P(), P(), P(("lvl", "lat"), "lon"),
            P(), P(), P(), P(), P(), P(),
        ),
        out_specs=P(None, ("lvl", "lat"), "lon", None),
        check_vma=False,
    )
```

```python
import functools
import math

import jax
import jax.numpy as jnp
import numpy as np
from jax import lax
from jax.experimental import pallas as pl
from jax.experimental.pallas import tpu as pltpu
from jax.sharding import PartitionSpec as P

HEADS = 16
WIN_LAT = 6
BLOCK = 16
CODE = 64
LANES = 128
VMEM = 63700000
MESH = pl.DeviceIdType.MESH
F32 = jnp.float32
BF16 = jnp.bfloat16


def layer_norm(tensor, gain_vec):
    average = jnp.mean(tensor, axis=-1, keepdims=True)
    centred = tensor - average
    spread = jnp.mean(centred * centred, axis=-1, keepdims=True)
    return centred * lax.rsqrt(spread + 1e-05) * gain_vec


def mm(a, b):
    return jnp.dot(a, b, preferred_element_type=F32)


def mm_nt(a, b):
    return lax.dot_general(a, b, (((1,), (1,)), ((), ())), preferred_element_type=F32)


def add_all(parts):
    total = parts[0]
    for part in parts[1:]:
        total = total + part
    return total


def span(low, high, total, unit):
    first = low // 8 * 8
    size = -(-(high - first) // unit) * unit
    return min(first, total - size), size


class Plan:
    def __init__(self, rows, cols, cap, levels):
        self.rows, self.cols, self.cap, self.levels = rows, cols, cap, levels
        m = self.margin = WIN_LAT // 2
        per = (BLOCK - 1) // cap
        assert per >= m and rows < CODE and rows * cols <= LANES and cols == 2 * WIN_LAT
        groups = [list(range(per))]
        groups += [list(range(c, min(c + per, cols - per))) for c in range(per, cols - per, per)]
        groups += [list(range(cols - per, cols))]
        self.blocks = len(groups)
        self.tile_rows = self.blocks * BLOCK
        col_of = np.full((self.blocks, BLOCK), -1)
        for b, group in enumerate(groups):
            for k, c in enumerate(group):
                col_of[b, k * cap : (k + 1) * cap] = c
        self.col_of = col_of.reshape(-1)
        self.tiles = [(0, self.tile_rows), (self.tile_rows, self.tile_rows)]
        self.tiles += [(2 * self.tile_rows + k * BLOCK, BLOCK) for k in range(4)]
        self.wide_rows = 2 * self.tile_rows + 4 * BLOCK
        depth = min(levels, levels * cap - rows + 1)
        self.planes = [list(range(levels))] if depth == 1 else [[l] for l in range(levels)]
        share = len(self.planes[0])
        self.parts = [[0], [1], [2, 3, 4, 5]]
        first, last = self.col_of[:BLOCK], self.col_of[-BLOCK:]
        cols_of_tile = [self.col_of, self.col_of, last, last, first, first]
        self.row_code = np.full((8, LANES), -100000, np.int32)
        for g, part in enumerate(self.parts):
            codes = [
                np.where(cols_of_tile[t] >= 0, (k * cols + cols_of_tile[t]) * CODE, -100000)
                for k, t in enumerate(part)
            ]
            codes = np.concatenate(codes * share)
            assert len(codes) <= LANES
            self.row_code[g, : len(codes)] = codes
        edges = [0, m, cols - m, cols]
        spans = [range(edges[w], edges[w + 1]) for w in range(3)]
        own = [(i, j, w) for w in range(3) for i in range(rows) for j in spans[w]]
        self.own_cells = own
        self.own = n = rows * cols
        bounds = np.cumsum([0] + [rows * len(s) for s in spans])
        self.bounds = [int(b) for b in bounds]
        cells = [(t, 0, i, j) for t in (0, 1) for i, j, _ in own]
        halo = [spans[2], spans[2], spans[0], spans[0]]
        cells += [(2 + k, k, i, j) for k in range(4) for i in range(rows) for j in halo[k]]
        self.count = len(cells)
        assert self.count == 3 * n and n % 8 == 0
        self.info = np.full((self.count, LANES), -1, np.int32)
        t, k, i, j = np.array(cells).T
        self.info[:, 0] = (k * cols + j) * CODE + i
        self.info[:, 1] = i * cols + j
        self.info[:, 2] = t
        self.q_spans = [span(bounds[w], bounds[w + 1], n, 8) for w in range(3)]
        self.slots = [[], [], []]
        half = 2 * rows * m
        ranges = {0: [(w, bounds[w], bounds[w + 1]) for w in range(3)]}
        ranges[1] = ranges[0]
        ranges[2] = [(0, 0, half), (2, half, 2 * half)]
        self.used = [0, 0, 0]
        for g in range(3):
            for w, low, high in ranges[g]:
                low, high = int(low), int(high)
                first, size = (int(x) for x in span(low, high, n, 16))
                base = self.used[w]
                self.slots[g].append((w, first, size, base))
                self.info[g * n + low : g * n + high, 3 + w] = base + np.arange(low, high) - first
                self.used[w] += size
        assert max(self.used) <= LANES


def front_kernel(
    plan, names, sizes,
    patches, weight, level_embed, ids, labels, lq, cross_gain, swin_gain, info_in, code_in, hm_in,
    cross_query, cross_kv, cross_out, swin_qkv, swin_out, mlp_up, mlp_down,
    start, queries, kw, vw, mask, o_so, o_up, o_down,
    pbuf, wbuf, lebuf, idbuf, labbuf, lqbuf, cgain, sgain, info, codes, hm,
    b_query, b_kv, b_out, b_qkv, buf, wide, kq, ebuf, sems, send, recv,
):
    rows, cols, cap = plan.rows, plan.cols, plan.cap
    levels, lat_count, lon_count = sizes
    bands = levels
    width = weight.shape[1]
    latents = lq.shape[0]
    head_dim = width // HEADS
    inv_root = 1.0 / math.sqrt(head_dim)
    tile_rows = plan.tile_rows
    n = plan.own

    pairs = [
        (ids, idbuf), (labels, labbuf), (patches, pbuf), (weight, wbuf), (level_embed, lebuf),
        (lq, lqbuf), (cross_gain, cgain), (swin_gain, sgain), (info_in, info), (code_in, codes),
        (hm_in, hm), (cross_query, b_query), (cross_kv, b_kv), (cross_out, b_out),
        (swin_qkv, b_qkv), (swin_out, o_so), (mlp_up, o_up), (mlp_down, o_down),
    ]
    loads = [pltpu.make_async_copy(a, b, sems.at[k]) for k, (a, b) in enumerate(pairs)]
    for load in loads[:5]:
        load.start()

    me_l, me_a, me_o = (lax.axis_index(name) for name in names)
    partner = me_a + 1 - 2 * lax.rem(me_a, 2)
    lats = (me_a, partner)
    lons = {
        0: me_o,
        1: lax.rem(me_o + 1, lon_count),
        -1: lax.rem(me_o + lon_count - 1, lon_count),
    }
    band_of = [lax.rem(me_l + dm, levels) for dm in range(levels)]
    moves = [(dm, 0, 0) for dm in range(1, levels)]
    moves += [(dm, 1, 0) for dm in list(range(1, levels)) + [0]]
    moves += [(dm, da, do) for dm in list(range(1, levels)) + [0] for da in (1, 0) for do in (-1, 1)]
    barrier = pltpu.get_barrier_semaphore()
    for dm, da, do in moves:
        pl.semaphore_signal(
            barrier, inc=1, device_id=(band_of[dm], lats[da], lons[do]), device_id_type=MESH
        )

    row = lax.broadcasted_iota(jnp.int32, (tile_rows, 1), 0)
    in_block = jnp.bitwise_and(row, BLOCK - 1)
    col_step = add_all([(in_block >= k * cap).astype(jnp.int32) for k in range(1, BLOCK // cap + 1)])
    slot_of = in_block - col_step * cap
    col_of = jnp.zeros((tile_rows, 1), jnp.int32)
    used = jnp.zeros((tile_rows, 1), jnp.bool_)
    for b in range(plan.blocks):
        here = plan.col_of[b * BLOCK : (b + 1) * BLOCK]
        inside = (row >= b * BLOCK) & (row < (b + 1) * BLOCK)
        col_of = jnp.where(inside, int(here[0]) + col_step, col_of)
        used = used | ((row >= b * BLOCK) & (row < b * BLOCK + int((here >= 0).sum())))
    lane = lax.broadcasted_iota(jnp.int32, (1, LANES), 1)
    lane_in = jnp.bitwise_and(lane, BLOCK - 1)
    lane_step = add_all([(lane_in >= k * cap).astype(jnp.int32) for k in range(1, BLOCK // cap + 1)])
    lane_slot = lane_in - lane_step * cap
    cell = lax.broadcasted_iota(jnp.int32, (LANES, 1), 0)
    cell_i = add_all([(cell >= k * cols).astype(jnp.int32) for k in range(1, rows)])
    cell_j = cell - cell_i * cols
    picked_j = lax.broadcasted_iota(jnp.int32, (LANES, cols), 1) == cell_j
    eye = lax.broadcasted_iota(jnp.int32, (LANES, LANES), 0) == lax.broadcasted_iota(
        jnp.int32, (LANES, LANES), 1
    )
    loads[0].wait()
    loads[1].wait()
    lab = labbuf[...].astype(F32)
    col_lab = jnp.zeros((LANES, cols), F32)
    for k in range(rows):
        col_lab = jnp.where(cell_i == k, lab[k : k + 1, :], col_lab)
    lab_col = jnp.sum(jnp.where(picked_j, col_lab, 0.0), axis=1, keepdims=True)
    lab_row = jnp.sum(jnp.where(eye, lab_col, 0.0), axis=0, keepdims=True)
    picks, metas = [], []
    cells_all = rows * cols * bands
    source = lax.broadcasted_iota(jnp.int32, (tile_rows, cells_all), 1)
    for band in range(bands):
        id_col = jnp.full((tile_rows, 1), -1, jnp.int32)
        id_row = jnp.full((1, LANES), -1, jnp.int32)
        for s in range(cap):
            number = idbuf[0, band, 0, 0, s]
            id_col = jnp.where(slot_of == s, number, id_col)
            id_row = jnp.where(lane_slot == s, number, id_row)
        wanted = jnp.where(used & (id_col >= 0), (id_col * cols + col_of) * bands + band, -1)
        picks.append(jnp.where(source == wanted, 1.0, 0.0))
        pad = jnp.zeros((1, width - 2 * LANES), F32)
        metas.append(jnp.concatenate([id_row.astype(F32), lab_row, pad], axis=1))
    pick = jnp.concatenate(picks, axis=0).astype(BF16)
    loads[2].wait()
    cells_in = pbuf[...].reshape(cells_all, patches.shape[-1])
    loads[3].wait()
    for load in loads[5:]:
        load.start()
    loads[4].wait()
    embedded = (mm(cells_in, wbuf[...]) + lebuf[...]).astype(BF16)
    listed = mm(pick, embedded)
    for band in range(bands):
        part = listed[band * tile_rows : (band + 1) * tile_rows]
        buf[band] = jnp.where(in_block == BLOCK - 1, metas[band], part).astype(BF16)
    pl.semaphore_wait(barrier, len(moves))
    copies = {}
    for k, (dm, da, do) in enumerate(moves):
        if do == 0:
            origin, target, size = 0, plan.tiles[da][0], tile_rows
        elif do == 1:
            origin, target, size = tile_rows - BLOCK, plan.tiles[2 + da][0], BLOCK
        else:
            origin, target, size = 0, plan.tiles[4 + da][0], BLOCK
        copies[dm, da, do] = pltpu.make_async_remote_copy(
            src_ref=buf.at[band_of[dm], pl.ds(origin, size)],
            dst_ref=wide.at[me_l, pl.ds(target, size)],
            send_sem=send.at[k],
            recv_sem=recv.at[k],
            device_id=(band_of[dm], lats[da], lons[do]),
            device_id_type=MESH,
        )
        copies[dm, da, do].start()
    wide[me_l, pl.ds(0, tile_rows)] = buf[me_l]

    for w in range(3):
        for p in range(latents):
            if plan.used[w] < LANES:
                fill = jnp.zeros((LANES - plan.used[w], width), BF16)
                kw[w, p, plan.used[w] :] = fill
                vw[w, p, plan.used[w] :] = fill
    for load in loads[5:11]:
        load.wait()
    lq_f = lqbuf[...].astype(F32)
    hm_f = hm[...].astype(F32)
    hm_all = jnp.concatenate([hm_f] * latents, axis=0)
    hm_row = lax.broadcasted_iota(jnp.int32, hm_all.shape, 0)
    for q in range(latents):
        ebuf[:, q * width : (q + 1) * width] = jnp.where(
            (hm_row >= q * HEADS) & (hm_row < (q + 1) * HEADS), hm_all, 0.0
        ).astype(BF16)
    loads[11].wait()
    cq = (mm(lqbuf[...], b_query[...]) * inv_root).astype(BF16).astype(F32)
    masked = jnp.concatenate([cq[q : q + 1] * hm_f for q in range(latents)], axis=0).astype(BF16)
    loads[12].wait()
    kq[...] = mm_nt(b_kv[:, :width], masked).astype(BF16)
    loads[13].wait()
    loads[14].wait()

    def group_latents(g):
        part = plan.parts[g]
        code_c = info[g * n : (g + 1) * n, 0:1]
        low = plan.tiles[part[0]][0]
        size = sum(plan.tiles[t][1] for t in part)
        exps, values = [], []
        for plane in plan.planes:
            tokens = jnp.concatenate([wide[l, low : low + size] for l in plane], axis=0)
            id_row = jnp.full((1, LANES), -1.0, F32)
            begin = 0
            for l in plane:
                for t in part:
                    meta = plan.tiles[t][0]
                    line = wide[l, meta : meta + BLOCK, :LANES].astype(F32)[BLOCK - 1 :]
                    id_row = jnp.where(lane >= begin, line, id_row)
                    begin += plan.tiles[t][1]
            id_row = id_row.astype(jnp.int32)
            code_r = jnp.where(id_row >= 0, codes[g : g + 1, :] + id_row, -1)
            pick = jnp.where(code_c == code_r, 1.0, 0.0)[:, :begin]
            keys_in = layer_norm(mm(pick.astype(BF16), tokens), cgain[...]).astype(BF16)
            present = jnp.sum(pick, axis=1, keepdims=True)
            values.append(mm(keys_in, b_kv[:, width:]))
            exps.append(jnp.exp(mm(keys_in, kq[...])) * present)
        norm = add_all(exps)
        mixes = []
        for e, v in zip(exps, values):
            spread = mm((e / norm).astype(BF16), ebuf[...])
            mixes.append(
                jnp.concatenate(
                    [spread[:, q * width : (q + 1) * width] * v for q in range(latents)], axis=0
                )
            )
        out = mm(add_all(mixes).astype(BF16), b_out[...])
        latent = jnp.concatenate(
            [out[q * n : (q + 1) * n] + lq_f[q : q + 1] for q in range(latents)], axis=0
        )
        return latent, layer_norm(latent, sgain[...]).astype(BF16)

    def put(g, keys, values):
        for p in range(latents):
            for w, first, size, base in plan.slots[g]:
                cut = slice(p * n + first, p * n + first + size)
                kw[w, p, base : base + size] = keys[cut].astype(BF16)
                vw[w, p, base : base + size] = values[cut].astype(BF16)

    for move in moves:
        if move[1:] == (0, 0):
            copies[move].wait_recv()
    latent, normed = group_latents(0)
    start[...] = latent
    queries[...] = mm(normed, b_qkv[:, :width]) * inv_root
    put(0, mm(normed, b_qkv[:, width : 2 * width]), mm(normed, b_qkv[:, 2 * width :]))
    for move in moves:
        if move[1:] == (1, 0):
            copies[move].wait_recv()
    _, normed = group_latents(1)
    put(1, mm(normed, b_qkv[:, width : 2 * width]), mm(normed, b_qkv[:, 2 * width :]))
    for move in moves:
        if move[2] != 0:
            copies[move].wait_recv()
    _, normed = group_latents(2)
    put(2, mm(normed, b_qkv[:, width : 2 * width]), mm(normed, b_qkv[:, 2 * width :]))

    tile_c = info[:, 2:3]
    seg = jnp.zeros((plan.count, LANES), F32)
    for t, (first, _) in enumerate(plan.tiles):
        line = wide[me_l, first : first + BLOCK, LANES : 2 * LANES].astype(F32)[BLOCK - 1 :]
        seg = jnp.where(tile_c == t, line, seg)
    lab_col = jnp.sum(jnp.where(lane == info[:, 1:2], seg, 0.0), axis=1, keepdims=True)
    outside = ((tile_c >= 2) & (tile_c < 4) & (me_o == 0)) | ((tile_c >= 4) & (me_o == lon_count - 1))
    lab_key = jnp.where(outside, -1.0, lab_col)
    at = 0
    for w, (first, size) in enumerate(plan.q_spans):
        keys = jnp.where(lane == info[:, 3 + w : 4 + w], lab_key + 1.0, 0.0)
        keys = jnp.sum(keys, axis=0, keepdims=True) - 1.0
        mask[at : at + size] = jnp.where(lab_col[first : first + size] == keys, 1.0, 0.0)
        at += size

    for copy in copies.values():
        copy.wait_send()
    for load in loads[15:]:
        load.wait()


def back_kernel(plan, start, queries, kw, vw, mask, gain, b_so, b_up, b_down, out, obuf, sems):
    width = b_so.shape[0]
    head_dim = width // HEADS
    n = plan.own
    latents = start.shape[0] // n
    group = LANES // head_dim
    lane = lax.broadcasted_iota(jnp.int32, (1, LANES), 1)
    lane_head = [(lane >= h * head_dim) & (lane < (h + 1) * head_dim) for h in range(group)]
    low_half = lane < LANES // 2
    odd = add_all([jnp.where(lane_head[h], 1.0, 0.0) for h in range(1, group, 2)])
    halves = [(1.0 - odd).astype(BF16), odd.astype(BF16)]
    masks, at = [], 0
    for first, size in plan.q_spans:
        masks.append(mask[at : at + size])
        at += size
    sets = {}
    for p in range(latents):
        sets.setdefault((p + 1) // 2, []).append(p)
    sets = list(sets.values())
    units = [(g, w) for g in range(width // LANES) for w in range(3)]
    found = {}

    def scores(g, w):
        cut = slice(g * LANES, (g + 1) * LANES)
        first, size = plan.q_spans[w]
        raised = []
        for members in sets:
            parts = [queries[p * n + first : p * n + first + size, cut] for p in members]
            base = jnp.concatenate(parts, axis=0)
            if len(members) == 2:
                stack = jnp.concatenate([jnp.where(h, base, 0.0) for h in lane_head], axis=0)
                keys = jnp.concatenate([kw[w, p, :, cut] for p in members], axis=0)
            else:
                stack = jnp.concatenate(
                    [jnp.where(low_half, base, 0.0), jnp.where(low_half, 0.0, base)], axis=0
                )
                keys = jnp.concatenate([kw[w, members[0], :, cut] * h for h in halves], axis=0)
            raised.append(mm_nt(stack.astype(BF16), keys))
        return raised

    def mixed(g, w, raised):
        cut = slice(g * LANES, (g + 1) * LANES)
        first, size = plan.q_spans[w]
        weights = []
        for members, score in zip(sets, raised):
            allowed = jnp.concatenate([masks[w]] * (score.shape[0] // size), axis=0) > 0.5
            left = jnp.where(allowed, jnp.exp(score[:, :LANES]), 0.0)
            right = jnp.where(allowed, jnp.exp(score[:, LANES:]), 0.0)
            if len(members) == 2:
                inverse = 1.0 / jnp.sum(left + right, axis=1, keepdims=True)
                left, right = left * inverse, right * inverse
            else:
                left = left * (1.0 / jnp.sum(left, axis=1, keepdims=True))
                right = right * (1.0 / jnp.sum(right, axis=1, keepdims=True))
            weights.append(jnp.concatenate([left, right], axis=1).astype(BF16))
        for members, weight in zip(sets, weights):
            many = len(members) * size
            if len(members) == 2:
                values = jnp.concatenate([vw[w, p, :, cut] for p in members], axis=0)
                total = mm(weight, values)
                piece = total[:many]
                for h in range(1, group):
                    piece = jnp.where(lane_head[h], total[h * many : (h + 1) * many], piece)
            else:
                values = jnp.concatenate([vw[w, members[0], :, cut] * h for h in halves], axis=0)
                total = mm(weight, values)
                piece = jnp.where(low_half, total[:many], total[many:])
            for k, p in enumerate(members):
                found[p, g, w] = piece[k * size : (k + 1) * size]

    ahead = scores(*units[0])
    for k, unit in enumerate(units):
        now = ahead
        if k + 1 < len(units):
            ahead = scores(*units[k + 1])
        mixed(*unit, now)
    row = lax.broadcasted_iota(jnp.int32, (8, 1), 0)
    mixes = []
    for p in range(latents):
        columns = []
        for g in range(width // LANES):
            tiles = []
            for r in range(0, n, 8):
                tile = None
                for w, (first, size) in enumerate(plan.q_spans):
                    if plan.bounds[w] < r + 8 and plan.bounds[w + 1] > r:
                        here = found[p, g, w][r - first : r - first + 8]
                        tile = here if tile is None else jnp.where(row + r < plan.bounds[w], tile, here)
                tiles.append(tile)
            columns.append(jnp.concatenate(tiles, axis=0))
        mixes.append(jnp.concatenate(columns, axis=1))
    attended = start[...] + mm(jnp.concatenate(mixes, axis=0).astype(BF16), b_so[...])
    mlp_in = layer_norm(attended, gain[...]).astype(BF16)
    result = attended
    step = 512
    for c in range(0, b_up.shape[1], step):
        up = mm(mlp_in, b_up[:, c : c + step])
        act = (up * (1.0 + lax.erf(up * math.sqrt(0.5))) * 0.5).astype(BF16)
        result = result + mm(act, b_down[c : c + step, :])
    for p in range(latents):
        obuf[:, p, :] = result[p * n : (p + 1) * n]
    writes, k = [], 0
    while k < n:
        i, j, w = plan.own_cells[k]
        size = 1
        while k + size < n and plan.own_cells[k + size] == (i, j + size, w):
            size += 1
        target = i * plan.cols + j
        writes.append(
            pltpu.make_async_copy(
                obuf.at[pl.ds(k, size)], out.at[pl.ds(target, size)], sems.at[len(writes)]
            )
        )
        k += size
    for write in writes:
        write.start()
    for write in writes:
        write.wait()


def shards(
    sizes, names,
    patches, level_embed, embed_weight, block_ids, latent_queries, cross_gain, cross_query, cross_kv,
    cross_out, region_ids, swin_gain, swin_qkv, swin_out, mlp_gain, mlp_up, mlp_down,
):
    levels = sizes[0]
    _, bands, rows, cols, features = patches.shape
    assert bands == levels
    width = embed_weight.shape[1]
    latents = latent_queries.shape[0]
    plan = Plan(rows, cols, block_ids.shape[-1], levels)
    n = plan.own
    head_mask = np.arange(width)[None, :] // (width // HEADS) == np.arange(HEADS)[:, None]
    vmem = pl.BlockSpec(memory_space=pltpu.VMEM)
    hbm = pl.BlockSpec(memory_space=pl.ANY)
    moves = 6 * levels - 1
    q_rows = sum(size for _, size in plan.q_spans)
    handed = [
        ((latents * n, width), F32), ((latents * n, width), F32),
        ((3, latents, LANES, width), BF16), ((3, latents, LANES, width), BF16),
        ((q_rows, LANES), F32),
        (swin_out.shape, BF16), (mlp_up.shape, BF16), (mlp_down.shape, BF16),
    ]
    room = int(sum(math.prod(shape) * np.dtype(kind).itemsize for shape, kind in handed))
    inputs = (
        patches[0].transpose(1, 2, 0, 3), embed_weight, level_embed, block_ids, region_ids,
        latent_queries, cross_gain.reshape(1, -1), swin_gain.reshape(1, -1),
        jnp.asarray(plan.info), jnp.asarray(plan.row_code), jnp.asarray(head_mask, BF16),
    )
    weights = (cross_query, cross_kv, cross_out, swin_qkv)
    later = (swin_out, mlp_up, mlp_down)
    held = [pltpu.VMEM(x.shape, x.dtype) for x in inputs]
    held[3] = pltpu.SMEM(block_ids.shape, jnp.int32)
    order = (0, 1, 2, 3, 4, 5, 6, 7, 8, 9, 10)
    outs = pl.pallas_call(
        functools.partial(front_kernel, plan, names, sizes),
        out_shape=[pltpu.VMEM(shape, kind) for shape, kind in handed],
        in_specs=[hbm] * 18,
        out_specs=[vmem] * 8,
        scratch_shapes=[held[k] for k in order]
        + [pltpu.VMEM(w.shape, BF16) for w in weights]
        + [
            pltpu.VMEM((bands, plan.tile_rows, width), BF16),
            pltpu.VMEM((levels, plan.wide_rows, width), BF16),
            pltpu.VMEM((width, latents * HEADS), BF16),
            pltpu.VMEM((latents * HEADS, latents * width), BF16),
            pltpu.SemaphoreType.DMA((18,)),
            pltpu.SemaphoreType.DMA((moves,)),
            pltpu.SemaphoreType.DMA((moves,)),
        ],
        compiler_params=pltpu.CompilerParams(
            collective_id=0, has_side_effects=True, vmem_limit_bytes=VMEM - room
        ),
        name="front",
    )(*inputs, *weights, *later)
    outs = [pltpu.with_memory_space_constraint(x, pltpu.VMEM) for x in outs]
    tokens = pl.pallas_call(
        functools.partial(back_kernel, plan),
        out_shape=jax.ShapeDtypeStruct((n, latents, width), F32),
        in_specs=[vmem] * 9,
        out_specs=hbm,
        scratch_shapes=[
            pltpu.VMEM((n, latents, width), F32),
            pltpu.SemaphoreType.DMA((3 * rows,)),
        ],
        compiler_params=pltpu.CompilerParams(vmem_limit_bytes=40 << 20),
        name="back",
    )(*outs[:5], mlp_gain.reshape(1, -1), *outs[5:])
    return tokens.reshape(rows, cols, latents, width).transpose(2, 0, 1, 3)


def solution(mesh):
    names = ("lvl", "lat", "lon")
    sizes = tuple(mesh.shape[name] for name in names)
    tiled = P("lvl", None, "lat", "lon", None)
    return jax.shard_map(
        functools.partial(shards, sizes, names),
        mesh=mesh,
        in_specs=(
            tiled, P("lvl", None), P(), tiled, P(), P(), P(), P(), P(), P(("lvl", "lat"), "lon"),
            P(), P(), P(), P(), P(), P(),
        ),
        out_specs=P(None, ("lvl", "lat"), "lon", None),
        check_vma=False,
    )
```

```python
import functools
import math

import jax
import jax.numpy as jnp
import numpy as np
from jax import lax
from jax.experimental import pallas as pl
from jax.experimental.pallas import tpu as pltpu
from jax.sharding import PartitionSpec as P

HEADS = 16
WIN_LAT = 6
BLOCK = 16
CODE = 64
LANES = 128
VMEM = 63700000
MESH = pl.DeviceIdType.MESH
F32 = jnp.float32
BF16 = jnp.bfloat16


def layer_norm(tensor, gain_vec):
    average = jnp.mean(tensor, axis=-1, keepdims=True)
    centred = tensor - average
    spread = jnp.mean(centred * centred, axis=-1, keepdims=True)
    return centred * lax.rsqrt(spread + 1e-05) * gain_vec


def mm(a, b):
    return jnp.dot(a, b, preferred_element_type=F32)


def mm_nt(a, b):
    return lax.dot_general(a, b, (((1,), (1,)), ((), ())), preferred_element_type=F32)


def add_all(parts):
    total = parts[0]
    for part in parts[1:]:
        total = total + part
    return total


def span(low, high, total, unit):
    first = low // 8 * 8
    size = -(-(high - first) // unit) * unit
    return min(first, total - size), size


class Plan:
    def __init__(self, rows, cols, cap, levels):
        self.rows, self.cols, self.cap, self.levels = rows, cols, cap, levels
        m = self.margin = WIN_LAT // 2
        per = (BLOCK - 1) // cap
        assert per >= m and rows < CODE and rows * cols <= LANES and cols == 2 * WIN_LAT
        groups = [list(range(per))]
        groups += [list(range(c, min(c + per, cols - per))) for c in range(per, cols - per, per)]
        groups += [list(range(cols - per, cols))]
        self.blocks = len(groups)
        self.tile_rows = self.blocks * BLOCK
        col_of = np.full((self.blocks, BLOCK), -1)
        for b, group in enumerate(groups):
            for k, c in enumerate(group):
                col_of[b, k * cap : (k + 1) * cap] = c
        self.col_of = col_of.reshape(-1)
        self.tiles = [(0, self.tile_rows), (self.tile_rows, self.tile_rows)]
        self.tiles += [(2 * self.tile_rows + k * BLOCK, BLOCK) for k in range(4)]
        self.wide_rows = 2 * self.tile_rows + 4 * BLOCK
        depth = min(levels, levels * cap - rows + 1)
        self.planes = [list(range(levels))] if depth == 1 else [[l] for l in range(levels)]
        share = len(self.planes[0])
        self.parts = [[0], [1], [2, 3, 4, 5]]
        first, last = self.col_of[:BLOCK], self.col_of[-BLOCK:]
        cols_of_tile = [self.col_of, self.col_of, last, last, first, first]
        self.row_code = np.full((8, LANES), -100000, np.int32)
        for g, part in enumerate(self.parts):
            codes = [
                np.where(cols_of_tile[t] >= 0, (k * cols + cols_of_tile[t]) * CODE, -100000)
                for k, t in enumerate(part)
            ]
            codes = np.concatenate(codes * share)
            assert len(codes) <= LANES
            self.row_code[g, : len(codes)] = codes
        edges = [0, m, cols - m, cols]
        spans = [range(edges[w], edges[w + 1]) for w in range(3)]
        own = [(i, j, w) for w in range(3) for i in range(rows) for j in spans[w]]
        self.own_cells = own
        self.own = n = rows * cols
        bounds = np.cumsum([0] + [rows * len(s) for s in spans])
        self.bounds = [int(b) for b in bounds]
        cells = [(t, 0, i, j) for t in (0, 1) for i, j, _ in own]
        halo = [spans[2], spans[2], spans[0], spans[0]]
        cells += [(2 + k, k, i, j) for k in range(4) for i in range(rows) for j in halo[k]]
        self.count = len(cells)
        assert self.count == 3 * n and n % 8 == 0
        self.info = np.full((self.count, LANES), -1, np.int32)
        t, k, i, j = np.array(cells).T
        self.info[:, 0] = (k * cols + j) * CODE + i
        self.info[:, 1] = i * cols + j
        self.info[:, 2] = t
        self.q_spans = [span(bounds[w], bounds[w + 1], n, 8) for w in range(3)]
        self.slots = [[], [], []]
        half = 2 * rows * m
        ranges = {0: [(w, bounds[w], bounds[w + 1]) for w in range(3)]}
        ranges[1] = ranges[0]
        ranges[2] = [(0, 0, half), (2, half, 2 * half)]
        self.used = [0, 0, 0]
        for g in range(3):
            for w, low, high in ranges[g]:
                low, high = int(low), int(high)
                first, size = (int(x) for x in span(low, high, n, 16))
                base = self.used[w]
                self.slots[g].append((w, first, size, base))
                self.info[g * n + low : g * n + high, 3 + w] = base + np.arange(low, high) - first
                self.used[w] += size
        assert max(self.used) <= LANES


def front_kernel(
    plan, names, sizes,
    patches, weight, level_embed, ids, labels, lq, cross_gain, swin_gain, info_in, code_in, hm_in,
    cross_query, cross_kv, cross_out, swin_qkv, swin_out, mlp_up, mlp_down,
    start, queries, kw, vw, mask, o_so, o_up, o_down,
    pbuf, wbuf, lebuf, idbuf, labbuf, lqbuf, cgain, sgain, info, codes, hm,
    b_query, b_kv, b_out, b_qkv, buf, wide, kq, ebuf, sems, send, recv,
):
    rows, cols, cap = plan.rows, plan.cols, plan.cap
    levels, lat_count, lon_count = sizes
    bands = levels
    width = weight.shape[1]
    latents = lq.shape[0]
    head_dim = width // HEADS
    inv_root = 1.0 / math.sqrt(head_dim)
    tile_rows = plan.tile_rows
    n = plan.own

    pairs = [
        (ids, idbuf), (labels, labbuf), (patches, pbuf), (weight, wbuf), (level_embed, lebuf),
        (lq, lqbuf), (cross_gain, cgain), (swin_gain, sgain), (info_in, info), (code_in, codes),
        (hm_in, hm), (cross_query, b_query), (cross_kv, b_kv), (cross_out, b_out),
        (swin_qkv, b_qkv), (swin_out, o_so), (mlp_up, o_up), (mlp_down, o_down),
    ]
    loads = [pltpu.make_async_copy(a, b, sems.at[k]) for k, (a, b) in enumerate(pairs)]
    for load in loads[:5]:
        load.start()

    me_l, me_a, me_o = (lax.axis_index(name) for name in names)
    partner = me_a + 1 - 2 * lax.rem(me_a, 2)
    lats = (me_a, partner)
    lons = {
        0: me_o,
        1: lax.rem(me_o + 1, lon_count),
        -1: lax.rem(me_o + lon_count - 1, lon_count),
    }
    band_of = [lax.rem(me_l + dm, levels) for dm in range(levels)]
    direct = [(dm, 0) for dm in range(1, levels)] + [(dm, 1) for dm in range(levels)]
    targets = [(band_of[dm], lats[da], me_o) for dm, da in direct]
    sides = [(da, do) for da in (0, 1) for do in (1, -1)]
    beside = {(da, do): (me_l, lats[da], lons[do]) for da, do in sides}
    inner = {1: me_o < lon_count - 1, -1: me_o > 0}
    barrier = pltpu.get_barrier_semaphore()
    for target in targets:
        pl.semaphore_signal(barrier, inc=1, device_id=target, device_id_type=MESH)
    for do in (1, -1):

        @pl.when(inner[do])
        def _():
            for da in (0, 1):
                pl.semaphore_signal(barrier, inc=1, device_id=beside[da, do], device_id_type=MESH)

    row = lax.broadcasted_iota(jnp.int32, (tile_rows, 1), 0)
    in_block = jnp.bitwise_and(row, BLOCK - 1)
    col_step = add_all([(in_block >= k * cap).astype(jnp.int32) for k in range(1, BLOCK // cap + 1)])
    slot_of = in_block - col_step * cap
    col_of = jnp.zeros((tile_rows, 1), jnp.int32)
    used = jnp.zeros((tile_rows, 1), jnp.bool_)
    for b in range(plan.blocks):
        here = plan.col_of[b * BLOCK : (b + 1) * BLOCK]
        inside = (row >= b * BLOCK) & (row < (b + 1) * BLOCK)
        col_of = jnp.where(inside, int(here[0]) + col_step, col_of)
        used = used | ((row >= b * BLOCK) & (row < b * BLOCK + int((here >= 0).sum())))
    lane = lax.broadcasted_iota(jnp.int32, (1, LANES), 1)
    lane_in = jnp.bitwise_and(lane, BLOCK - 1)
    lane_step = add_all([(lane_in >= k * cap).astype(jnp.int32) for k in range(1, BLOCK // cap + 1)])
    lane_slot = lane_in - lane_step * cap
    cell = lax.broadcasted_iota(jnp.int32, (LANES, 1), 0)
    cell_i = add_all([(cell >= k * cols).astype(jnp.int32) for k in range(1, rows)])
    cell_j = cell - cell_i * cols
    picked_j = lax.broadcasted_iota(jnp.int32, (LANES, cols), 1) == cell_j
    eye = lax.broadcasted_iota(jnp.int32, (LANES, LANES), 0) == lax.broadcasted_iota(
        jnp.int32, (LANES, LANES), 1
    )
    loads[0].wait()
    loads[1].wait()
    lab = labbuf[...].astype(F32)
    col_lab = jnp.zeros((LANES, cols), F32)
    for k in range(rows):
        col_lab = jnp.where(cell_i == k, lab[k : k + 1, :], col_lab)
    lab_col = jnp.sum(jnp.where(picked_j, col_lab, 0.0), axis=1, keepdims=True)
    lab_row = jnp.sum(jnp.where(eye, lab_col, 0.0), axis=0, keepdims=True)
    picks, metas = [], []
    cells_all = rows * cols * bands
    source = lax.broadcasted_iota(jnp.int32, (tile_rows, cells_all), 1)
    for band in range(bands):
        id_col = jnp.full((tile_rows, 1), -1, jnp.int32)
        id_row = jnp.full((1, LANES), -1, jnp.int32)
        for s in range(cap):
            number = idbuf[0, band, 0, 0, s]
            id_col = jnp.where(slot_of == s, number, id_col)
            id_row = jnp.where(lane_slot == s, number, id_row)
        wanted = jnp.where(used & (id_col >= 0), (id_col * cols + col_of) * bands + band, -1)
        picks.append(jnp.where(source == wanted, 1.0, 0.0))
        pad = jnp.zeros((1, width - 2 * LANES), F32)
        metas.append(jnp.concatenate([id_row.astype(F32), lab_row, pad], axis=1))
    pick = jnp.concatenate(picks, axis=0).astype(BF16)
    loads[2].wait()
    cells_in = pbuf[...].reshape(cells_all, patches.shape[-1])
    loads[3].wait()
    for load in loads[5:]:
        load.start()
    loads[4].wait()
    embedded = (mm(cells_in, wbuf[...]) + lebuf[...]).astype(BF16)
    listed = mm(pick, embedded)
    for band in range(bands):
        part = listed[band * tile_rows : (band + 1) * tile_rows]
        buf[band] = jnp.where(in_block == BLOCK - 1, metas[band], part).astype(BF16)
    pl.semaphore_wait(barrier, len(targets) + 2 * add_all([inner[do].astype(jnp.int32) for do in (1, -1)]))
    copies = {}
    for k, (dm, da) in enumerate(direct):
        copies[dm, da] = pltpu.make_async_remote_copy(
            src_ref=buf.at[band_of[dm]],
            dst_ref=wide.at[me_l, pl.ds(plan.tiles[da][0], tile_rows)],
            send_sem=send.at[k],
            recv_sem=recv.at[k],
            device_id=targets[k],
            device_id_type=MESH,
        )
    relays = {}
    for dm in range(levels):
        level = lax.rem(me_l + dm, levels)
        for da, do in sides:
            origin = tile_rows - BLOCK if do == 1 else 0
            target = plan.tiles[(2 if do == 1 else 4) + da][0]
            slot = len(direct) + len(relays)
            relays[dm, da, do] = pltpu.make_async_remote_copy(
                src_ref=(wide if dm else buf).at[level, pl.ds(origin, BLOCK)],
                dst_ref=wide.at[level, pl.ds(target, BLOCK)],
                send_sem=send.at[slot],
                recv_sem=recv.at[slot],
                device_id=beside[da, do],
                device_id_type=MESH,
            )
    near = [move for move in direct if move[0] == 0 or move[1] == 0]
    far = [move for move in direct if move not in near]
    for move in near:
        copies[move].start()
    for da, do in sides:
        pl.when(inner[do])(relays[0, da, do].start)
    wide[me_l, pl.ds(0, tile_rows)] = buf[me_l]
    for side, (first, count) in ((-1, (2, 2)), (1, (4, 2))):

        @pl.when(jnp.logical_not(inner[side]))
        def _():
            low = plan.tiles[first][0]
            wide[:, low : low + count * BLOCK] = jnp.zeros((levels, count * BLOCK, width), BF16)


    for w in range(3):
        for p in range(latents):
            if plan.used[w] < LANES:
                fill = jnp.zeros((LANES - plan.used[w], width), BF16)
                kw[w, p, plan.used[w] :] = fill
                vw[w, p, plan.used[w] :] = fill
    for move in far:
        copies[move].start()
    for load in loads[5:11]:
        load.wait()
    lq_f = lqbuf[...].astype(F32)
    hm_f = hm[...].astype(F32)
    hm_all = jnp.concatenate([hm_f] * latents, axis=0)
    hm_row = lax.broadcasted_iota(jnp.int32, hm_all.shape, 0)
    for q in range(latents):
        ebuf[:, q * width : (q + 1) * width] = jnp.where(
            (hm_row >= q * HEADS) & (hm_row < (q + 1) * HEADS), hm_all, 0.0
        ).astype(BF16)
    loads[11].wait()
    cq = (mm(lqbuf[...], b_query[...]) * inv_root).astype(BF16).astype(F32)
    masked = jnp.concatenate([cq[q : q + 1] * hm_f for q in range(latents)], axis=0).astype(BF16)
    loads[12].wait()
    kq[...] = mm_nt(b_kv[:, :width], masked).astype(BF16)
    loads[13].wait()
    loads[14].wait()

    def head(g):
        part = plan.parts[g]
        code_c = info[g * n : (g + 1) * n, 0:1]
        low = plan.tiles[part[0]][0]
        size = sum(plan.tiles[t][1] for t in part)
        exps, values = [], []
        for plane in plan.planes:
            tokens = jnp.concatenate([wide[l, low : low + size] for l in plane], axis=0)
            id_row = jnp.full((1, LANES), -1.0, F32)
            begin = 0
            for l in plane:
                for t in part:
                    meta = plan.tiles[t][0]
                    line = wide[l, meta : meta + BLOCK, :LANES].astype(F32)[BLOCK - 1 :]
                    id_row = jnp.where(lane >= begin, line, id_row)
                    begin += plan.tiles[t][1]
            id_row = id_row.astype(jnp.int32)
            code_r = jnp.where(id_row >= 0, codes[g : g + 1, :] + id_row, -1)
            pick = jnp.where(code_c == code_r, 1.0, 0.0)[:, :begin]
            found = mm(pick.astype(BF16), tokens)
            yield
            keys_in = layer_norm(found, cgain[...]).astype(BF16)
            present = jnp.sum(pick, axis=1, keepdims=True)
            score = mm(keys_in, kq[...])
            values.append(mm(keys_in, b_kv[:, width:]))
            yield
            exps.append(jnp.exp(score) * present)
        norm = add_all(exps)
        norm = jnp.where(norm > 0.0, norm, 1.0)
        mixers[g] = [(e / norm).astype(BF16) for e in exps], values

    def tail(g, picked):
        weights, values = mixers[g]
        low, high = picked[0] * width, (picked[-1] + 1) * width
        spreads = [mm(weight, ebuf[:, low:high]) for weight in weights]
        yield
        mixes = []
        for spread, v in zip(spreads, values):
            cuts = [spread[:, k * width : (k + 1) * width] * v for k in range(len(picked))]
            mixes.append(jnp.concatenate(cuts, axis=0))
        out = mm(add_all(mixes).astype(BF16), b_out[...])
        yield
        latent = jnp.concatenate(
            [out[k * n : (k + 1) * n] + lq_f[p : p + 1] for k, p in enumerate(picked)], axis=0
        )
        normed = layer_norm(latent, sgain[...]).astype(BF16)
        if g == 0:
            start[picked[0] * n : (picked[-1] + 1) * n] = latent
            asked = mm(normed, b_qkv[:, :width])
        keys = mm(normed, b_qkv[:, width : 2 * width])
        values = mm(normed, b_qkv[:, 2 * width :])
        yield
        if g == 0:
            queries[picked[0] * n : (picked[-1] + 1) * n] = asked * inv_root
        for k, p in enumerate(picked):
            for w, first, size, base in plan.slots[g]:
                cut = slice(k * n + first, k * n + first + size)
                kw[w, p, base : base + size] = keys[cut].astype(BF16)
                vw[w, p, base : base + size] = values[cut].astype(BF16)

    def run(works):
        works = [iter(work) for work in works]
        waiting, live = list(works), []
        while waiting or live:
            if waiting:
                live.append(waiting.pop(0))
            for work in list(live):
                if next(work, run) is run:
                    live.remove(work)

    def view():
        tile_c = info[:, 2:3]
        seg = jnp.zeros((plan.count, LANES), F32)
        for t, (first, _) in enumerate(plan.tiles):
            line = wide[me_l, first : first + BLOCK, LANES : 2 * LANES].astype(F32)[BLOCK - 1 :]
            seg = jnp.where(tile_c == t, line, seg)
        lab_col = jnp.sum(jnp.where(lane == info[:, 1:2], seg, 0.0), axis=1, keepdims=True)
        yield
        outside = (tile_c >= 2) & (tile_c < 4) & (me_o == 0)
        outside = outside | ((tile_c >= 4) & (me_o == lon_count - 1))
        lab_key = jnp.where(outside, -1.0, lab_col)
        at = 0
        for w, (first, size) in enumerate(plan.q_spans):
            keys = jnp.where(lane == info[:, 3 + w : 4 + w], lab_key + 1.0, 0.0)
            keys = jnp.sum(keys, axis=0, keepdims=True) - 1.0
            mask[at : at + size] = jnp.where(lab_col[first : first + size] == keys, 1.0, 0.0)
            at += size
            yield

    mixers = {}
    half = -(-latents // 2)
    halves = [list(range(latents))]
    for move in direct:
        if move[1] == 0:
            copies[move].wait_recv()
    for (dm, _, do), relay in relays.items():
        if dm:
            pl.when(inner[do])(relay.start)
    run([head(0)])
    run([tail(0, picked) for picked in halves])
    for move in direct:
        if move[1] == 1:
            copies[move].wait_recv()
    run([head(1)])
    run([tail(1, picked) for picked in halves])
    for (_, _, do), relay in relays.items():
        pl.when(inner[-do])(relay.wait_recv)
    run([head(2), view()])
    run([tail(2, picked) for picked in halves])

    for copy in copies.values():
        copy.wait_send()
    for (_, _, do), relay in relays.items():
        pl.when(inner[do])(relay.wait_send)
    for load in loads[15:]:
        load.wait()


def back_kernel(plan, start, queries, kw, vw, mask, gain, b_so, b_up, b_down, out, obuf, sems):
    width = b_so.shape[0]
    head_dim = width // HEADS
    n = plan.own
    latents = start.shape[0] // n
    group = LANES // head_dim
    lane = lax.broadcasted_iota(jnp.int32, (1, LANES), 1)
    lane_head = [(lane >= h * head_dim) & (lane < (h + 1) * head_dim) for h in range(group)]
    low_half = lane < LANES // 2
    odd = add_all([jnp.where(lane_head[h], 1.0, 0.0) for h in range(1, group, 2)])
    halves = [(1.0 - odd).astype(BF16), odd.astype(BF16)]
    masks, at = [], 0
    for first, size in plan.q_spans:
        masks.append(mask[at : at + size])
        at += size
    sets = {}
    for p in range(latents):
        sets.setdefault((p + 1) // 2, []).append(p)
    sets = list(sets.values())
    units = [(g, w) for g in range(width // LANES) for w in range(3)]
    found = {}

    def scores(g, w):
        cut = slice(g * LANES, (g + 1) * LANES)
        first, size = plan.q_spans[w]
        raised = []
        for members in sets:
            parts = [queries[p * n + first : p * n + first + size, cut] for p in members]
            base = jnp.concatenate(parts, axis=0)
            if len(members) == 2:
                stack = jnp.concatenate([jnp.where(h, base, 0.0) for h in lane_head], axis=0)
                keys = jnp.concatenate([kw[w, p, :, cut] for p in members], axis=0)
            else:
                stack = jnp.concatenate(
                    [jnp.where(low_half, base, 0.0), jnp.where(low_half, 0.0, base)], axis=0
                )
                keys = jnp.concatenate([kw[w, members[0], :, cut] * h for h in halves], axis=0)
            raised.append(mm_nt(stack.astype(BF16), keys))
        return raised

    def mixed(g, w, raised):
        cut = slice(g * LANES, (g + 1) * LANES)
        first, size = plan.q_spans[w]
        weights = []
        for members, score in zip(sets, raised):
            allowed = jnp.concatenate([masks[w]] * (score.shape[0] // size), axis=0) > 0.5
            left = jnp.where(allowed, jnp.exp(score[:, :LANES]), 0.0)
            right = jnp.where(allowed, jnp.exp(score[:, LANES:]), 0.0)
            if len(members) == 2:
                inverse = 1.0 / jnp.sum(left + right, axis=1, keepdims=True)
                left, right = left * inverse, right * inverse
            else:
                left = left * (1.0 / jnp.sum(left, axis=1, keepdims=True))
                right = right * (1.0 / jnp.sum(right, axis=1, keepdims=True))
            weights.append(jnp.concatenate([left, right], axis=1).astype(BF16))
        for members, weight in zip(sets, weights):
            many = len(members) * size
            if len(members) == 2:
                values = jnp.concatenate([vw[w, p, :, cut] for p in members], axis=0)
                total = mm(weight, values)
                piece = total[:many]
                for h in range(1, group):
                    piece = jnp.where(lane_head[h], total[h * many : (h + 1) * many], piece)
            else:
                values = jnp.concatenate([vw[w, members[0], :, cut] * h for h in halves], axis=0)
                total = mm(weight, values)
                piece = jnp.where(low_half, total[:many], total[many:])
            for k, p in enumerate(members):
                found[p, g, w] = piece[k * size : (k + 1) * size]

    row = lax.broadcasted_iota(jnp.int32, (8, 1), 0)

    def merged(p, g):
        tiles = []
        for r in range(0, n, 8):
            tile = None
            for w, (first, size) in enumerate(plan.q_spans):
                if plan.bounds[w] < r + 8 and plan.bounds[w + 1] > r:
                    here = found[p, g, w][r - first : r - first + 8]
                    tile = here if tile is None else jnp.where(row + r < plan.bounds[w], tile, here)
            tiles.append(tile)
        return jnp.concatenate(tiles, axis=0)

    half = -(-latents // 2)
    halves_of = [list(range(half)), list(range(half, latents))]
    attended = {}

    def project(low, high):
        for k, picked in enumerate(halves_of):
            mix = [[merged(p, g) for g in range(low, high)] for p in picked]
            mix = jnp.concatenate([jnp.concatenate(m, axis=1) for m in mix], axis=0).astype(BF16)
            base = attended[k] if low else start[picked[0] * n : (picked[-1] + 1) * n]
            attended[k] = base + mm(mix, b_so[low * LANES : high * LANES])

    results = {}
    step = 512

    def tail(picked):
        k = halves_of.index(picked)
        result = attended[k]
        mlp_in = layer_norm(result, gain[...]).astype(BF16)
        chunks = list(range(0, b_up.shape[1], step))
        ahead = mm(mlp_in, b_up[:, :step])
        yield
        for c in chunks:
            up = ahead
            if c + step < b_up.shape[1]:
                ahead = mm(mlp_in, b_up[:, c + step : c + 2 * step])
            act = (up * (1.0 + lax.erf(up * math.sqrt(0.5))) * 0.5).astype(BF16)
            result = result + mm(act, b_down[c : c + step, :])
            yield
        for m, p in enumerate(picked):
            results[p] = result[m * n : (m + 1) * n]

    middle = width // LANES // 2
    ahead = scores(*units[0])
    for k, unit in enumerate(units):
        now = ahead
        if k + 1 < len(units):
            ahead = scores(*units[k + 1])
        mixed(*unit, now)
    project(0, width // LANES)
    works = [tail(picked) for picked in halves_of]
    waiting, live = works, []
    while waiting or live:
        if waiting:
            live.append(waiting.pop(0))
        for work in list(live):
            if next(work, works) is works:
                live.remove(work)
    for p in range(latents):
        obuf[:, p, :] = results[p]
    writes, k = [], 0
    while k < n:
        i, j, w = plan.own_cells[k]
        size = 1
        while k + size < n and plan.own_cells[k + size] == (i, j + size, w):
            size += 1
        target = i * plan.cols + j
        writes.append(
            pltpu.make_async_copy(
                obuf.at[pl.ds(k, size)], out.at[pl.ds(target, size)], sems.at[len(writes)]
            )
        )
        k += size
    for write in writes:
        write.start()
    for write in writes:
        write.wait()


def shards(
    sizes, names,
    patches, level_embed, embed_weight, block_ids, latent_queries, cross_gain, cross_query, cross_kv,
    cross_out, region_ids, swin_gain, swin_qkv, swin_out, mlp_gain, mlp_up, mlp_down,
):
    levels = sizes[0]
    _, bands, rows, cols, features = patches.shape
    assert bands == levels
    width = embed_weight.shape[1]
    latents = latent_queries.shape[0]
    plan = Plan(rows, cols, block_ids.shape[-1], levels)
    n = plan.own
    head_mask = np.arange(width)[None, :] // (width // HEADS) == np.arange(HEADS)[:, None]
    vmem = pl.BlockSpec(memory_space=pltpu.VMEM)
    hbm = pl.BlockSpec(memory_space=pl.ANY)
    moves = 6 * levels - 1
    q_rows = sum(size for _, size in plan.q_spans)
    handed = [
        ((latents * n, width), F32), ((latents * n, width), F32),
        ((3, latents, LANES, width), BF16), ((3, latents, LANES, width), BF16),
        ((q_rows, LANES), F32),
        (swin_out.shape, BF16), (mlp_up.shape, BF16), (mlp_down.shape, BF16),
    ]
    room = int(sum(math.prod(shape) * np.dtype(kind).itemsize for shape, kind in handed))
    inputs = (
        patches[0].transpose(1, 2, 0, 3), embed_weight, level_embed, block_ids, region_ids,
        latent_queries, cross_gain.reshape(1, -1), swin_gain.reshape(1, -1),
        jnp.asarray(plan.info), jnp.asarray(plan.row_code), jnp.asarray(head_mask, BF16),
    )
    weights = (cross_query, cross_kv, cross_out, swin_qkv)
    later = (swin_out, mlp_up, mlp_down)
    held = [pltpu.VMEM(x.shape, x.dtype) for x in inputs]
    held[3] = pltpu.SMEM(block_ids.shape, jnp.int32)
    order = (0, 1, 2, 3, 4, 5, 6, 7, 8, 9, 10)
    outs = pl.pallas_call(
        functools.partial(front_kernel, plan, names, sizes),
        out_shape=[pltpu.VMEM(shape, kind) for shape, kind in handed],
        in_specs=[hbm] * 18,
        out_specs=[vmem] * 8,
        scratch_shapes=[held[k] for k in order]
        + [pltpu.VMEM(w.shape, BF16) for w in weights]
        + [
            pltpu.VMEM((bands, plan.tile_rows, width), BF16),
            pltpu.VMEM((levels, plan.wide_rows, width), BF16),
            pltpu.VMEM((width, latents * HEADS), BF16),
            pltpu.VMEM((latents * HEADS, latents * width), BF16),
            pltpu.SemaphoreType.DMA((18,)),
            pltpu.SemaphoreType.DMA((moves,)),
            pltpu.SemaphoreType.DMA((moves,)),
        ],
        compiler_params=pltpu.CompilerParams(
            collective_id=0, has_side_effects=True, vmem_limit_bytes=VMEM - room
        ),
        name="front",
    )(*inputs, *weights, *later)
    outs = [pltpu.with_memory_space_constraint(x, pltpu.VMEM) for x in outs]
    tokens = pl.pallas_call(
        functools.partial(back_kernel, plan),
        out_shape=jax.ShapeDtypeStruct((n, latents, width), F32),
        in_specs=[vmem] * 9,
        out_specs=hbm,
        scratch_shapes=[
            pltpu.VMEM((n, latents, width), F32),
            pltpu.SemaphoreType.DMA((3 * rows,)),
        ],
        compiler_params=pltpu.CompilerParams(vmem_limit_bytes=40 << 20),
        name="back",
    )(*outs[:5], mlp_gain.reshape(1, -1), *outs[5:])
    return tokens.reshape(rows, cols, latents, width).transpose(2, 0, 1, 3)


def solution(mesh):
    names = ("lvl", "lat", "lon")
    sizes = tuple(mesh.shape[name] for name in names)
    tiled = P("lvl", None, "lat", "lon", None)
    return jax.shard_map(
        functools.partial(shards, sizes, names),
        mesh=mesh,
        in_specs=(
            tiled, P("lvl", None), P(), tiled, P(), P(), P(), P(), P(), P(("lvl", "lat"), "lon"),
            P(), P(), P(), P(), P(), P(),
        ),
        out_specs=P(None, ("lvl", "lat"), "lon", None),
        check_vma=False,
    )
```

```python
import functools
import math

import jax
import jax.numpy as jnp
import numpy as np
from jax import lax
from jax.experimental import pallas as pl
from jax.experimental.pallas import tpu as pltpu
from jax.sharding import PartitionSpec as P

HEADS = 16
WIN_LAT = 6
BLOCK = 16
CODE = 64
KCUT = 256
AHEAD = 2
LANES = 128
VMEM = 63700000
MESH = pl.DeviceIdType.MESH
F32 = jnp.float32
BF16 = jnp.bfloat16


def layer_norm(tensor, gain_vec):
    average = jnp.mean(tensor, axis=-1, keepdims=True)
    centred = tensor - average
    spread = jnp.mean(centred * centred, axis=-1, keepdims=True)
    return centred * lax.rsqrt(spread + 1e-05) * gain_vec


def mm(a, b):
    return jnp.dot(a, b, preferred_element_type=F32)


def mm_nt(a, b):
    return lax.dot_general(a, b, (((1,), (1,)), ((), ())), preferred_element_type=F32)


def add_all(parts):
    total = parts[0]
    for part in parts[1:]:
        total = total + part
    return total


def span(low, high, total, unit):
    first = low // 8 * 8
    size = -(-(high - first) // unit) * unit
    return min(first, total - size), size


class Plan:
    def __init__(self, rows, cols, cap, levels):
        self.rows, self.cols, self.cap, self.levels = rows, cols, cap, levels
        m = self.margin = WIN_LAT // 2
        per = (BLOCK - 1) // cap
        assert per >= m and rows < CODE and rows * cols <= LANES and cols == 2 * WIN_LAT
        groups = [list(range(per))]
        groups += [list(range(c, min(c + per, cols - per))) for c in range(per, cols - per, per)]
        groups += [list(range(cols - per, cols))]
        sizes = [-(-len(group) * cap // 8) * 8 for group in groups]
        sizes[0] = sizes[-1] = BLOCK
        self.starts = [sum(sizes[:b]) for b in range(len(groups))]
        self.groups = groups
        self.tile_rows = sum(sizes)
        self.col_of = np.full(self.tile_rows, -1)
        for first, group in zip(self.starts, groups):
            for k, c in enumerate(group):
                self.col_of[first + k * cap : first + (k + 1) * cap] = c
        pitch = -(-self.tile_rows // BLOCK) * BLOCK
        self.tiles = [(0, self.tile_rows), (pitch, self.tile_rows)]
        self.tiles += [(2 * pitch + k * BLOCK, BLOCK) for k in range(4)]
        self.wide_rows = 2 * pitch + 4 * BLOCK
        depth = min(levels, levels * cap - rows + 1)
        self.planes = [list(range(levels))] if depth == 1 else [[l] for l in range(levels)]
        share = len(self.planes[0])
        self.parts = [[0], [1], [2, 3, 4, 5]]
        first, last = self.col_of[:BLOCK], self.col_of[-BLOCK:]
        cols_of_tile = [self.col_of, self.col_of, last, last, first, first]
        self.row_code = np.full((8, LANES), -100000, np.int32)
        for g, part in enumerate(self.parts):
            codes = [
                np.where(cols_of_tile[t] >= 0, (k * cols + cols_of_tile[t]) * CODE, -100000)
                for k, t in enumerate(part)
            ]
            codes = np.concatenate(codes * share)
            assert len(codes) <= LANES
            self.row_code[g, : len(codes)] = codes
        edges = [0, m, cols - m, cols]
        spans = [range(edges[w], edges[w + 1]) for w in range(3)]
        own = [(i, j, w) for w in range(3) for i in range(rows) for j in spans[w]]
        self.own_cells = own
        self.own = n = rows * cols
        bounds = np.cumsum([0] + [rows * len(s) for s in spans])
        self.bounds = [int(b) for b in bounds]
        cells = [(t, 0, i, j) for t in (0, 1) for i, j, _ in own]
        halo = [spans[2], spans[2], spans[0], spans[0]]
        cells += [(2 + k, k, i, j) for k in range(4) for i in range(rows) for j in halo[k]]
        self.count = len(cells)
        assert self.count == 3 * n and n % 8 == 0
        self.info = np.full((self.count, LANES), -1, np.int32)
        t, k, i, j = np.array(cells).T
        self.info[:, 0] = (k * cols + j) * CODE + i
        self.info[:, 1] = i * cols + j
        self.info[:, 2] = t
        self.q_spans = [span(bounds[w], bounds[w + 1], n, 8) for w in range(3)]
        self.slots = [[], [], []]
        half = 2 * rows * m
        ranges = {0: [(w, bounds[w], bounds[w + 1]) for w in range(3)]}
        ranges[1] = ranges[0]
        ranges[2] = [(0, 0, half), (2, half, 2 * half)]
        self.used = [0, 0, 0]
        for g in range(3):
            for w, low, high in ranges[g]:
                low, high = int(low), int(high)
                first, size = (int(x) for x in span(low, high, n, 16))
                base = self.used[w]
                self.slots[g].append((w, first, size, base))
                self.info[g * n + low : g * n + high, 3 + w] = base + np.arange(low, high) - first
                self.used[w] += size
        assert max(self.used) <= LANES


def attention(plan, latents, queries, kw, vw, allowed_of, units, found):
    width = queries.shape[1]
    head_dim = width // HEADS
    n = plan.own
    group = LANES // head_dim
    lane = lax.broadcasted_iota(jnp.int32, (1, LANES), 1)
    lane_head = [(lane >= h * head_dim) & (lane < (h + 1) * head_dim) for h in range(group)]
    low_half = lane < LANES // 2
    odd = add_all([jnp.where(lane_head[h], 1.0, 0.0) for h in range(1, group, 2)])
    halves = [(1.0 - odd).astype(BF16), odd.astype(BF16)]
    sets = {}
    for p in range(latents):
        sets.setdefault((p + 1) // 2, []).append(p)
    sets = list(sets.values())
    def scores(g, w):
        cut = slice(g * LANES, (g + 1) * LANES)
        first, size = plan.q_spans[w]
        raised = []
        for members in sets:
            parts = [queries[p * n + first : p * n + first + size, cut] for p in members]
            base = jnp.concatenate(parts, axis=0)
            if len(members) == 2:
                stack = jnp.concatenate([jnp.where(h, base, 0.0) for h in lane_head], axis=0)
                keys = jnp.concatenate([kw[w, p, :, cut] for p in members], axis=0)
            else:
                stack = jnp.concatenate(
                    [jnp.where(low_half, base, 0.0), jnp.where(low_half, 0.0, base)], axis=0
                )
                keys = jnp.concatenate([kw[w, members[0], :, cut] * h for h in halves], axis=0)
            raised.append(mm_nt(stack.astype(BF16), keys))
        return raised

    def mixed(g, w, raised):
        cut = slice(g * LANES, (g + 1) * LANES)
        first, size = plan.q_spans[w]
        weights = []
        for members, score in zip(sets, raised):
            allowed = jnp.concatenate([allowed_of(w)] * (score.shape[0] // size), axis=0) > 0.5
            left = jnp.where(allowed, jnp.exp(score[:, :LANES]), 0.0)
            right = jnp.where(allowed, jnp.exp(score[:, LANES:]), 0.0)
            if len(members) == 2:
                inverse = 1.0 / jnp.sum(left + right, axis=1, keepdims=True)
                left, right = left * inverse, right * inverse
            else:
                left = left * (1.0 / jnp.sum(left, axis=1, keepdims=True))
                right = right * (1.0 / jnp.sum(right, axis=1, keepdims=True))
            weights.append(jnp.concatenate([left, right], axis=1).astype(BF16))
        for members, weight in zip(sets, weights):
            many = len(members) * size
            if len(members) == 2:
                values = jnp.concatenate([vw[w, p, :, cut] for p in members], axis=0)
                total = mm(weight, values)
                piece = total[:many]
                for h in range(1, group):
                    piece = jnp.where(lane_head[h], total[h * many : (h + 1) * many], piece)
            else:
                values = jnp.concatenate([vw[w, members[0], :, cut] * h for h in halves], axis=0)
                total = mm(weight, values)
                piece = jnp.where(low_half, total[:many], total[many:])
            for k, p in enumerate(members):
                found[p, g, w] = piece[k * size : (k + 1) * size]

    ahead = [scores(*unit) for unit in units[:AHEAD]]
    yield
    for k, unit in enumerate(units):
        if k + AHEAD < len(units):
            ahead.append(scores(*units[k + AHEAD]))
        mixed(*unit, ahead.pop(0))
        yield


def run(works):
    waiting, live = [iter(work) for work in works], []
    while waiting or live:
        if waiting:
            live.append(waiting.pop(0))
        for work in list(live):
            if next(work, run) is run:
                live.remove(work)


def front_kernel(
    plan, names, sizes,
    patches, weight, level_embed, ids, labels, cross_gain, lq, swin_gain, info_in, code_in, hm_in,
    cross_query, cross_kv, cross_out, swin_qkv, swin_out, mlp_up, mlp_down,
    start, queries, kw, vw, mask, early, o_so, o_up, o_down,
    pbuf, wbuf, lebuf, idbuf, labbuf, cgain, lqbuf, sgain, info, codes, hm,
    b_query, b_kv, b_out, b_qkv, buf, wide, kq, sems, wsems, send, recv,
):
    rows, cols, cap = plan.rows, plan.cols, plan.cap
    levels, lat_count, lon_count = sizes
    bands = levels
    width = weight.shape[1]
    latents = lq.shape[0]
    head_dim = width // HEADS
    inv_root = 1.0 / math.sqrt(head_dim)
    tile_rows = plan.tile_rows
    n = plan.own

    pairs = [
        (ids, idbuf), (labels, labbuf), (patches, pbuf), (weight, wbuf), (level_embed, lebuf),
        (cross_gain, cgain), (lq, lqbuf), (swin_gain, sgain), (info_in, info), (code_in, codes),
        (hm_in, hm), (cross_query, b_query), (cross_kv, b_kv), (cross_out, b_out),
        (swin_qkv, b_qkv), (swin_out, o_so), (mlp_up, o_up), (mlp_down, o_down),
    ]
    loads = [
        None if k == 3 else pltpu.make_async_copy(a, b, sems.at[k]) for k, (a, b) in enumerate(pairs)
    ]
    features = weight.shape[0]
    chunks = [(k, min(KCUT, features - k)) for k in range(0, features, KCUT)]
    pieces = [
        pltpu.make_async_copy(weight.at[pl.ds(k, size)], wbuf.at[pl.ds(k, size)], wsems.at[i])
        for i, (k, size) in enumerate(chunks)
    ]
    for k in (0, 1, 2):
        loads[k].start()
    for piece in pieces:
        piece.start()
    for k in (4, 5):
        loads[k].start()

    me_l, me_a, me_o = (lax.axis_index(name) for name in names)
    partner = me_a + 1 - 2 * lax.rem(me_a, 2)
    lats = (me_a, partner)
    lons = {
        0: me_o,
        1: lax.rem(me_o + 1, lon_count),
        -1: lax.rem(me_o + lon_count - 1, lon_count),
    }
    band_of = [lax.rem(me_l + dm, levels) for dm in range(levels)]
    direct = [(dm, 0) for dm in range(1, levels)] + [(dm, 1) for dm in range(levels)]
    targets = [(band_of[dm], lats[da], me_o) for dm, da in direct]
    sides = [(da, do) for da in (0, 1) for do in (1, -1)]
    beside = {(da, do): (me_l, lats[da], lons[do]) for da, do in sides}
    inner = {1: me_o < lon_count - 1, -1: me_o > 0}
    barrier = pltpu.get_barrier_semaphore()
    for target in targets:
        pl.semaphore_signal(barrier, inc=1, device_id=target, device_id_type=MESH)
    for do in (1, -1):

        @pl.when(inner[do])
        def _():
            for da in (0, 1):
                pl.semaphore_signal(barrier, inc=1, device_id=beside[da, do], device_id_type=MESH)

    def step_of(inner_row):
        return add_all([(inner_row >= k * cap).astype(jnp.int32) for k in range(1, BLOCK // cap + 1)])

    def locate(place):
        inner_row, base, held = place, jnp.zeros_like(place), place < 0
        for first, group in zip(plan.starts, plan.groups):
            inner_row = jnp.where(place >= first, place - first, inner_row)
            base = jnp.where(place >= first, group[0], base)
            held = held | ((place >= first) & (place < first + cap * len(group)))
        step = step_of(inner_row)
        return base + step, inner_row - step * cap, held

    row = lax.broadcasted_iota(jnp.int32, (tile_rows, 1), 0)
    col_of, slot_of, used = locate(row)
    meta_row = (row == BLOCK - 1) | (row == tile_rows - 1)
    lane = lax.broadcasted_iota(jnp.int32, (1, LANES), 1)
    lane_row = lane
    for k in range(1, len(plan.planes[0])):
        lane_row = jnp.where(lane >= k * tile_rows, lane - k * tile_rows, lane_row)
    _, lane_slot, _ = locate(lane_row)
    lane_in = jnp.bitwise_and(lane, BLOCK - 1)
    halo_slot = lane_in - step_of(lane_in) * cap
    cell = lax.broadcasted_iota(jnp.int32, (LANES, 1), 0)
    cell_i = add_all([(cell >= k * cols).astype(jnp.int32) for k in range(1, rows)])
    cell_j = cell - cell_i * cols
    picked_j = lax.broadcasted_iota(jnp.int32, (LANES, cols), 1) == cell_j
    eye = lax.broadcasted_iota(jnp.int32, (LANES, LANES), 0) == lax.broadcasted_iota(
        jnp.int32, (LANES, LANES), 1
    )
    loads[0].wait()
    loads[1].wait()
    lab = labbuf[...].astype(F32)
    col_lab = jnp.zeros((LANES, cols), F32)
    for k in range(rows):
        col_lab = jnp.where(cell_i == k, lab[k : k + 1, :], col_lab)
    lab_col = jnp.sum(jnp.where(picked_j, col_lab, 0.0), axis=1, keepdims=True)
    lab_row = jnp.sum(jnp.where(eye, lab_col, 0.0), axis=0, keepdims=True)
    picks, metas = [], []
    cells_all = rows * cols * bands
    source = lax.broadcasted_iota(jnp.int32, (tile_rows, cells_all), 1)
    for band in range(bands):
        id_col = jnp.full((tile_rows, 1), -1, jnp.int32)
        id_row = jnp.full((1, LANES), -1, jnp.int32)
        halo_row = jnp.full((1, LANES), -1, jnp.int32)
        for s in range(cap):
            number = idbuf[0, band, 0, 0, s]
            id_col = jnp.where(slot_of == s, number, id_col)
            id_row = jnp.where(lane_slot == s, number, id_row)
            halo_row = jnp.where(halo_slot == s, number, halo_row)
        wanted = jnp.where(used & (id_col >= 0), (id_col * cols + col_of) * bands + band, -1)
        picks.append(jnp.where(source == wanted, 1.0, 0.0))
        pad = jnp.zeros((1, width - 3 * LANES), F32)
        metas.append(jnp.concatenate([id_row.astype(F32), lab_row, halo_row.astype(F32), pad], axis=1))
    pick = jnp.concatenate(picks, axis=0).astype(BF16)
    loads[2].wait()
    cells_in = pbuf[...].reshape(cells_all, patches.shape[-1])
    cells_in = mm(pick, cells_in).astype(BF16)
    products = []
    for piece, (k, size) in zip(pieces, chunks):
        piece.wait()
        products.append(mm(cells_in[:, k : k + size], wbuf[k : k + size]))
    for load in loads[6:]:
        load.start()
    loads[4].wait()
    embedded = (add_all(products) + lebuf[...]).astype(BF16).astype(F32)
    loads[5].wait()
    listed = layer_norm(embedded, cgain[...])
    for band in range(bands):
        part = listed[band * tile_rows : (band + 1) * tile_rows]
        buf[band] = jnp.where(meta_row, metas[band], part).astype(BF16)
    pl.semaphore_wait(barrier, len(targets) + 2 * add_all([inner[do].astype(jnp.int32) for do in (1, -1)]))
    copies = {}
    for k, (dm, da) in enumerate(direct):
        copies[dm, da] = pltpu.make_async_remote_copy(
            src_ref=buf.at[band_of[dm]],
            dst_ref=wide.at[me_l, pl.ds(plan.tiles[da][0], tile_rows)],
            send_sem=send.at[k],
            recv_sem=recv.at[k],
            device_id=targets[k],
            device_id_type=MESH,
        )
    relays = {}
    for dm in range(levels):
        level = lax.rem(me_l + dm, levels)
        for da, do in sides:
            origin = tile_rows - BLOCK if do == 1 else 0
            target = plan.tiles[(2 if do == 1 else 4) + da][0]
            slot = len(direct) + len(relays)
            relays[dm, da, do] = pltpu.make_async_remote_copy(
                src_ref=(wide if dm else buf).at[level, pl.ds(origin, BLOCK)],
                dst_ref=wide.at[level, pl.ds(target, BLOCK)],
                send_sem=send.at[slot],
                recv_sem=recv.at[slot],
                device_id=beside[da, do],
                device_id_type=MESH,
            )
    near = [move for move in direct if move[0] == 0 or move[1] == 0]
    far = [move for move in direct if move not in near]
    for move in near:
        copies[move].start()
    for da, do in sides:
        pl.when(inner[do])(relays[0, da, do].start)
    wide[me_l, pl.ds(0, tile_rows)] = buf[me_l]
    for side, (first, count) in ((-1, (2, 2)), (1, (4, 2))):

        @pl.when(jnp.logical_not(inner[side]))
        def _():
            low = plan.tiles[first][0]
            wide[:, low : low + count * BLOCK] = jnp.zeros((levels, count * BLOCK, width), BF16)


    for w in range(3):
        for p in range(latents):
            if plan.used[w] < LANES:
                fill = jnp.zeros((LANES - plan.used[w], width), BF16)
                kw[w, p, plan.used[w] :] = fill
                vw[w, p, plan.used[w] :] = fill
    for move in far:
        copies[move].start()
    for load in loads[6:11]:
        load.wait()
    lq_f = lqbuf[...].astype(F32)
    hm_f = hm[...].astype(F32)
    loads[11].wait()
    cq = (mm(lqbuf[...], b_query[...]) * inv_root).astype(BF16).astype(F32)
    masked = jnp.concatenate([cq[q : q + 1] * hm_f for q in range(latents)], axis=0).astype(BF16)
    loads[12].wait()
    kq[...] = mm_nt(b_kv[:, :width], masked).astype(BF16)
    loads[13].wait()
    loads[14].wait()

    def head(g):
        part = plan.parts[g]
        code_c = info[g * n : (g + 1) * n, 0:1]
        low = plan.tiles[part[0]][0]
        size = sum(plan.tiles[t][1] for t in part)
        exps, values = [], []
        for plane in plan.planes:
            tokens = [wide[l, low : low + size].astype(F32) for l in plane]
            tokens = jnp.concatenate(tokens, axis=0).astype(BF16)
            id_row = jnp.full((1, LANES), -1.0, F32)
            begin = 0
            for l in plane:
                for t in part:
                    meta = plan.tiles[t][0]
                    ids_at = 2 * LANES if g == 2 else 0
                    line = wide[l, meta : meta + BLOCK, ids_at : ids_at + LANES]
                    line = line.astype(F32)[BLOCK - 1 :]
                    id_row = jnp.where(lane >= begin, line, id_row)
                    begin += plan.tiles[t][1]
            id_row = id_row.astype(jnp.int32)
            code_r = jnp.where(id_row >= 0, codes[g : g + 1, :] + id_row, -1)
            pick = jnp.where(code_c == code_r, 1.0, 0.0)[:, :begin]
            keys_in = mm(pick.astype(BF16), tokens).astype(BF16)
            yield
            present = jnp.sum(pick, axis=1, keepdims=True)
            score = mm(keys_in, kq[...])
            values.append(mm(keys_in, b_kv[:, width:]))
            yield
            exps.append(jnp.exp(score) * present)
        norm = add_all(exps)
        norm = jnp.where(norm > 0.0, norm, 1.0)
        wide_weights = []
        for e in exps:
            share = (e / norm).astype(BF16).astype(F32)
            wide_weights.append(jnp.concatenate([share, jnp.zeros_like(share)], axis=1))
        mixers[g] = wide_weights, values

    def tail(g, picked):
        weights, values = mixers[g]
        low, high = picked[0] * width, (picked[-1] + 1) * width
        mixes = []
        for weight, v in zip(weights, values):
            cuts = []
            for p in picked:
                spread = []
                for c in range(width // LANES):
                    where = jnp.broadcast_to(p * HEADS + (c * LANES + lane) // head_dim, (n, LANES))
                    spread.append(jnp.take_along_axis(weight, where, axis=1))
                cuts.append(jnp.concatenate(spread, axis=1) * v)
            mixes.append(jnp.concatenate(cuts, axis=0))
        out = mm(add_all(mixes).astype(BF16), b_out[...])
        yield
        latent = jnp.concatenate(
            [out[k * n : (k + 1) * n] + lq_f[p : p + 1] for k, p in enumerate(picked)], axis=0
        )
        normed = layer_norm(latent, sgain[...]).astype(BF16)
        if g == 0:
            start[picked[0] * n : (picked[-1] + 1) * n] = latent
            asked = mm(normed, b_qkv[:, :width])
        keys = mm(normed, b_qkv[:, width : 2 * width])
        values = mm(normed, b_qkv[:, 2 * width :])
        yield
        if g == 0:
            queries[picked[0] * n : (picked[-1] + 1) * n] = asked * inv_root
        for k, p in enumerate(picked):
            for w, first, size, base in plan.slots[g]:
                cut = slice(k * n + first, k * n + first + size)
                kw[w, p, base : base + size] = keys[cut].astype(BF16)
                vw[w, p, base : base + size] = values[cut].astype(BF16)

    lab_cols, lab_keys = {}, {}

    def labels_of(g):
        cells = slice(g * n, (g + 1) * n)
        tile_c = info[cells, 2:3]
        seg = jnp.zeros((n, LANES), F32)
        for t in plan.parts[g]:
            first = plan.tiles[t][0]
            line = wide[me_l, first : first + BLOCK, LANES : 2 * LANES].astype(F32)[BLOCK - 1 :]
            seg = jnp.where(tile_c == t, line, seg)
        lab_cols[g] = jnp.sum(jnp.where(lane == info[cells, 1:2], seg, 0.0), axis=1, keepdims=True)
        lab_keys[g] = lab_cols[g]
        if g == 2:
            outside = (tile_c < 4) & (me_o == 0) | (tile_c >= 4) & (me_o == lon_count - 1)
            lab_keys[g] = jnp.where(outside, -1.0, lab_cols[g])
        yield

    at_of = [sum(size for _, size in plan.q_spans[:w]) for w in range(3)]

    def view(groups, windows):
        for g in groups:
            yield from labels_of(g)
        for w in windows:
            first, size = plan.q_spans[w]
            keys = [
                jnp.where(lane == info[g * n : (g + 1) * n, 3 + w : 4 + w], lab_keys[g] + 1.0, 0.0)
                for g in sorted(lab_keys)
            ]
            keys = jnp.sum(add_all(keys), axis=0, keepdims=True) - 1.0
            seen = jnp.where(lab_cols[0][first : first + size] == keys, 1.0, 0.0)
            mask[at_of[w] : at_of[w] + size] = seen
            yield

    def allowed_of(w):
        return mask[at_of[w] : at_of[w] + plan.q_spans[w][1]]

    def halo():
        yield from head(2)
        yield from tail(2, halves[0])

    found = {}
    units = [(g, 1) for g in range(width // LANES)]
    mixers = {}
    half = -(-latents // 2)
    halves = [list(range(latents))]
    for move in direct:
        if move[1] == 0:
            copies[move].wait_recv()
    for (dm, _, do), relay in relays.items():
        if dm:
            pl.when(inner[do])(relay.start)
    run([head(0)])
    run([tail(0, picked) for picked in halves])
    for move in direct:
        if move[1] == 1:
            copies[move].wait_recv()
    run([head(1), view([0, 1], [1])])
    run([tail(1, picked) for picked in halves])
    for (dm, _, do), relay in relays.items():
        pl.when(inner[-do])(relay.wait_recv)
    run([halo(), attention(plan, latents, queries, kw, vw, allowed_of, units, found), view([2], [0, 2])])
    for (p, g, _), piece in found.items():
        early[p, :, g * LANES : (g + 1) * LANES] = piece

    for copy in copies.values():
        copy.wait_send()
    for (_, _, do), relay in relays.items():
        pl.when(inner[do])(relay.wait_send)
    for load in loads[15:]:
        load.wait()


def back_kernel(plan, start, queries, kw, vw, mask, early, gain, b_so, b_up, b_down, out, obuf, sems):
    width = b_so.shape[0]
    n = plan.own
    latents = start.shape[0] // n
    masks, at = [], 0
    for first, size in plan.q_spans:
        masks.append(mask[at : at + size])
        at += size
    found = {}
    row = lax.broadcasted_iota(jnp.int32, (8, 1), 0)

    def merged(p, g):
        tiles = []
        for r in range(0, n, 8):
            tile = None
            for w, (first, size) in enumerate(plan.q_spans):
                if plan.bounds[w] < r + 8 and plan.bounds[w + 1] > r:
                    here = found[p, g, w][r - first : r - first + 8]
                    tile = here if tile is None else jnp.where(row + r < plan.bounds[w], tile, here)
            tiles.append(tile)
        return jnp.concatenate(tiles, axis=0)

    whole = {}
    parts = [(0, n)]
    runs, k = [], 0
    while k < n:
        i, j, w = plan.own_cells[k]
        size = 1
        while (
            k + size < n
            and plan.own_cells[k + size] == (i, j + size, w)
            and not any(k + size == low for low, _ in parts)
        ):
            size += 1
        runs.append((k, size, i * plan.cols + j))
        k += size
    writes = [
        pltpu.make_async_copy(
            obuf.at[pl.ds(first, size)], out.at[pl.ds(target, size)], sems.at[k]
        )
        for k, (first, size, target) in enumerate(runs)
    ]
    step = 512

    def tail(low, high):
        size = high - low
        mix = jnp.concatenate([whole[p][low:high] for p in range(latents)], axis=0).astype(BF16)
        base = [start[p * n + low : p * n + high] for p in range(latents)]
        result = jnp.concatenate(base, axis=0) + mm(mix, b_so[...])
        yield
        mlp_in = layer_norm(result, gain[...]).astype(BF16)
        chunks = list(range(0, b_up.shape[1], step))
        ahead = mm(mlp_in, b_up[:, :step])
        yield
        for c in chunks:
            up = ahead
            if c + step < b_up.shape[1]:
                ahead = mm(mlp_in, b_up[:, c + step : c + 2 * step])
            act = (up * (1.0 + lax.erf(up * math.sqrt(0.5))) * 0.5).astype(BF16)
            result = result + mm(act, b_down[c : c + step, :])
            yield
        for p in range(latents):
            obuf[low:high, p, :] = result[p * size : (p + 1) * size]
        for write, (first, _, _) in zip(writes, runs):
            if low <= first < high:
                write.start()

    groups = range(width // LANES)
    for p in range(latents):
        for g in groups:
            found[p, g, 1] = early[p, :, g * LANES : (g + 1) * LANES]
    units = [(g, w) for g in groups for w in (0, 2)]
    run([attention(plan, latents, queries, kw, vw, masks.__getitem__, units, found)])
    for p in range(latents):
        whole[p] = jnp.concatenate([merged(p, g) for g in groups], axis=1)
    run([tail(low, high) for low, high in parts])
    for write in writes:
        write.wait()


def shards(
    sizes, names,
    patches, level_embed, embed_weight, block_ids, latent_queries, cross_gain, cross_query, cross_kv,
    cross_out, region_ids, swin_gain, swin_qkv, swin_out, mlp_gain, mlp_up, mlp_down,
):
    levels = sizes[0]
    _, bands, rows, cols, features = patches.shape
    assert bands == levels
    width = embed_weight.shape[1]
    latents = latent_queries.shape[0]
    plan = Plan(rows, cols, block_ids.shape[-1], levels)
    n = plan.own
    head_mask = np.arange(width)[None, :] // (width // HEADS) == np.arange(HEADS)[:, None]
    vmem = pl.BlockSpec(memory_space=pltpu.VMEM)
    hbm = pl.BlockSpec(memory_space=pl.ANY)
    moves = 6 * levels - 1
    q_rows = sum(size for _, size in plan.q_spans)
    handed = [
        ((latents * n, width), F32), ((latents * n, width), F32),
        ((3, latents, LANES, width), BF16), ((3, latents, LANES, width), BF16),
        ((q_rows, LANES), F32), ((latents, plan.q_spans[1][1], width), F32),
        (swin_out.shape, BF16), (mlp_up.shape, BF16), (mlp_down.shape, BF16),
    ]
    room = int(sum(math.prod(shape) * np.dtype(kind).itemsize for shape, kind in handed))
    inputs = (
        patches[0].transpose(1, 2, 0, 3), embed_weight, level_embed, block_ids, region_ids,
        cross_gain.reshape(1, -1), latent_queries, swin_gain.reshape(1, -1),
        jnp.asarray(plan.info), jnp.asarray(plan.row_code), jnp.asarray(head_mask, BF16),
    )
    weights = (cross_query, cross_kv, cross_out, swin_qkv)
    later = (swin_out, mlp_up, mlp_down)
    held = [pltpu.VMEM(x.shape, x.dtype) for x in inputs]
    held[3] = pltpu.SMEM(block_ids.shape, jnp.int32)
    outs = pl.pallas_call(
        functools.partial(front_kernel, plan, names, sizes),
        out_shape=[pltpu.VMEM(shape, kind) for shape, kind in handed],
        in_specs=[hbm] * 18,
        out_specs=[vmem] * len(handed),
        scratch_shapes=held
        + [pltpu.VMEM(w.shape, BF16) for w in weights]
        + [
            pltpu.VMEM((bands, plan.tile_rows, width), BF16),
            pltpu.VMEM((levels, plan.wide_rows, width), BF16),
            pltpu.VMEM((width, latents * HEADS), BF16),
            pltpu.SemaphoreType.DMA((18,)),
            pltpu.SemaphoreType.DMA((-(-features // KCUT),)),
            pltpu.SemaphoreType.DMA((moves,)),
            pltpu.SemaphoreType.DMA((moves,)),
        ],
        compiler_params=pltpu.CompilerParams(
            collective_id=0, has_side_effects=True, vmem_limit_bytes=VMEM - room
        ),
        name="front",
    )(*inputs, *weights, *later)
    outs = [pltpu.with_memory_space_constraint(x, pltpu.VMEM) for x in outs]
    tokens = pl.pallas_call(
        functools.partial(back_kernel, plan),
        out_shape=jax.ShapeDtypeStruct((n, latents, width), F32),
        in_specs=[vmem] * 10,
        out_specs=hbm,
        scratch_shapes=[
            pltpu.VMEM((n, latents, width), F32),
            pltpu.SemaphoreType.DMA((4 * rows,)),
        ],
        compiler_params=pltpu.CompilerParams(vmem_limit_bytes=40 << 20),
        name="back",
    )(*outs[:6], mlp_gain.reshape(1, -1), *outs[6:])
    return tokens.reshape(rows, cols, latents, width).transpose(2, 0, 1, 3)


def solution(mesh):
    names = ("lvl", "lat", "lon")
    sizes = tuple(mesh.shape[name] for name in names)
    tiled = P("lvl", None, "lat", "lon", None)
    return jax.shard_map(
        functools.partial(shards, sizes, names),
        mesh=mesh,
        in_specs=(
            tiled, P("lvl", None), P(), tiled, P(), P(), P(), P(), P(), P(("lvl", "lat"), "lon"),
            P(), P(), P(), P(), P(), P(),
        ),
        out_specs=P(None, ("lvl", "lat"), "lon", None),
        check_vma=False,
    )
```

```python
import functools
import math

import jax
import jax.numpy as jnp
import numpy as np
from jax import lax
from jax.experimental import pallas as pl
from jax.experimental.pallas import tpu as pltpu
from jax.sharding import PartitionSpec as P

HEADS = 16
WIN_LAT = 6
BLOCK = 16
CODE = 64
KCUT = 256
AHEAD = 2
LANES = 128
VMEM = 63700000
MESH = pl.DeviceIdType.MESH
F32 = jnp.float32
BF16 = jnp.bfloat16


def layer_norm(tensor, gain_vec):
    average = jnp.mean(tensor, axis=-1, keepdims=True)
    centred = tensor - average
    spread = jnp.mean(centred * centred, axis=-1, keepdims=True)
    return centred * lax.rsqrt(spread + 1e-05) * gain_vec


def mm(a, b):
    return jnp.dot(a, b, preferred_element_type=F32)


def mm_nt(a, b):
    return lax.dot_general(a, b, (((1,), (1,)), ((), ())), preferred_element_type=F32)


def add_all(parts):
    total = parts[0]
    for part in parts[1:]:
        total = total + part
    return total


def span(low, high, total, unit):
    first = low // 8 * 8
    size = -(-(high - first) // unit) * unit
    return min(first, total - size), size


class Plan:
    def __init__(self, rows, cols, cap, levels):
        self.rows, self.cols, self.cap, self.levels = rows, cols, cap, levels
        m = self.margin = WIN_LAT // 2
        per = (BLOCK - 1) // cap
        assert per >= m and rows < CODE and rows * cols <= LANES and cols == 2 * WIN_LAT
        groups = [list(range(per))]
        groups += [list(range(c, min(c + per, cols - per))) for c in range(per, cols - per, per)]
        groups += [list(range(cols - per, cols))]
        sizes = [-(-len(group) * cap // 8) * 8 for group in groups]
        sizes[0] = sizes[-1] = BLOCK
        self.starts = [sum(sizes[:b]) for b in range(len(groups))]
        self.groups = groups
        self.tile_rows = sum(sizes)
        self.col_of = np.full(self.tile_rows, -1)
        for first, group in zip(self.starts, groups):
            for k, c in enumerate(group):
                self.col_of[first + k * cap : first + (k + 1) * cap] = c
        pitch = -(-self.tile_rows // BLOCK) * BLOCK
        self.tiles = [(0, self.tile_rows), (pitch, self.tile_rows)]
        self.tiles += [(2 * pitch + k * BLOCK, BLOCK) for k in range(4)]
        self.wide_rows = 2 * pitch + 4 * BLOCK
        depth = min(levels, levels * cap - rows + 1)
        self.planes = [list(range(levels))] if depth == 1 else [[l] for l in range(levels)]
        share = len(self.planes[0])
        self.parts = [[0], [1], [2, 3, 4, 5]]
        first, last = self.col_of[:BLOCK], self.col_of[-BLOCK:]
        cols_of_tile = [self.col_of, self.col_of, last, last, first, first]
        self.row_code = np.full((8, LANES), -100000, np.int32)
        for g, part in enumerate(self.parts):
            codes = [
                np.where(cols_of_tile[t] >= 0, (k * cols + cols_of_tile[t]) * CODE, -100000)
                for k, t in enumerate(part)
            ]
            codes = np.concatenate(codes * share)
            assert len(codes) <= LANES
            self.row_code[g, : len(codes)] = codes
        edges = [0, m, cols - m, cols]
        spans = [range(edges[w], edges[w + 1]) for w in range(3)]
        own = [(i, j, w) for w in range(3) for i in range(rows) for j in spans[w]]
        self.own_cells = own
        self.own = n = rows * cols
        bounds = np.cumsum([0] + [rows * len(s) for s in spans])
        self.bounds = [int(b) for b in bounds]
        cells = [(t, 0, i, j) for t in (0, 1) for i, j, _ in own]
        halo = [spans[2], spans[2], spans[0], spans[0]]
        cells += [(2 + k, k, i, j) for k in range(4) for i in range(rows) for j in halo[k]]
        self.count = len(cells)
        assert self.count == 3 * n and n % 8 == 0
        self.info = np.full((self.count, LANES), -1, np.int32)
        t, k, i, j = np.array(cells).T
        self.info[:, 0] = (k * cols + j) * CODE + i
        self.info[:, 1] = i * cols + j
        self.info[:, 2] = t
        self.q_spans = [span(bounds[w], bounds[w + 1], n, 8) for w in range(3)]
        self.slots = [[], [], []]
        half = 2 * rows * m
        ranges = {0: [(w, bounds[w], bounds[w + 1]) for w in range(3)]}
        ranges[1] = ranges[0]
        ranges[2] = [(0, 0, half), (2, half, 2 * half)]
        self.used = [0, 0, 0]
        for g in range(3):
            for w, low, high in ranges[g]:
                low, high = int(low), int(high)
                first, size = (int(x) for x in span(low, high, n, 16))
                base = self.used[w]
                self.slots[g].append((w, first, size, base))
                self.info[g * n + low : g * n + high, 3 + w] = base + np.arange(low, high) - first
                self.used[w] += size
        assert max(self.used) <= LANES


def attention(plan, latents, queries, kw, vw, allowed_of, units, found, early=AHEAD):
    width = queries.shape[1]
    head_dim = width // HEADS
    n = plan.own
    group = LANES // head_dim
    lane = lax.broadcasted_iota(jnp.int32, (1, LANES), 1)
    lane_head = [(lane >= h * head_dim) & (lane < (h + 1) * head_dim) for h in range(group)]
    low_half = lane < LANES // 2
    odd = add_all([jnp.where(lane_head[h], 1.0, 0.0) for h in range(1, group, 2)])
    halves = [(1.0 - odd).astype(BF16), odd.astype(BF16)]
    sets = {}
    for p in range(latents):
        sets.setdefault((p + 1) // 2, []).append(p)
    sets = list(sets.values())
    def scores(g, w):
        cut = slice(g * LANES, (g + 1) * LANES)
        first, size = plan.q_spans[w]
        raised = []
        for members in sets:
            parts = [queries[p * n + first : p * n + first + size, cut] for p in members]
            base = jnp.concatenate(parts, axis=0)
            if len(members) == 2:
                stack = jnp.concatenate([jnp.where(h, base, 0.0) for h in lane_head], axis=0)
                keys = jnp.concatenate([kw[w, p, :, cut] for p in members], axis=0)
            else:
                stack = jnp.concatenate(
                    [jnp.where(low_half, base, 0.0), jnp.where(low_half, 0.0, base)], axis=0
                )
                keys = jnp.concatenate([kw[w, members[0], :, cut] * h for h in halves], axis=0)
            raised.append(mm_nt(stack.astype(BF16), keys))
        return raised

    def mixed(g, w, raised):
        cut = slice(g * LANES, (g + 1) * LANES)
        first, size = plan.q_spans[w]
        weights = []
        for members, score in zip(sets, raised):
            allowed = jnp.concatenate([allowed_of(w)] * (score.shape[0] // size), axis=0) > 0.5
            left = jnp.where(allowed, jnp.exp(score[:, :LANES]), 0.0)
            right = jnp.where(allowed, jnp.exp(score[:, LANES:]), 0.0)
            if len(members) == 2:
                inverse = 1.0 / jnp.sum(left + right, axis=1, keepdims=True)
                left, right = left * inverse, right * inverse
            else:
                left = left * (1.0 / jnp.sum(left, axis=1, keepdims=True))
                right = right * (1.0 / jnp.sum(right, axis=1, keepdims=True))
            weights.append(jnp.concatenate([left, right], axis=1).astype(BF16))
        for members, weight in zip(sets, weights):
            many = len(members) * size
            if len(members) == 2:
                values = jnp.concatenate([vw[w, p, :, cut] for p in members], axis=0)
                total = mm(weight, values)
                piece = total[:many]
                for h in range(1, group):
                    piece = jnp.where(lane_head[h], total[h * many : (h + 1) * many], piece)
            else:
                values = jnp.concatenate([vw[w, members[0], :, cut] * h for h in halves], axis=0)
                total = mm(weight, values)
                piece = jnp.where(low_half, total[:many], total[many:])
            for k, p in enumerate(members):
                found[p, g, w] = piece[k * size : (k + 1) * size]

    ahead = [scores(*unit) for unit in units[:early]]
    yield
    for k, unit in enumerate(units):
        if k + early < len(units):
            ahead.append(scores(*units[k + early]))
        mixed(*unit, ahead.pop(0))
        yield


def run(works):
    waiting, live = [iter(work) for work in works], []
    while waiting or live:
        if waiting:
            live.append(waiting.pop(0))
        for work in list(live):
            if next(work, run) is run:
                live.remove(work)


def front_kernel(
    plan, names, sizes,
    patches, weight, level_embed, ids, labels, cross_gain, lq, swin_gain, info_in, code_in, hm_in,
    cross_query, cross_kv, cross_out, swin_qkv, swin_out, mlp_up, mlp_down,
    start, queries, kw, vw, mask, early, o_so, o_up, o_down,
    pbuf, wbuf, lebuf, idbuf, labbuf, cgain, lqbuf, sgain, info, codes, hm,
    b_query, b_kv, b_out, b_qkv, buf, wide, kq, sems, wsems, send, recv,
):
    rows, cols, cap = plan.rows, plan.cols, plan.cap
    levels, lat_count, lon_count = sizes
    bands = levels
    width = weight.shape[1]
    latents = lq.shape[0]
    head_dim = width // HEADS
    inv_root = 1.0 / math.sqrt(head_dim)
    tile_rows = plan.tile_rows
    n = plan.own

    pairs = [
        (ids, idbuf), (labels, labbuf), (patches, pbuf), (weight, wbuf), (level_embed, lebuf),
        (cross_gain, cgain), (lq, lqbuf), (swin_gain, sgain), (info_in, info), (code_in, codes),
        (hm_in, hm), (cross_query, b_query), (cross_kv, b_kv), (cross_out, b_out),
        (swin_qkv, b_qkv), (swin_out, o_so), (mlp_up, o_up), (mlp_down, o_down),
    ]
    loads = [
        None if k == 3 else pltpu.make_async_copy(a, b, sems.at[k]) for k, (a, b) in enumerate(pairs)
    ]
    features = weight.shape[0]
    chunks = [(k, min(KCUT, features - k)) for k in range(0, features, KCUT)]
    pieces = [
        pltpu.make_async_copy(weight.at[pl.ds(k, size)], wbuf.at[pl.ds(k, size)], wsems.at[i])
        for i, (k, size) in enumerate(chunks)
    ]
    for k in (0, 1, 2):
        loads[k].start()
    for piece in pieces:
        piece.start()
    for k in (4, 5):
        loads[k].start()

    me_l, me_a, me_o = (lax.axis_index(name) for name in names)
    partner = me_a + 1 - 2 * lax.rem(me_a, 2)
    lats = (me_a, partner)
    lons = {
        0: me_o,
        1: lax.rem(me_o + 1, lon_count),
        -1: lax.rem(me_o + lon_count - 1, lon_count),
    }
    band_of = [lax.rem(me_l + dm, levels) for dm in range(levels)]
    direct = [(dm, 0) for dm in range(1, levels)] + [(dm, 1) for dm in range(levels)]
    targets = [(band_of[dm], lats[da], me_o) for dm, da in direct]
    sides = [(da, do) for da in (0, 1) for do in (1, -1)]
    beside = {(da, do): (me_l, lats[da], lons[do]) for da, do in sides}
    inner = {1: me_o < lon_count - 1, -1: me_o > 0}
    barrier = pltpu.get_barrier_semaphore()
    for target in targets:
        pl.semaphore_signal(barrier, inc=1, device_id=target, device_id_type=MESH)
    for do in (1, -1):

        @pl.when(inner[do])
        def _():
            for da in (0, 1):
                pl.semaphore_signal(barrier, inc=1, device_id=beside[da, do], device_id_type=MESH)

    def step_of(inner_row):
        return add_all([(inner_row >= k * cap).astype(jnp.int32) for k in range(1, BLOCK // cap + 1)])

    def locate(place):
        inner_row, base, held = place, jnp.zeros_like(place), place < 0
        for first, group in zip(plan.starts, plan.groups):
            inner_row = jnp.where(place >= first, place - first, inner_row)
            base = jnp.where(place >= first, group[0], base)
            held = held | ((place >= first) & (place < first + cap * len(group)))
        step = step_of(inner_row)
        return base + step, inner_row - step * cap, held

    row = lax.broadcasted_iota(jnp.int32, (tile_rows, 1), 0)
    col_of, slot_of, used = locate(row)
    meta_row = (row == BLOCK - 1) | (row == tile_rows - 1)
    lane = lax.broadcasted_iota(jnp.int32, (1, LANES), 1)
    lane_row = lane
    for k in range(1, len(plan.planes[0])):
        lane_row = jnp.where(lane >= k * tile_rows, lane - k * tile_rows, lane_row)
    _, lane_slot, _ = locate(lane_row)
    lane_in = jnp.bitwise_and(lane, BLOCK - 1)
    halo_slot = lane_in - step_of(lane_in) * cap
    cell = lax.broadcasted_iota(jnp.int32, (LANES, 1), 0)
    cell_i = add_all([(cell >= k * cols).astype(jnp.int32) for k in range(1, rows)])
    cell_j = cell - cell_i * cols
    picked_j = lax.broadcasted_iota(jnp.int32, (LANES, cols), 1) == cell_j
    eye = lax.broadcasted_iota(jnp.int32, (LANES, LANES), 0) == lax.broadcasted_iota(
        jnp.int32, (LANES, LANES), 1
    )
    loads[0].wait()
    loads[1].wait()
    lab = labbuf[...].astype(F32)
    col_lab = jnp.zeros((LANES, cols), F32)
    for k in range(rows):
        col_lab = jnp.where(cell_i == k, lab[k : k + 1, :], col_lab)
    lab_col = jnp.sum(jnp.where(picked_j, col_lab, 0.0), axis=1, keepdims=True)
    lab_row = jnp.sum(jnp.where(eye, lab_col, 0.0), axis=0, keepdims=True)
    picks, metas = [], []
    cells_all = rows * cols * bands
    source = lax.broadcasted_iota(jnp.int32, (tile_rows, cells_all), 1)
    for band in range(bands):
        id_col = jnp.full((tile_rows, 1), -1, jnp.int32)
        id_row = jnp.full((1, LANES), -1, jnp.int32)
        halo_row = jnp.full((1, LANES), -1, jnp.int32)
        for s in range(cap):
            number = idbuf[0, band, 0, 0, s]
            id_col = jnp.where(slot_of == s, number, id_col)
            id_row = jnp.where(lane_slot == s, number, id_row)
            halo_row = jnp.where(halo_slot == s, number, halo_row)
        wanted = jnp.where(used & (id_col >= 0), (id_col * cols + col_of) * bands + band, -1)
        picks.append(jnp.where(source == wanted, 1.0, 0.0))
        pad = jnp.zeros((1, width - 3 * LANES), F32)
        metas.append(jnp.concatenate([id_row.astype(F32), lab_row, halo_row.astype(F32), pad], axis=1))
    pick = jnp.concatenate(picks, axis=0).astype(BF16)
    loads[2].wait()
    cells_in = pbuf[...].reshape(cells_all, patches.shape[-1])
    cells_in = mm(pick, cells_in).astype(BF16)
    products = []
    for piece, (k, size) in zip(pieces, chunks):
        piece.wait()
        products.append(mm(cells_in[:, k : k + size], wbuf[k : k + size]))
    for load in loads[6:15]:
        load.start()
    loads[4].wait()
    embedded = (add_all(products) + lebuf[...]).astype(BF16).astype(F32)
    loads[5].wait()
    listed = layer_norm(embedded, cgain[...])
    for band in range(bands):
        part = listed[band * tile_rows : (band + 1) * tile_rows]
        buf[band] = jnp.where(meta_row, metas[band], part).astype(BF16)
    pl.semaphore_wait(barrier, len(targets) + 2 * add_all([inner[do].astype(jnp.int32) for do in (1, -1)]))
    copies = {}
    for k, (dm, da) in enumerate(direct):
        copies[dm, da] = pltpu.make_async_remote_copy(
            src_ref=buf.at[band_of[dm]],
            dst_ref=wide.at[me_l, pl.ds(plan.tiles[da][0], tile_rows)],
            send_sem=send.at[k],
            recv_sem=recv.at[k],
            device_id=targets[k],
            device_id_type=MESH,
        )
    relays = {}
    for dm in range(levels):
        level = lax.rem(me_l + dm, levels)
        for da, do in sides:
            origin = tile_rows - BLOCK if do == 1 else 0
            target = plan.tiles[(2 if do == 1 else 4) + da][0]
            slot = len(direct) + len(relays)
            held_by_me = dm == 0 and da == 1
            relays[dm, da, do] = pltpu.make_async_remote_copy(
                src_ref=wide.at[level, pl.ds(plan.tiles[1][0] + origin, BLOCK)]
                if held_by_me
                else (wide if dm else buf).at[level, pl.ds(origin, BLOCK)],
                dst_ref=wide.at[level, pl.ds(target, BLOCK)],
                send_sem=send.at[slot],
                recv_sem=recv.at[slot],
                device_id=beside[0 if held_by_me else da, do],
                device_id_type=MESH,
            )
    near = [move for move in direct if move[0] == 0 or move[1] == 0]
    far = [move for move in direct if move not in near]
    for move in near:
        copies[move].start()
    for do in (1, -1):
        pl.when(inner[do])(relays[0, 0, do].start)
    wide[me_l, pl.ds(0, tile_rows)] = buf[me_l]
    for side, (first, count) in ((-1, (2, 2)), (1, (4, 2))):

        @pl.when(jnp.logical_not(inner[side]))
        def _():
            low = plan.tiles[first][0]
            wide[:, low : low + count * BLOCK] = jnp.zeros((levels, count * BLOCK, width), BF16)


    for w in range(3):
        for p in range(latents):
            if plan.used[w] < LANES:
                fill = jnp.zeros((LANES - plan.used[w], width), BF16)
                kw[w, p, plan.used[w] :] = fill
                vw[w, p, plan.used[w] :] = fill
    for move in far:
        copies[move].start()
    for load in loads[6:11]:
        load.wait()
    lq_f = lqbuf[...].astype(F32)
    hm_f = hm[...].astype(F32)
    loads[11].wait()
    cq = (mm(lqbuf[...], b_query[...]) * inv_root).astype(BF16).astype(F32)
    masked = jnp.concatenate([cq[q : q + 1] * hm_f for q in range(latents)], axis=0).astype(BF16)
    loads[12].wait()
    kq[...] = mm_nt(b_kv[:, :width], masked).astype(BF16)
    loads[13].wait()
    loads[14].wait()

    def head(g):
        part = plan.parts[g]
        code_c = info[g * n : (g + 1) * n, 0:1]
        low = plan.tiles[part[0]][0]
        size = sum(plan.tiles[t][1] for t in part)
        exps, values = [], []
        for plane in plan.planes:
            tokens = [wide[l, low : low + size].astype(F32) for l in plane]
            tokens = jnp.concatenate(tokens, axis=0).astype(BF16)
            id_row = jnp.full((1, LANES), -1.0, F32)
            begin = 0
            for l in plane:
                for t in part:
                    meta = plan.tiles[t][0]
                    ids_at = 2 * LANES if g == 2 else 0
                    line = wide[l, meta : meta + BLOCK, ids_at : ids_at + LANES]
                    line = line.astype(F32)[BLOCK - 1 :]
                    id_row = jnp.where(lane >= begin, line, id_row)
                    begin += plan.tiles[t][1]
            id_row = id_row.astype(jnp.int32)
            code_r = jnp.where(id_row >= 0, codes[g : g + 1, :] + id_row, -1)
            pick = jnp.where(code_c == code_r, 1.0, 0.0)[:, :begin]
            keys_in = mm(pick.astype(BF16), tokens).astype(BF16)
            yield
            present = jnp.sum(pick, axis=1, keepdims=True)
            score = mm(keys_in, kq[...])
            values.append(mm(keys_in, b_kv[:, width:]))
            yield
            exps.append(jnp.exp(score) * present)
        norm = add_all(exps)
        norm = jnp.where(norm > 0.0, norm, 1.0)
        wide_weights = []
        for e in exps:
            share = (e / norm).astype(BF16).astype(F32)
            wide_weights.append(jnp.concatenate([share, jnp.zeros_like(share)], axis=1))
        mixers[g] = wide_weights, values

    def tail(g, picked):
        weights, values = mixers[g]
        low, high = picked[0] * width, (picked[-1] + 1) * width
        mixes = []
        for weight, v in zip(weights, values):
            cuts = []
            for p in picked:
                spread = []
                for c in range(width // LANES):
                    where = jnp.broadcast_to(p * HEADS + (c * LANES + lane) // head_dim, (n, LANES))
                    spread.append(jnp.take_along_axis(weight, where, axis=1))
                cuts.append(jnp.concatenate(spread, axis=1) * v)
            mixes.append(jnp.concatenate(cuts, axis=0))
        out = mm(add_all(mixes).astype(BF16), b_out[...])
        yield
        latent = jnp.concatenate(
            [out[k * n : (k + 1) * n] + lq_f[p : p + 1] for k, p in enumerate(picked)], axis=0
        )
        normed = layer_norm(latent, sgain[...]).astype(BF16)
        if g == 0:
            start[picked[0] * n : (picked[-1] + 1) * n] = latent
            asked = mm(normed, b_qkv[:, :width])
        keys = mm(normed, b_qkv[:, width : 2 * width])
        values = mm(normed, b_qkv[:, 2 * width :])
        yield
        if g == 0:
            queries[picked[0] * n : (picked[-1] + 1) * n] = asked * inv_root
        for k, p in enumerate(picked):
            for w, first, size, base in plan.slots[g]:
                cut = slice(k * n + first, k * n + first + size)
                kw[w, p, base : base + size] = keys[cut].astype(BF16)
                vw[w, p, base : base + size] = values[cut].astype(BF16)

    lab_cols, lab_keys = {}, {}

    def labels_of(g):
        cells = slice(g * n, (g + 1) * n)
        tile_c = info[cells, 2:3]
        seg = jnp.zeros((n, LANES), F32)
        for t in plan.parts[g]:
            first = plan.tiles[t][0]
            line = wide[me_l, first : first + BLOCK, LANES : 2 * LANES].astype(F32)[BLOCK - 1 :]
            seg = jnp.where(tile_c == t, line, seg)
        lab_cols[g] = jnp.sum(jnp.where(lane == info[cells, 1:2], seg, 0.0), axis=1, keepdims=True)
        lab_keys[g] = lab_cols[g]
        if g == 2:
            outside = (tile_c < 4) & (me_o == 0) | (tile_c >= 4) & (me_o == lon_count - 1)
            lab_keys[g] = jnp.where(outside, -1.0, lab_cols[g])
        yield

    at_of = [sum(size for _, size in plan.q_spans[:w]) for w in range(3)]

    def view(groups, windows):
        for g in groups:
            yield from labels_of(g)
        for w in windows:
            first, size = plan.q_spans[w]
            keys = [
                jnp.where(lane == info[g * n : (g + 1) * n, 3 + w : 4 + w], lab_keys[g] + 1.0, 0.0)
                for g in sorted(lab_keys)
            ]
            keys = jnp.sum(add_all(keys), axis=0, keepdims=True) - 1.0
            seen = jnp.where(lab_cols[0][first : first + size] == keys, 1.0, 0.0)
            mask[at_of[w] : at_of[w] + size] = seen
            yield

    def allowed_of(w):
        return mask[at_of[w] : at_of[w] + plan.q_spans[w][1]]

    def halo():
        yield from head(2)
        yield from tail(2, halves[0])

    found = {}
    units = [(g, 1) for g in range(width // LANES)]
    mixers = {}
    half = -(-latents // 2)
    halves = [list(range(latents))]
    for move in direct:
        if move[1] == 0:
            copies[move].wait_recv()
    for (dm, _, do), relay in relays.items():
        if dm:
            pl.when(inner[do])(relay.start)
    copies[0, 1].wait_recv()
    for do in (1, -1):
        pl.when(inner[do])(relays[0, 1, do].start)
    for load in loads[15:]:
        load.start()
    run([head(0)])
    run([tail(0, picked) for picked in halves])
    for move in direct:
        if move[0] and move[1]:
            copies[move].wait_recv()
    run([head(1), view([0, 1], [1])])
    run([tail(1, picked) for picked in halves])
    run([attention(plan, latents, queries, kw, vw, allowed_of, units, found)])
    for (dm, _, do), relay in relays.items():
        pl.when(inner[-do])(relay.wait_recv)
    run([halo(), view([2], [0, 2])])
    for (p, g, _), piece in found.items():
        early[p, :, g * LANES : (g + 1) * LANES] = piece

    for copy in copies.values():
        copy.wait_send()
    for (_, _, do), relay in relays.items():
        pl.when(inner[do])(relay.wait_send)
    for load in loads[15:]:
        load.wait()


def back_kernel(plan, start, queries, kw, vw, mask, early, gain, b_so, b_up, b_down, out, obuf, sems):
    width = b_so.shape[0]
    n = plan.own
    latents = start.shape[0] // n
    masks, at = [], 0
    for first, size in plan.q_spans:
        masks.append(mask[at : at + size])
        at += size
    found = {}
    row = lax.broadcasted_iota(jnp.int32, (8, 1), 0)

    def merged(p, g):
        tiles = []
        for r in range(0, n, 8):
            tile = None
            for w, (first, size) in enumerate(plan.q_spans):
                if plan.bounds[w] < r + 8 and plan.bounds[w + 1] > r:
                    here = found[p, g, w][r - first : r - first + 8]
                    tile = here if tile is None else jnp.where(row + r < plan.bounds[w], tile, here)
            tiles.append(tile)
        return jnp.concatenate(tiles, axis=0)

    whole = {}
    middle = n // 16 * 8 + 8
    parts = [(0, middle), (middle, n)] if middle < n else [(0, n)]
    runs, k = [], 0
    while k < n:
        i, j, w = plan.own_cells[k]
        size = 1
        while (
            k + size < n
            and plan.own_cells[k + size] == (i, j + size, w)
            and not any(k + size == low for low, _ in parts)
        ):
            size += 1
        runs.append((k, size, i * plan.cols + j))
        k += size
    writes = [
        pltpu.make_async_copy(
            obuf.at[pl.ds(first, size)], out.at[pl.ds(target, size)], sems.at[k]
        )
        for k, (first, size, target) in enumerate(runs)
    ]
    step = 512

    def finish():
        mix = jnp.concatenate([whole[p] for p in range(latents)], axis=0).astype(BF16)
        result = start[...] + mm(mix, b_so[...])
        mlp_in = layer_norm(result, gain[...]).astype(BF16)
        chunks = list(range(0, b_up.shape[1], step))
        ahead = mm(mlp_in, b_up[:, :step])
        for c in chunks:
            up = ahead
            if c + step < b_up.shape[1]:
                ahead = mm(mlp_in, b_up[:, c + step : c + 2 * step])
            act = up * (1.0 + lax.erf(up * math.sqrt(0.5))) * 0.5
            if c != chunks[-1]:
                result = result + mm(act.astype(BF16), b_down[c : c + step, :])
        for low, high in parts:
            cuts = [slice(p * n + low, p * n + high) for p in range(latents)]
            done = jnp.concatenate([act[cut] for cut in cuts], axis=0).astype(BF16)
            done = jnp.concatenate([result[cut] for cut in cuts], axis=0) + mm(done, b_down[c:, :])
            for p in range(latents):
                obuf[low:high, p, :] = done[p * (high - low) : (p + 1) * (high - low)]
            for write, (first, _, _) in zip(writes, runs):
                if low <= first < high:
                    write.start()

    groups = range(width // LANES)
    for p in range(latents):
        for g in groups:
            found[p, g, 1] = early[p, :, g * LANES : (g + 1) * LANES]
    units = [(g, w) for g in groups for w in (0, 2)]
    run([attention(plan, latents, queries, kw, vw, masks.__getitem__, units, found, 3)])
    for p in range(latents):
        whole[p] = jnp.concatenate([merged(p, g) for g in groups], axis=1)
    finish()
    for write in writes:
        write.wait()


def shards(
    sizes, names,
    patches, level_embed, embed_weight, block_ids, latent_queries, cross_gain, cross_query, cross_kv,
    cross_out, region_ids, swin_gain, swin_qkv, swin_out, mlp_gain, mlp_up, mlp_down,
):
    levels = sizes[0]
    _, bands, rows, cols, features = patches.shape
    assert bands == levels
    width = embed_weight.shape[1]
    latents = latent_queries.shape[0]
    plan = Plan(rows, cols, block_ids.shape[-1], levels)
    n = plan.own
    head_mask = np.arange(width)[None, :] // (width // HEADS) == np.arange(HEADS)[:, None]
    vmem = pl.BlockSpec(memory_space=pltpu.VMEM)
    hbm = pl.BlockSpec(memory_space=pl.ANY)
    moves = 6 * levels - 1
    q_rows = sum(size for _, size in plan.q_spans)
    handed = [
        ((latents * n, width), F32), ((latents * n, width), F32),
        ((3, latents, LANES, width), BF16), ((3, latents, LANES, width), BF16),
        ((q_rows, LANES), F32), ((latents, plan.q_spans[1][1], width), F32),
        (swin_out.shape, BF16), (mlp_up.shape, BF16), (mlp_down.shape, BF16),
    ]
    room = int(sum(math.prod(shape) * np.dtype(kind).itemsize for shape, kind in handed))
    inputs = (
        patches[0].transpose(1, 2, 0, 3), embed_weight, level_embed, block_ids, region_ids,
        cross_gain.reshape(1, -1), latent_queries, swin_gain.reshape(1, -1),
        jnp.asarray(plan.info), jnp.asarray(plan.row_code), jnp.asarray(head_mask, BF16),
    )
    weights = (cross_query, cross_kv, cross_out, swin_qkv)
    later = (swin_out, mlp_up, mlp_down)
    held = [pltpu.VMEM(x.shape, x.dtype) for x in inputs]
    held[3] = pltpu.SMEM(block_ids.shape, jnp.int32)
    outs = pl.pallas_call(
        functools.partial(front_kernel, plan, names, sizes),
        out_shape=[pltpu.VMEM(shape, kind) for shape, kind in handed],
        in_specs=[hbm] * 18,
        out_specs=[vmem] * len(handed),
        scratch_shapes=held
        + [pltpu.VMEM(w.shape, BF16) for w in weights]
        + [
            pltpu.VMEM((bands, plan.tile_rows, width), BF16),
            pltpu.VMEM((levels, plan.wide_rows, width), BF16),
            pltpu.VMEM((width, latents * HEADS), BF16),
            pltpu.SemaphoreType.DMA((18,)),
            pltpu.SemaphoreType.DMA((-(-features // KCUT),)),
            pltpu.SemaphoreType.DMA((moves,)),
            pltpu.SemaphoreType.DMA((moves,)),
        ],
        compiler_params=pltpu.CompilerParams(
            collective_id=0, has_side_effects=True, vmem_limit_bytes=VMEM - room
        ),
        name="front",
    )(*inputs, *weights, *later)
    outs = [pltpu.with_memory_space_constraint(x, pltpu.VMEM) for x in outs]
    tokens = pl.pallas_call(
        functools.partial(back_kernel, plan),
        out_shape=jax.ShapeDtypeStruct((n, latents, width), F32),
        in_specs=[vmem] * 10,
        out_specs=hbm,
        scratch_shapes=[
            pltpu.VMEM((n, latents, width), F32),
            pltpu.SemaphoreType.DMA((4 * rows,)),
        ],
        compiler_params=pltpu.CompilerParams(vmem_limit_bytes=40 << 20),
        name="back",
    )(*outs[:6], mlp_gain.reshape(1, -1), *outs[6:])
    return tokens.reshape(rows, cols, latents, width).transpose(2, 0, 1, 3)


def solution(mesh):
    names = ("lvl", "lat", "lon")
    sizes = tuple(mesh.shape[name] for name in names)
    tiled = P("lvl", None, "lat", "lon", None)
    return jax.shard_map(
        functools.partial(shards, sizes, names),
        mesh=mesh,
        in_specs=(
            tiled, P("lvl", None), P(), tiled, P(), P(), P(), P(), P(), P(("lvl", "lat"), "lon"),
            P(), P(), P(), P(), P(), P(),
        ),
        out_specs=P(None, ("lvl", "lat"), "lon", None),
        check_vma=False,
    )
```

```python
import functools
import math

import jax
import jax.numpy as jnp
import numpy as np
from jax import lax
from jax.experimental import pallas as pl
from jax.experimental.pallas import tpu as pltpu
from jax.sharding import PartitionSpec as P

HEADS = 16
WIN_LAT = 6
BLOCK = 16
CODE = 64
KCUT = 256
AHEAD = 2
LANES = 128
VMEM = 63700000
MESH = pl.DeviceIdType.MESH
F32 = jnp.float32
BF16 = jnp.bfloat16


def layer_norm(tensor, gain_vec):
    average = jnp.mean(tensor, axis=-1, keepdims=True)
    centred = tensor - average
    spread = jnp.mean(centred * centred, axis=-1, keepdims=True)
    return centred * lax.rsqrt(spread + 1e-05) * gain_vec


def mm(a, b):
    return jnp.dot(a, b, preferred_element_type=F32)


def mm_nt(a, b):
    return lax.dot_general(a, b, (((1,), (1,)), ((), ())), preferred_element_type=F32)


def add_all(parts):
    total = parts[0]
    for part in parts[1:]:
        total = total + part
    return total


def span(low, high, total, unit):
    first = low // 8 * 8
    size = -(-(high - first) // unit) * unit
    return min(first, total - size), size


class Plan:
    def __init__(self, rows, cols, cap, levels):
        self.rows, self.cols, self.cap, self.levels = rows, cols, cap, levels
        m = self.margin = WIN_LAT // 2
        per = (BLOCK - 1) // cap
        assert per >= m and rows < CODE and rows * cols <= LANES and cols == 2 * WIN_LAT
        groups = [list(range(per))]
        groups += [list(range(c, min(c + per, cols - per))) for c in range(per, cols - per, per)]
        groups += [list(range(cols - per, cols))]
        sizes = [-(-len(group) * cap // 8) * 8 for group in groups]
        sizes[0] = sizes[-1] = BLOCK
        self.starts = [sum(sizes[:b]) for b in range(len(groups))]
        self.groups = groups
        self.tile_rows = sum(sizes)
        self.col_of = np.full(self.tile_rows, -1)
        for first, group in zip(self.starts, groups):
            for k, c in enumerate(group):
                self.col_of[first + k * cap : first + (k + 1) * cap] = c
        pitch = -(-self.tile_rows // BLOCK) * BLOCK
        self.tiles = [(0, self.tile_rows), (pitch, self.tile_rows)]
        self.tiles += [(2 * pitch + k * BLOCK, BLOCK) for k in range(4)]
        self.wide_rows = 2 * pitch + 4 * BLOCK
        depth = min(levels, levels * cap - rows + 1)
        self.planes = [list(range(levels))] if depth == 1 else [[l] for l in range(levels)]
        share = len(self.planes[0])
        self.parts = [[0], [1], [2, 3, 4, 5]]
        first, last = self.col_of[:BLOCK], self.col_of[-BLOCK:]
        cols_of_tile = [self.col_of, self.col_of, last, last, first, first]
        self.row_code = np.full((8, LANES), -100000, np.int32)
        for g, part in enumerate(self.parts):
            codes = [
                np.where(cols_of_tile[t] >= 0, (k * cols + cols_of_tile[t]) * CODE, -100000)
                for k, t in enumerate(part)
            ]
            codes = np.concatenate(codes * share)
            assert len(codes) <= LANES
            self.row_code[g, : len(codes)] = codes
        edges = [0, m, cols - m, cols]
        spans = [range(edges[w], edges[w + 1]) for w in range(3)]
        own = [(i, j, w) for w in range(3) for i in range(rows) for j in spans[w]]
        self.own_cells = own
        self.own = n = rows * cols
        bounds = np.cumsum([0] + [rows * len(s) for s in spans])
        self.bounds = [int(b) for b in bounds]
        cells = [(t, 0, i, j) for t in (0, 1) for i, j, _ in own]
        halo = [spans[2], spans[2], spans[0], spans[0]]
        cells += [(2 + k, k, i, j) for k in range(4) for i in range(rows) for j in halo[k]]
        self.count = len(cells)
        assert self.count == 3 * n and n % 8 == 0
        self.info = np.full((self.count, LANES), -1, np.int32)
        t, k, i, j = np.array(cells).T
        self.info[:, 0] = (k * cols + j) * CODE + i
        self.info[:, 1] = i * cols + j
        self.info[:, 2] = t
        self.q_spans = [span(bounds[w], bounds[w + 1], n, 8) for w in range(3)]
        self.slots = [[], [], []]
        half = 2 * rows * m
        ranges = {0: [(w, bounds[w], bounds[w + 1]) for w in range(3)]}
        ranges[1] = ranges[0]
        ranges[2] = [(0, 0, half), (2, half, 2 * half)]
        self.used = [0, 0, 0]
        for g in range(3):
            for w, low, high in ranges[g]:
                low, high = int(low), int(high)
                first, size = (int(x) for x in span(low, high, n, 16))
                base = self.used[w]
                self.slots[g].append((w, first, size, base))
                self.info[g * n + low : g * n + high, 3 + w] = base + np.arange(low, high) - first
                self.used[w] += size
        assert max(self.used) <= LANES


def attention(plan, latents, queries, kw, vw, allowed_of, units, found, early=AHEAD):
    width = queries.shape[1]
    head_dim = width // HEADS
    n = plan.own
    group = LANES // head_dim
    lane = lax.broadcasted_iota(jnp.int32, (1, LANES), 1)
    lane_head = [(lane >= h * head_dim) & (lane < (h + 1) * head_dim) for h in range(group)]
    low_half = lane < LANES // 2
    odd = add_all([jnp.where(lane_head[h], 1.0, 0.0) for h in range(1, group, 2)])
    halves = [(1.0 - odd).astype(BF16), odd.astype(BF16)]
    sets = {}
    for p in range(latents):
        sets.setdefault((p + 1) // 2, []).append(p)
    sets = list(sets.values())
    def scores(g, w):
        cut = slice(g * LANES, (g + 1) * LANES)
        first, size = plan.q_spans[w]
        raised = []
        for members in sets:
            parts = [queries[p * n + first : p * n + first + size, cut] for p in members]
            base = jnp.concatenate(parts, axis=0)
            if len(members) == 2:
                stack = jnp.concatenate([jnp.where(h, base, 0.0) for h in lane_head], axis=0)
                keys = jnp.concatenate([kw[w, p, :, cut] for p in members], axis=0)
            else:
                stack = jnp.concatenate(
                    [jnp.where(low_half, base, 0.0), jnp.where(low_half, 0.0, base)], axis=0
                )
                keys = jnp.concatenate([kw[w, members[0], :, cut] * h for h in halves], axis=0)
            raised.append(mm_nt(stack.astype(BF16), keys))
        return raised

    def mixed(g, w, raised):
        cut = slice(g * LANES, (g + 1) * LANES)
        first, size = plan.q_spans[w]
        weights = []
        for members, score in zip(sets, raised):
            allowed = jnp.concatenate([allowed_of(w)] * (score.shape[0] // size), axis=0) > 0.5
            left = jnp.where(allowed, jnp.exp(score[:, :LANES]), 0.0)
            right = jnp.where(allowed, jnp.exp(score[:, LANES:]), 0.0)
            if len(members) == 2:
                inverse = 1.0 / jnp.sum(left + right, axis=1, keepdims=True)
                left, right = left * inverse, right * inverse
            else:
                left = left * (1.0 / jnp.sum(left, axis=1, keepdims=True))
                right = right * (1.0 / jnp.sum(right, axis=1, keepdims=True))
            weights.append(jnp.concatenate([left, right], axis=1).astype(BF16))
        for members, weight in zip(sets, weights):
            many = len(members) * size
            if len(members) == 2:
                values = jnp.concatenate([vw[w, p, :, cut] for p in members], axis=0)
                total = mm(weight, values)
                piece = total[:many]
                for h in range(1, group):
                    piece = jnp.where(lane_head[h], total[h * many : (h + 1) * many], piece)
            else:
                values = jnp.concatenate([vw[w, members[0], :, cut] * h for h in halves], axis=0)
                total = mm(weight, values)
                piece = jnp.where(low_half, total[:many], total[many:])
            for k, p in enumerate(members):
                found[p, g, w] = piece[k * size : (k + 1) * size]

    ahead = [scores(*unit) for unit in units[:early]]
    yield
    for k, unit in enumerate(units):
        if k + early < len(units):
            ahead.append(scores(*units[k + early]))
        mixed(*unit, ahead.pop(0))
        yield


def run(works):
    waiting, live = [iter(work) for work in works], []
    while waiting or live:
        if waiting:
            live.append(waiting.pop(0))
        for work in list(live):
            if next(work, run) is run:
                live.remove(work)


def front_kernel(
    plan, names, sizes,
    patches, weight, level_embed, ids, labels, cross_gain, lq, swin_gain, info_in, code_in, hm_in,
    cross_query, cross_kv, cross_out, swin_qkv, swin_out, mlp_up, mlp_down,
    start, queries, kw, vw, mask, early, o_so, o_up, o_down,
    pbuf, wbuf, lebuf, idbuf, labbuf, cgain, lqbuf, sgain, info, codes, hm,
    b_query, b_kv, b_out, b_qkv, buf, wide, kq, own_normed, sems, wsems, send, recv,
):
    rows, cols, cap = plan.rows, plan.cols, plan.cap
    levels, lat_count, lon_count = sizes
    bands = levels
    width = weight.shape[1]
    latents = lq.shape[0]
    head_dim = width // HEADS
    inv_root = 1.0 / math.sqrt(head_dim)
    tile_rows = plan.tile_rows
    n = plan.own

    pairs = [
        (ids, idbuf), (labels, labbuf), (patches, pbuf), (weight, wbuf), (level_embed, lebuf),
        (cross_gain, cgain), (lq, lqbuf), (swin_gain, sgain), (info_in, info), (code_in, codes),
        (hm_in, hm), (cross_query, b_query), (cross_kv, b_kv), (cross_out, b_out),
        (swin_qkv, b_qkv), (swin_out, o_so), (mlp_up, o_up), (mlp_down, o_down),
    ]
    loads = [
        None if k == 3 else pltpu.make_async_copy(a, b, sems.at[k]) for k, (a, b) in enumerate(pairs)
    ]
    features = weight.shape[0]
    chunks = [(k, min(KCUT, features - k)) for k in range(0, features, KCUT)]
    pieces = [
        pltpu.make_async_copy(weight.at[pl.ds(k, size)], wbuf.at[pl.ds(k, size)], wsems.at[i])
        for i, (k, size) in enumerate(chunks)
    ]
    for k in (0, 1, 2):
        loads[k].start()
    for piece in pieces:
        piece.start()
    for k in (4, 5):
        loads[k].start()

    me_l, me_a, me_o = (lax.axis_index(name) for name in names)
    partner = me_a + 1 - 2 * lax.rem(me_a, 2)
    lats = (me_a, partner)
    lons = {
        0: me_o,
        1: lax.rem(me_o + 1, lon_count),
        -1: lax.rem(me_o + lon_count - 1, lon_count),
    }
    band_of = [lax.rem(me_l + dm, levels) for dm in range(levels)]
    direct = [(dm, 0) for dm in range(1, levels)] + [(dm, 1) for dm in range(levels)]
    targets = [(band_of[dm], lats[da], me_o) for dm, da in direct]
    sides = [(da, do) for da in (0, 1) for do in (1, -1)]
    beside = {(da, do): (me_l, lats[da], lons[do]) for da, do in sides}
    inner = {1: me_o < lon_count - 1, -1: me_o > 0}
    barrier = pltpu.get_barrier_semaphore()
    for target in targets:
        pl.semaphore_signal(barrier, inc=1, device_id=target, device_id_type=MESH)
    for do in (1, -1):

        @pl.when(inner[do])
        def _():
            pl.semaphore_signal(barrier, inc=1, device_id=beside[0, do], device_id_type=MESH)

    def step_of(inner_row):
        return add_all([(inner_row >= k * cap).astype(jnp.int32) for k in range(1, BLOCK // cap + 1)])

    def locate(place):
        inner_row, base, held = place, jnp.zeros_like(place), place < 0
        for first, group in zip(plan.starts, plan.groups):
            inner_row = jnp.where(place >= first, place - first, inner_row)
            base = jnp.where(place >= first, group[0], base)
            held = held | ((place >= first) & (place < first + cap * len(group)))
        step = step_of(inner_row)
        return base + step, inner_row - step * cap, held

    row = lax.broadcasted_iota(jnp.int32, (tile_rows, 1), 0)
    col_of, slot_of, used = locate(row)
    meta_row = (row == BLOCK - 1) | (row == tile_rows - 1)
    lane = lax.broadcasted_iota(jnp.int32, (1, LANES), 1)
    lane_row = lane
    for k in range(1, len(plan.planes[0])):
        lane_row = jnp.where(lane >= k * tile_rows, lane - k * tile_rows, lane_row)
    _, lane_slot, _ = locate(lane_row)
    lane_in = jnp.bitwise_and(lane, BLOCK - 1)
    halo_slot = lane_in - step_of(lane_in) * cap
    cell = lax.broadcasted_iota(jnp.int32, (LANES, 1), 0)
    cell_i = add_all([(cell >= k * cols).astype(jnp.int32) for k in range(1, rows)])
    cell_j = cell - cell_i * cols
    picked_j = lax.broadcasted_iota(jnp.int32, (LANES, cols), 1) == cell_j
    eye = lax.broadcasted_iota(jnp.int32, (LANES, LANES), 0) == lax.broadcasted_iota(
        jnp.int32, (LANES, LANES), 1
    )
    loads[0].wait()
    loads[1].wait()
    lab = labbuf[...].astype(F32)
    col_lab = jnp.zeros((LANES, cols), F32)
    for k in range(rows):
        col_lab = jnp.where(cell_i == k, lab[k : k + 1, :], col_lab)
    lab_col = jnp.sum(jnp.where(picked_j, col_lab, 0.0), axis=1, keepdims=True)
    lab_row = jnp.sum(jnp.where(eye, lab_col, 0.0), axis=0, keepdims=True)
    picks, metas = [], []
    cells_all = rows * cols * bands
    source = lax.broadcasted_iota(jnp.int32, (tile_rows, cells_all), 1)
    for band in range(bands):
        id_col = jnp.full((tile_rows, 1), -1, jnp.int32)
        id_row = jnp.full((1, LANES), -1, jnp.int32)
        halo_row = jnp.full((1, LANES), -1, jnp.int32)
        for s in range(cap):
            number = idbuf[0, band, 0, 0, s]
            id_col = jnp.where(slot_of == s, number, id_col)
            id_row = jnp.where(lane_slot == s, number, id_row)
            halo_row = jnp.where(halo_slot == s, number, halo_row)
        wanted = jnp.where(used & (id_col >= 0), (id_col * cols + col_of) * bands + band, -1)
        picks.append(jnp.where(source == wanted, 1.0, 0.0))
        pad = jnp.zeros((1, width - 3 * LANES), F32)
        metas.append(jnp.concatenate([id_row.astype(F32), lab_row, halo_row.astype(F32), pad], axis=1))
    pick = jnp.concatenate(picks, axis=0).astype(BF16)
    loads[2].wait()
    cells_in = pbuf[...].reshape(cells_all, patches.shape[-1])
    cells_in = mm(pick, cells_in).astype(BF16)
    products = []
    for piece, (k, size) in zip(pieces, chunks):
        piece.wait()
        products.append(mm(cells_in[:, k : k + size], wbuf[k : k + size]))
    for load in loads[6:15]:
        load.start()
    loads[4].wait()
    embedded = (add_all(products) + lebuf[...]).astype(BF16).astype(F32)
    loads[5].wait()
    listed = layer_norm(embedded, cgain[...])
    for band in range(bands):
        part = listed[band * tile_rows : (band + 1) * tile_rows]
        buf[band] = jnp.where(meta_row, metas[band], part).astype(BF16)
    pl.semaphore_wait(barrier, len(targets) + add_all([inner[do].astype(jnp.int32) for do in (1, -1)]))
    copies = {}
    for k, (dm, da) in enumerate(direct):
        copies[dm, da] = pltpu.make_async_remote_copy(
            src_ref=buf.at[band_of[dm]],
            dst_ref=wide.at[me_l, pl.ds(plan.tiles[da][0], tile_rows)],
            send_sem=send.at[k],
            recv_sem=recv.at[k],
            device_id=targets[k],
            device_id_type=MESH,
        )
    relays = {}
    for dm in range(levels):
        level = lax.rem(me_l + dm, levels)
        for da, do in sides:
            origin = tile_rows - BLOCK if do == 1 else 0
            target = plan.tiles[(2 if do == 1 else 4) + da][0]
            slot = len(direct) + len(relays)
            held_by_me = da == 1
            relays[dm, da, do] = pltpu.make_async_remote_copy(
                src_ref=wide.at[level, pl.ds(plan.tiles[1][0] + origin, BLOCK)]
                if held_by_me
                else (wide if dm else buf).at[level, pl.ds(origin, BLOCK)],
                dst_ref=wide.at[level, pl.ds(target, BLOCK)],
                send_sem=send.at[slot],
                recv_sem=recv.at[slot],
                device_id=beside[0, do],
                device_id_type=MESH,
            )
    near = [move for move in direct if move[0] == 0 or move[1] == 0]
    far = [move for move in direct if move not in near]
    for move in far:
        copies[move].start()
    for move in near:
        copies[move].start()
    for do in (1, -1):
        pl.when(inner[do])(relays[0, 0, do].start)
    wide[me_l, pl.ds(0, tile_rows)] = buf[me_l]
    for side, (first, count) in ((-1, (2, 2)), (1, (4, 2))):

        @pl.when(jnp.logical_not(inner[side]))
        def _():
            low = plan.tiles[first][0]
            wide[:, low : low + count * BLOCK] = jnp.zeros((levels, count * BLOCK, width), BF16)


    for w in range(3):
        for p in range(latents):
            if plan.used[w] < LANES:
                fill = jnp.zeros((LANES - plan.used[w], width), BF16)
                kw[w, p, plan.used[w] :] = fill
                vw[w, p, plan.used[w] :] = fill
    for load in loads[6:11]:
        load.wait()
    lq_f = lqbuf[...].astype(F32)
    hm_f = hm[...].astype(F32)
    loads[11].wait()
    cq = (mm(lqbuf[...], b_query[...]) * inv_root).astype(BF16).astype(F32)
    masked = jnp.concatenate([cq[q : q + 1] * hm_f for q in range(latents)], axis=0).astype(BF16)
    loads[12].wait()
    kq[...] = mm_nt(b_kv[:, :width], masked).astype(BF16)
    loads[13].wait()
    loads[14].wait()

    def head(g):
        part = plan.parts[g]
        code_c = info[g * n : (g + 1) * n, 0:1]
        low = plan.tiles[part[0]][0]
        size = sum(plan.tiles[t][1] for t in part)
        exps, values = [], []
        for plane in plan.planes:
            tokens = [wide[l, low : low + size].astype(F32) for l in plane]
            tokens = jnp.concatenate(tokens, axis=0).astype(BF16)
            id_row = jnp.full((1, LANES), -1.0, F32)
            begin = 0
            for l in plane:
                for t in part:
                    meta = plan.tiles[t][0]
                    ids_at = 2 * LANES if g == 2 else 0
                    line = wide[l, meta : meta + BLOCK, ids_at : ids_at + LANES]
                    line = line.astype(F32)[BLOCK - 1 :]
                    id_row = jnp.where(lane >= begin, line, id_row)
                    begin += plan.tiles[t][1]
            id_row = id_row.astype(jnp.int32)
            code_r = jnp.where(id_row >= 0, codes[g : g + 1, :] + id_row, -1)
            pick = jnp.where(code_c == code_r, 1.0, 0.0)[:, :begin]
            keys_in = mm(pick.astype(BF16), tokens).astype(BF16)
            yield
            present = jnp.sum(pick, axis=1, keepdims=True)
            score = mm(keys_in, kq[...])
            values.append(mm(keys_in, b_kv[:, width:]))
            yield
            exps.append(jnp.exp(score) * present)
        norm = add_all(exps)
        norm = jnp.where(norm > 0.0, norm, 1.0)
        wide_weights = []
        for e in exps:
            share = (e / norm).astype(BF16).astype(F32)
            wide_weights.append(jnp.concatenate([share, jnp.zeros_like(share)], axis=1))
        mixers[g] = wide_weights, values

    def tail(g, picked):
        weights, values = mixers[g]
        low, high = picked[0] * width, (picked[-1] + 1) * width
        mixes = []
        for weight, v in zip(weights, values):
            cuts = []
            for p in picked:
                spread = []
                for c in range(width // LANES):
                    where = jnp.broadcast_to(p * HEADS + (c * LANES + lane) // head_dim, (n, LANES))
                    spread.append(jnp.take_along_axis(weight, where, axis=1))
                cuts.append(jnp.concatenate(spread, axis=1) * v)
            mixes.append(jnp.concatenate(cuts, axis=0))
        out = mm(add_all(mixes).astype(BF16), b_out[...])
        yield
        latent = jnp.concatenate(
            [out[k * n : (k + 1) * n] + lq_f[p : p + 1] for k, p in enumerate(picked)], axis=0
        )
        normed = layer_norm(latent, sgain[...]).astype(BF16)
        if g == 0:
            start[picked[0] * n : (picked[-1] + 1) * n] = latent
            own_normed[...] = normed
            return
        keys = mm(normed, b_qkv[:, width : 2 * width])
        values = mm(normed, b_qkv[:, 2 * width :])
        yield
        put(g, picked, keys, values)

    def put(g, picked, keys, values):
        for k, p in enumerate(picked):
            for w, first, size, base in plan.slots[g]:
                cut = slice(k * n + first, k * n + first + size)
                kw[w, p, base : base + size] = keys[cut].astype(BF16)
                vw[w, p, base : base + size] = values[cut].astype(BF16)

    lab_cols, lab_keys = {}, {}

    def labels_of(g):
        cells = slice(g * n, (g + 1) * n)
        tile_c = info[cells, 2:3]
        seg = jnp.zeros((n, LANES), F32)
        for t in plan.parts[g]:
            first = plan.tiles[t][0]
            line = wide[me_l, first : first + BLOCK, LANES : 2 * LANES].astype(F32)[BLOCK - 1 :]
            seg = jnp.where(tile_c == t, line, seg)
        lab_cols[g] = jnp.sum(jnp.where(lane == info[cells, 1:2], seg, 0.0), axis=1, keepdims=True)
        lab_keys[g] = lab_cols[g]
        if g == 2:
            outside = (tile_c < 4) & (me_o == 0) | (tile_c >= 4) & (me_o == lon_count - 1)
            lab_keys[g] = jnp.where(outside, -1.0, lab_cols[g])
        yield

    at_of = [sum(size for _, size in plan.q_spans[:w]) for w in range(3)]

    def view(groups, windows):
        for g in groups:
            yield from labels_of(g)
        for w in windows:
            first, size = plan.q_spans[w]
            keys = [
                jnp.where(lane == info[g * n : (g + 1) * n, 3 + w : 4 + w], lab_keys[g] + 1.0, 0.0)
                for g in sorted(lab_keys)
            ]
            keys = jnp.sum(add_all(keys), axis=0, keepdims=True) - 1.0
            seen = jnp.where(lab_cols[0][first : first + size] == keys, 1.0, 0.0)
            mask[at_of[w] : at_of[w] + size] = seen
            yield

    def allowed_of(w):
        return mask[at_of[w] : at_of[w] + plan.q_spans[w][1]]

    def ask():
        normed = own_normed[...]
        asked = mm(normed, b_qkv[:, :width])
        yield
        queries[...] = asked * inv_root
        keys = mm(normed, b_qkv[:, width : 2 * width])
        values = mm(normed, b_qkv[:, 2 * width :])
        yield
        put(0, halves[0], keys, values)

    def halo():
        yield from head(2)
        yield from tail(2, halves[0])

    found = {}
    units = [(g, 1) for g in range(width // LANES)]
    mixers = {}
    half = -(-latents // 2)
    halves = [list(range(latents))]
    for move in direct:
        if move[1] == 0:
            copies[move].wait_recv()
    for (dm, da, do), relay in relays.items():
        if dm and not da:
            pl.when(inner[do])(relay.start)
    for load in loads[15:]:
        load.start()
    run([head(0)])
    run([tail(0, picked) for picked in halves])
    for move in direct:
        if move[1]:
            copies[move].wait_recv()
    for (_, da, do), relay in relays.items():
        if da:
            pl.when(inner[do])(relay.start)
    def mate():
        yield from head(1)
        yield from tail(1, halves[0])

    run([mate(), ask(), view([0, 1], [1])])
    run([attention(plan, latents, queries, kw, vw, allowed_of, units, found)])
    for (dm, _, do), relay in relays.items():
        pl.when(inner[-do])(relay.wait_recv)
    run([halo(), view([2], [0, 2])])
    for (p, g, _), piece in found.items():
        early[p, :, g * LANES : (g + 1) * LANES] = piece

    for copy in copies.values():
        copy.wait_send()
    for (_, _, do), relay in relays.items():
        pl.when(inner[do])(relay.wait_send)
    for load in loads[15:]:
        load.wait()


def back_kernel(plan, start, queries, kw, vw, mask, early, gain, b_so, b_up, b_down, out, obuf, sems):
    width = b_so.shape[0]
    n = plan.own
    latents = start.shape[0] // n
    masks, at = [], 0
    for first, size in plan.q_spans:
        masks.append(mask[at : at + size])
        at += size
    found = {}
    row = lax.broadcasted_iota(jnp.int32, (8, 1), 0)

    def merged(p, g):
        tiles = []
        for r in range(0, n, 8):
            tile = None
            for w, (first, size) in enumerate(plan.q_spans):
                if plan.bounds[w] < r + 8 and plan.bounds[w + 1] > r:
                    here = found[p, g, w][r - first : r - first + 8]
                    tile = here if tile is None else jnp.where(row + r < plan.bounds[w], tile, here)
            tiles.append(tile)
        return jnp.concatenate(tiles, axis=0)

    whole = {}
    middle = n // 16 * 8 + 8
    parts = [(0, middle), (middle, n)] if middle < n else [(0, n)]
    runs, k = [], 0
    while k < n:
        i, j, w = plan.own_cells[k]
        size = 1
        while (
            k + size < n
            and plan.own_cells[k + size] == (i, j + size, w)
            and not any(k + size == low for low, _ in parts)
        ):
            size += 1
        runs.append((k, size, i * plan.cols + j))
        k += size
    writes = [
        pltpu.make_async_copy(
            obuf.at[pl.ds(first, size)], out.at[pl.ds(target, size)], sems.at[k]
        )
        for k, (first, size, target) in enumerate(runs)
    ]
    step = 512

    def finish():
        mix = jnp.concatenate([whole[p] for p in range(latents)], axis=0).astype(BF16)
        result = start[...] + mm(mix, b_so[...])
        mlp_in = layer_norm(result, gain[...]).astype(BF16)
        chunks = list(range(0, b_up.shape[1], step))
        ahead = mm(mlp_in, b_up[:, :step])
        for c in chunks:
            up = ahead
            if c + step < b_up.shape[1]:
                ahead = mm(mlp_in, b_up[:, c + step : c + 2 * step])
            act = up * (1.0 + lax.erf(up * math.sqrt(0.5))) * 0.5
            if c != chunks[-1]:
                result = result + mm(act.astype(BF16), b_down[c : c + step, :])
        for low, high in parts:
            cuts = [slice(p * n + low, p * n + high) for p in range(latents)]
            done = jnp.concatenate([act[cut] for cut in cuts], axis=0).astype(BF16)
            done = jnp.concatenate([result[cut] for cut in cuts], axis=0) + mm(done, b_down[c:, :])
            for p in range(latents):
                obuf[low:high, p, :] = done[p * (high - low) : (p + 1) * (high - low)]
            for write, (first, _, _) in zip(writes, runs):
                if low <= first < high:
                    write.start()

    groups = range(width // LANES)
    for p in range(latents):
        for g in groups:
            found[p, g, 1] = early[p, :, g * LANES : (g + 1) * LANES]
    units = [(g, w) for g in groups for w in (0, 2)]
    run([attention(plan, latents, queries, kw, vw, masks.__getitem__, units, found, 3)])
    for p in range(latents):
        whole[p] = jnp.concatenate([merged(p, g) for g in groups], axis=1)
    finish()
    for write in writes:
        write.wait()


def shards(
    sizes, names,
    patches, level_embed, embed_weight, block_ids, latent_queries, cross_gain, cross_query, cross_kv,
    cross_out, region_ids, swin_gain, swin_qkv, swin_out, mlp_gain, mlp_up, mlp_down,
):
    levels = sizes[0]
    _, bands, rows, cols, features = patches.shape
    assert bands == levels
    width = embed_weight.shape[1]
    latents = latent_queries.shape[0]
    plan = Plan(rows, cols, block_ids.shape[-1], levels)
    n = plan.own
    head_mask = np.arange(width)[None, :] // (width // HEADS) == np.arange(HEADS)[:, None]
    vmem = pl.BlockSpec(memory_space=pltpu.VMEM)
    hbm = pl.BlockSpec(memory_space=pl.ANY)
    moves = 6 * levels - 1
    q_rows = sum(size for _, size in plan.q_spans)
    handed = [
        ((latents * n, width), F32), ((latents * n, width), F32),
        ((3, latents, LANES, width), BF16), ((3, latents, LANES, width), BF16),
        ((q_rows, LANES), F32), ((latents, plan.q_spans[1][1], width), F32),
        (swin_out.shape, BF16), (mlp_up.shape, BF16), (mlp_down.shape, BF16),
    ]
    room = int(sum(math.prod(shape) * np.dtype(kind).itemsize for shape, kind in handed))
    inputs = (
        patches[0].transpose(1, 2, 0, 3), embed_weight, level_embed, block_ids, region_ids,
        cross_gain.reshape(1, -1), latent_queries, swin_gain.reshape(1, -1),
        jnp.asarray(plan.info), jnp.asarray(plan.row_code), jnp.asarray(head_mask, BF16),
    )
    weights = (cross_query, cross_kv, cross_out, swin_qkv)
    later = (swin_out, mlp_up, mlp_down)
    held = [pltpu.VMEM(x.shape, x.dtype) for x in inputs]
    held[3] = pltpu.SMEM(block_ids.shape, jnp.int32)
    outs = pl.pallas_call(
        functools.partial(front_kernel, plan, names, sizes),
        out_shape=[pltpu.VMEM(shape, kind) for shape, kind in handed],
        in_specs=[hbm] * 18,
        out_specs=[vmem] * len(handed),
        scratch_shapes=held
        + [pltpu.VMEM(w.shape, BF16) for w in weights]
        + [
            pltpu.VMEM((bands, plan.tile_rows, width), BF16),
            pltpu.VMEM((levels, plan.wide_rows, width), BF16),
            pltpu.VMEM((width, latents * HEADS), BF16),
            pltpu.VMEM((latents * n, width), BF16),
            pltpu.SemaphoreType.DMA((18,)),
            pltpu.SemaphoreType.DMA((-(-features // KCUT),)),
            pltpu.SemaphoreType.DMA((moves,)),
            pltpu.SemaphoreType.DMA((moves,)),
        ],
        compiler_params=pltpu.CompilerParams(
            collective_id=0, has_side_effects=True, vmem_limit_bytes=VMEM - room
        ),
        name="front",
    )(*inputs, *weights, *later)
    outs = [pltpu.with_memory_space_constraint(x, pltpu.VMEM) for x in outs]
    tokens = pl.pallas_call(
        functools.partial(back_kernel, plan),
        out_shape=jax.ShapeDtypeStruct((n, latents, width), F32),
        in_specs=[vmem] * 10,
        out_specs=hbm,
        scratch_shapes=[
            pltpu.VMEM((n, latents, width), F32),
            pltpu.SemaphoreType.DMA((4 * rows,)),
        ],
        compiler_params=pltpu.CompilerParams(vmem_limit_bytes=40 << 20),
        name="back",
    )(*outs[:6], mlp_gain.reshape(1, -1), *outs[6:])
    return tokens.reshape(rows, cols, latents, width).transpose(2, 0, 1, 3)


def solution(mesh):
    names = ("lvl", "lat", "lon")
    sizes = tuple(mesh.shape[name] for name in names)
    tiled = P("lvl", None, "lat", "lon", None)
    return jax.shard_map(
        functools.partial(shards, sizes, names),
        mesh=mesh,
        in_specs=(
            tiled, P("lvl", None), P(), tiled, P(), P(), P(), P(), P(), P(("lvl", "lat"), "lon"),
            P(), P(), P(), P(), P(), P(),
        ),
        out_specs=P(None, ("lvl", "lat"), "lon", None),
        check_vma=False,
    )
```

```python
import functools
import math

import jax
import jax.numpy as jnp
import numpy as np
from jax import lax
from jax.experimental import pallas as pl
from jax.experimental.pallas import tpu as pltpu
from jax.sharding import PartitionSpec as P

HEADS = 16
WIN_LAT = 6
BLOCK = 16
CODE = 64
KCUT = 256
AHEAD = 2
LANES = 128
VMEM = 63700000
MESH = pl.DeviceIdType.MESH
F32 = jnp.float32
BF16 = jnp.bfloat16


def layer_norm(tensor, gain_vec):
    average = jnp.mean(tensor, axis=-1, keepdims=True)
    centred = tensor - average
    spread = jnp.mean(centred * centred, axis=-1, keepdims=True)
    return centred * lax.rsqrt(spread + 1e-05) * gain_vec


def mm(a, b):
    return jnp.dot(a, b, preferred_element_type=F32)


def mm_nt(a, b):
    return lax.dot_general(a, b, (((1,), (1,)), ((), ())), preferred_element_type=F32)


def add_all(parts):
    total = parts[0]
    for part in parts[1:]:
        total = total + part
    return total


def span(low, high, total, unit):
    first = low // 8 * 8
    size = -(-(high - first) // unit) * unit
    return min(first, total - size), size


class Plan:
    def __init__(self, rows, cols, cap, levels):
        self.rows, self.cols, self.cap, self.levels = rows, cols, cap, levels
        m = self.margin = WIN_LAT // 2
        per = (BLOCK - 1) // cap
        assert per >= m and rows < CODE and rows * cols <= LANES and cols == 2 * WIN_LAT
        groups = [list(range(per))]
        groups += [list(range(c, min(c + per, cols - per))) for c in range(per, cols - per, per)]
        groups += [list(range(cols - per, cols))]
        sizes = [-(-len(group) * cap // 8) * 8 for group in groups]
        sizes[0] = sizes[-1] = BLOCK
        self.starts = [sum(sizes[:b]) for b in range(len(groups))]
        self.groups = groups
        self.tile_rows = sum(sizes)
        self.col_of = np.full(self.tile_rows, -1)
        for first, group in zip(self.starts, groups):
            for k, c in enumerate(group):
                self.col_of[first + k * cap : first + (k + 1) * cap] = c
        pitch = -(-self.tile_rows // BLOCK) * BLOCK
        self.tiles = [(0, self.tile_rows), (pitch, self.tile_rows)]
        self.tiles += [(2 * pitch + k * BLOCK, BLOCK) for k in range(4)]
        self.wide_rows = 2 * pitch + 4 * BLOCK
        depth = min(levels, levels * cap - rows + 1)
        self.planes = [list(range(levels))] if depth == 1 else [[l] for l in range(levels)]
        share = len(self.planes[0])
        self.parts = [[0], [1], [2, 3, 4, 5]]
        first, last = self.col_of[:BLOCK], self.col_of[-BLOCK:]
        cols_of_tile = [self.col_of, self.col_of, last, last, first, first]
        self.row_code = np.full((8, LANES), -100000, np.int32)
        for g, part in enumerate(self.parts):
            codes = [
                np.where(cols_of_tile[t] >= 0, (k * cols + cols_of_tile[t]) * CODE, -100000)
                for k, t in enumerate(part)
            ]
            codes = np.concatenate(codes * share)
            assert len(codes) <= LANES
            self.row_code[g, : len(codes)] = codes
        edges = [0, m, cols - m, cols]
        spans = [range(edges[w], edges[w + 1]) for w in range(3)]
        own = [(i, j, w) for w in range(3) for i in range(rows) for j in spans[w]]
        self.own_cells = own
        self.own = n = rows * cols
        bounds = np.cumsum([0] + [rows * len(s) for s in spans])
        self.bounds = [int(b) for b in bounds]
        cells = [(t, 0, i, j) for t in (0, 1) for i, j, _ in own]
        halo = [spans[2], spans[2], spans[0], spans[0]]
        cells += [(2 + k, k, i, j) for k in range(4) for i in range(rows) for j in halo[k]]
        self.count = len(cells)
        assert self.count == 3 * n and n % 8 == 0
        self.info = np.full((self.count, LANES), -1, np.int32)
        t, k, i, j = np.array(cells).T
        self.info[:, 0] = (k * cols + j) * CODE + i
        self.info[:, 1] = i * cols + j
        self.info[:, 2] = t
        self.q_spans = [span(bounds[w], bounds[w + 1], n, 8) for w in range(3)]
        self.slots = [[], [], []]
        half = 2 * rows * m
        ranges = {0: [(w, bounds[w], bounds[w + 1]) for w in range(3)]}
        ranges[1] = ranges[0]
        ranges[2] = [(0, 0, half), (2, half, 2 * half)]
        self.used = [0, 0, 0]
        for g in range(3):
            for w, low, high in ranges[g]:
                low, high = int(low), int(high)
                first, size = (int(x) for x in span(low, high, n, 16))
                base = self.used[w]
                self.slots[g].append((w, first, size, base))
                self.info[g * n + low : g * n + high, 3 + w] = base + np.arange(low, high) - first
                self.used[w] += size
        assert max(self.used) <= LANES


def attention(plan, latents, queries, kw, vw, allowed_of, units, found, early=AHEAD):
    width = queries.shape[1]
    head_dim = width // HEADS
    n = plan.own
    group = LANES // head_dim
    lane = lax.broadcasted_iota(jnp.int32, (1, LANES), 1)
    lane_head = [(lane >= h * head_dim) & (lane < (h + 1) * head_dim) for h in range(group)]
    low_half = lane < LANES // 2
    odd = add_all([jnp.where(lane_head[h], 1.0, 0.0) for h in range(1, group, 2)])
    halves = [(1.0 - odd).astype(BF16), odd.astype(BF16)]
    sets = {}
    for p in range(latents):
        sets.setdefault((p + 1) // 2, []).append(p)
    sets = list(sets.values())
    def scores(g, w):
        cut = slice(g * LANES, (g + 1) * LANES)
        first, size = plan.q_spans[w]
        raised = []
        for members in sets:
            parts = [queries[p * n + first : p * n + first + size, cut] for p in members]
            base = jnp.concatenate(parts, axis=0)
            if len(members) == 2:
                stack = jnp.concatenate([jnp.where(h, base, 0.0) for h in lane_head], axis=0)
                keys = jnp.concatenate([kw[w, p, :, cut] for p in members], axis=0)
            else:
                stack = jnp.concatenate(
                    [jnp.where(low_half, base, 0.0), jnp.where(low_half, 0.0, base)], axis=0
                )
                keys = jnp.concatenate([kw[w, members[0], :, cut] * h for h in halves], axis=0)
            raised.append(mm_nt(stack.astype(BF16), keys))
        return raised

    def mixed(g, w, raised):
        cut = slice(g * LANES, (g + 1) * LANES)
        first, size = plan.q_spans[w]
        weights = []
        for members, score in zip(sets, raised):
            allowed = jnp.concatenate([allowed_of(w)] * (score.shape[0] // size), axis=0) > 0.5
            left = jnp.where(allowed, jnp.exp(score[:, :LANES]), 0.0)
            right = jnp.where(allowed, jnp.exp(score[:, LANES:]), 0.0)
            if len(members) == 2:
                inverse = 1.0 / jnp.sum(left + right, axis=1, keepdims=True)
                left, right = left * inverse, right * inverse
            else:
                left = left * (1.0 / jnp.sum(left, axis=1, keepdims=True))
                right = right * (1.0 / jnp.sum(right, axis=1, keepdims=True))
            weights.append(jnp.concatenate([left, right], axis=1).astype(BF16))
        for members, weight in zip(sets, weights):
            many = len(members) * size
            if len(members) == 2:
                values = jnp.concatenate([vw[w, p, :, cut] for p in members], axis=0)
                total = mm(weight, values)
                piece = total[:many]
                for h in range(1, group):
                    piece = jnp.where(lane_head[h], total[h * many : (h + 1) * many], piece)
            else:
                values = jnp.concatenate([vw[w, members[0], :, cut] * h for h in halves], axis=0)
                total = mm(weight, values)
                piece = jnp.where(low_half, total[:many], total[many:])
            for k, p in enumerate(members):
                found[p, g, w] = piece[k * size : (k + 1) * size]

    ahead = [scores(*unit) for unit in units[:early]]
    yield
    for k, unit in enumerate(units):
        if k + early < len(units):
            ahead.append(scores(*units[k + early]))
        mixed(*unit, ahead.pop(0))
        yield


def run(works):
    waiting, live = [iter(work) for work in works], []
    while waiting or live:
        if waiting:
            live.append(waiting.pop(0))
        for work in list(live):
            if next(work, run) is run:
                live.remove(work)


def front_kernel(
    plan, names, sizes,
    patches, weight, level_embed, ids, labels, cross_gain, lq, swin_gain, info_in, code_in, hm_in,
    cross_query, cross_kv, cross_out, swin_qkv, swin_out, mlp_up, mlp_down,
    start, queries, kw, vw, mask, early, o_so, o_up, o_down,
    pbuf, wbuf, lebuf, idbuf, labbuf, cgain, lqbuf, sgain, info, codes, hm,
    b_query, b_kv, b_out, b_qkv, buf, wide, kq, own_normed, sems, wsems, send, recv,
):
    rows, cols, cap = plan.rows, plan.cols, plan.cap
    levels, lat_count, lon_count = sizes
    bands = levels
    width = weight.shape[1]
    latents = lq.shape[0]
    head_dim = width // HEADS
    inv_root = 1.0 / math.sqrt(head_dim)
    tile_rows = plan.tile_rows
    n = plan.own

    pairs = [
        (ids, idbuf), (labels, labbuf), (patches, pbuf), (weight, wbuf), (level_embed, lebuf),
        (cross_gain, cgain), (lq, lqbuf), (swin_gain, sgain), (info_in, info), (code_in, codes),
        (hm_in, hm), (cross_query, b_query), (cross_kv, b_kv), (cross_out, b_out),
        (swin_qkv, b_qkv), (swin_out, o_so), (mlp_up, o_up), (mlp_down, o_down),
    ]
    loads = [
        None if k == 3 else pltpu.make_async_copy(a, b, sems.at[k]) for k, (a, b) in enumerate(pairs)
    ]
    features = weight.shape[0]
    chunks = [(k, min(KCUT, features - k)) for k in range(0, features, KCUT)]
    pieces = [
        pltpu.make_async_copy(weight.at[pl.ds(k, size)], wbuf.at[pl.ds(k, size)], wsems.at[i])
        for i, (k, size) in enumerate(chunks)
    ]
    for k in (0, 1, 2):
        loads[k].start()
    for piece in pieces:
        piece.start()
    for k in (4, 5):
        loads[k].start()

    me_l, me_a, me_o = (lax.axis_index(name) for name in names)
    partner = me_a + 1 - 2 * lax.rem(me_a, 2)
    lats = (me_a, partner)
    lons = {
        0: me_o,
        1: lax.rem(me_o + 1, lon_count),
        -1: lax.rem(me_o + lon_count - 1, lon_count),
    }
    band_of = [lax.rem(me_l + dm, levels) for dm in range(levels)]
    direct = [(dm, 0) for dm in range(1, levels)] + [(dm, 1) for dm in range(levels)]
    targets = [(band_of[dm], lats[da], me_o) for dm, da in direct]
    sides = [(da, do) for da in (0, 1) for do in (1, -1)]
    beside = {(da, do): (me_l, lats[da], lons[do]) for da, do in sides}
    inner = {1: me_o < lon_count - 1, -1: me_o > 0}
    barrier = pltpu.get_barrier_semaphore()
    for target in targets:
        pl.semaphore_signal(barrier, inc=1, device_id=target, device_id_type=MESH)
    for do in (1, -1):

        @pl.when(inner[do])
        def _():
            pl.semaphore_signal(barrier, inc=1, device_id=beside[0, do], device_id_type=MESH)

    def step_of(inner_row):
        return add_all([(inner_row >= k * cap).astype(jnp.int32) for k in range(1, BLOCK // cap + 1)])

    def locate(place):
        inner_row, base, held = place, jnp.zeros_like(place), place < 0
        for first, group in zip(plan.starts, plan.groups):
            inner_row = jnp.where(place >= first, place - first, inner_row)
            base = jnp.where(place >= first, group[0], base)
            held = held | ((place >= first) & (place < first + cap * len(group)))
        step = step_of(inner_row)
        return base + step, inner_row - step * cap, held

    row = lax.broadcasted_iota(jnp.int32, (tile_rows, 1), 0)
    col_of, slot_of, used = locate(row)
    meta_row = (row == BLOCK - 1) | (row == tile_rows - 1)
    lane = lax.broadcasted_iota(jnp.int32, (1, LANES), 1)
    lane_row = lane
    for k in range(1, len(plan.planes[0])):
        lane_row = jnp.where(lane >= k * tile_rows, lane - k * tile_rows, lane_row)
    _, lane_slot, _ = locate(lane_row)
    lane_in = jnp.bitwise_and(lane, BLOCK - 1)
    halo_slot = lane_in - step_of(lane_in) * cap
    cell = lax.broadcasted_iota(jnp.int32, (LANES, 1), 0)
    cell_i = add_all([(cell >= k * cols).astype(jnp.int32) for k in range(1, rows)])
    cell_j = cell - cell_i * cols
    picked_j = lax.broadcasted_iota(jnp.int32, (LANES, cols), 1) == cell_j
    eye = lax.broadcasted_iota(jnp.int32, (LANES, LANES), 0) == lax.broadcasted_iota(
        jnp.int32, (LANES, LANES), 1
    )
    loads[0].wait()
    loads[1].wait()
    lab = labbuf[...].astype(F32)
    col_lab = jnp.zeros((LANES, cols), F32)
    for k in range(rows):
        col_lab = jnp.where(cell_i == k, lab[k : k + 1, :], col_lab)
    lab_col = jnp.sum(jnp.where(picked_j, col_lab, 0.0), axis=1, keepdims=True)
    lab_row = jnp.sum(jnp.where(eye, lab_col, 0.0), axis=0, keepdims=True)
    picks, metas = [], []
    cells_all = rows * cols * bands
    source = lax.broadcasted_iota(jnp.int32, (tile_rows, cells_all), 1)
    for band in range(bands):
        id_col = jnp.full((tile_rows, 1), -1, jnp.int32)
        id_row = jnp.full((1, LANES), -1, jnp.int32)
        halo_row = jnp.full((1, LANES), -1, jnp.int32)
        for s in range(cap):
            number = idbuf[0, band, 0, 0, s]
            id_col = jnp.where(slot_of == s, number, id_col)
            id_row = jnp.where(lane_slot == s, number, id_row)
            halo_row = jnp.where(halo_slot == s, number, halo_row)
        wanted = jnp.where(used & (id_col >= 0), (id_col * cols + col_of) * bands + band, -1)
        picks.append(jnp.where(source == wanted, 1.0, 0.0))
        pad = jnp.zeros((1, width - 3 * LANES), F32)
        metas.append(jnp.concatenate([id_row.astype(F32), lab_row, halo_row.astype(F32), pad], axis=1))
    pick = jnp.concatenate(picks, axis=0).astype(BF16)
    loads[2].wait()
    cells_in = pbuf[...].reshape(cells_all, patches.shape[-1])
    cells_in = mm(pick, cells_in).astype(BF16)
    products = []
    for piece, (k, size) in zip(pieces, chunks):
        piece.wait()
        products.append(mm(cells_in[:, k : k + size], wbuf[k : k + size]))
    for load in loads[6:15]:
        load.start()
    loads[4].wait()
    embedded = (add_all(products) + lebuf[...]).astype(BF16).astype(F32)
    loads[5].wait()
    listed = layer_norm(embedded, cgain[...])
    for band in range(bands):
        part = listed[band * tile_rows : (band + 1) * tile_rows]
        buf[band] = jnp.where(meta_row, metas[band], part).astype(BF16)
    pl.semaphore_wait(barrier, len(targets) + add_all([inner[do].astype(jnp.int32) for do in (1, -1)]))
    copies = {}
    for k, (dm, da) in enumerate(direct):
        copies[dm, da] = pltpu.make_async_remote_copy(
            src_ref=buf.at[band_of[dm]],
            dst_ref=wide.at[me_l, pl.ds(plan.tiles[da][0], tile_rows)],
            send_sem=send.at[k],
            recv_sem=recv.at[k],
            device_id=targets[k],
            device_id_type=MESH,
        )
    relays = {}
    for dm in range(levels):
        level = lax.rem(me_l + dm, levels)
        for da, do in sides:
            origin = tile_rows - BLOCK if do == 1 else 0
            target = plan.tiles[(2 if do == 1 else 4) + da][0]
            slot = len(direct) + len(relays)
            held_by_me = da == 1
            relays[dm, da, do] = pltpu.make_async_remote_copy(
                src_ref=wide.at[level, pl.ds(plan.tiles[1][0] + origin, BLOCK)]
                if held_by_me
                else (wide if dm else buf).at[level, pl.ds(origin, BLOCK)],
                dst_ref=wide.at[level, pl.ds(target, BLOCK)],
                send_sem=send.at[slot],
                recv_sem=recv.at[slot],
                device_id=beside[0, do],
                device_id_type=MESH,
            )
    near = [move for move in direct if move[0] == 0 or move[1] == 0]
    far = [move for move in direct if move not in near]
    for move in far:
        copies[move].start()
    for move in near:
        copies[move].start()
    for do in (1, -1):
        pl.when(inner[do])(relays[0, 0, do].start)
    wide[me_l, pl.ds(0, tile_rows)] = buf[me_l]
    for side, (first, count) in ((-1, (2, 2)), (1, (4, 2))):

        @pl.when(jnp.logical_not(inner[side]))
        def _():
            low = plan.tiles[first][0]
            wide[:, low : low + count * BLOCK] = jnp.zeros((levels, count * BLOCK, width), BF16)


    for w in range(3):
        for p in range(latents):
            if plan.used[w] < LANES:
                fill = jnp.zeros((LANES - plan.used[w], width), BF16)
                kw[w, p, plan.used[w] :] = fill
                vw[w, p, plan.used[w] :] = fill
    for load in loads[6:11]:
        load.wait()
    lq_f = lqbuf[...].astype(F32)
    hm_f = hm[...].astype(F32)
    loads[11].wait()
    cq = (mm(lqbuf[...], b_query[...]) * inv_root).astype(BF16).astype(F32)
    masked = jnp.concatenate([cq[q : q + 1] * hm_f for q in range(latents)], axis=0).astype(BF16)
    loads[12].wait()
    kq[...] = mm_nt(b_kv[:, :width], masked).astype(BF16)
    loads[13].wait()
    loads[14].wait()

    def head(g):
        part = plan.parts[g]
        code_c = info[g * n : (g + 1) * n, 0:1]
        low = plan.tiles[part[0]][0]
        size = sum(plan.tiles[t][1] for t in part)
        exps, values = [], []
        for plane in plan.planes:
            tokens = [wide[l, low : low + size].astype(F32) for l in plane]
            tokens = jnp.concatenate(tokens, axis=0).astype(BF16)
            id_row = jnp.full((1, LANES), -1.0, F32)
            begin = 0
            for l in plane:
                for t in part:
                    meta = plan.tiles[t][0]
                    ids_at = 2 * LANES if g == 2 else 0
                    line = wide[l, meta : meta + BLOCK, ids_at : ids_at + LANES]
                    line = line.astype(F32)[BLOCK - 1 :]
                    id_row = jnp.where(lane >= begin, line, id_row)
                    begin += plan.tiles[t][1]
            id_row = id_row.astype(jnp.int32)
            code_r = jnp.where(id_row >= 0, codes[g : g + 1, :] + id_row, -1)
            pick = jnp.where(code_c == code_r, 1.0, 0.0)[:, :begin]
            keys_in = mm(pick.astype(BF16), tokens).astype(BF16)
            yield
            present = jnp.sum(pick, axis=1, keepdims=True)
            score = mm(keys_in, kq[...])
            values.append(mm(keys_in, b_kv[:, width:]))
            yield
            exps.append(jnp.exp(score) * present)
        norm = add_all(exps)
        norm = jnp.where(norm > 0.0, norm, 1.0)
        wide_weights = []
        for e in exps:
            share = (e / norm).astype(BF16).astype(F32)
            wide_weights.append(jnp.concatenate([share, jnp.zeros_like(share)], axis=1))
        mixers[g] = wide_weights, values

    def tail(g, picked):
        weights, values = mixers[g]
        low, high = picked[0] * width, (picked[-1] + 1) * width
        mixes = []
        for weight, v in zip(weights, values):
            cuts = []
            for p in picked:
                spread = []
                for c in range(width // LANES):
                    where = jnp.broadcast_to(p * HEADS + (c * LANES + lane) // head_dim, (n, LANES))
                    spread.append(jnp.take_along_axis(weight, where, axis=1))
                cuts.append(jnp.concatenate(spread, axis=1) * v)
            mixes.append(jnp.concatenate(cuts, axis=0))
        out = mm(add_all(mixes).astype(BF16), b_out[...])
        yield
        latent = jnp.concatenate(
            [out[k * n : (k + 1) * n] + lq_f[p : p + 1] for k, p in enumerate(picked)], axis=0
        )
        normed = layer_norm(latent, sgain[...]).astype(BF16)
        if g == 0:
            start[picked[0] * n : (picked[-1] + 1) * n] = latent
            own_normed[...] = normed
            return
        keys = mm(normed, b_qkv[:, width : 2 * width])
        values = mm(normed, b_qkv[:, 2 * width :])
        yield
        put(g, picked, keys, values)

    def put(g, picked, keys, values):
        for k, p in enumerate(picked):
            for w, first, size, base in plan.slots[g]:
                cut = slice(k * n + first, k * n + first + size)
                kw[w, p, base : base + size] = keys[cut].astype(BF16)
                vw[w, p, base : base + size] = values[cut].astype(BF16)

    lab_cols, lab_keys = {}, {}

    def labels_of(g):
        cells = slice(g * n, (g + 1) * n)
        tile_c = info[cells, 2:3]
        seg = jnp.zeros((n, LANES), F32)
        for t in plan.parts[g]:
            first = plan.tiles[t][0]
            line = wide[me_l, first : first + BLOCK, LANES : 2 * LANES].astype(F32)[BLOCK - 1 :]
            seg = jnp.where(tile_c == t, line, seg)
        lab_cols[g] = jnp.sum(jnp.where(lane == info[cells, 1:2], seg, 0.0), axis=1, keepdims=True)
        lab_keys[g] = lab_cols[g]
        if g == 2:
            outside = (tile_c < 4) & (me_o == 0) | (tile_c >= 4) & (me_o == lon_count - 1)
            lab_keys[g] = jnp.where(outside, -1.0, lab_cols[g])
        yield

    at_of = [sum(size for _, size in plan.q_spans[:w]) for w in range(3)]

    def view(groups, windows):
        for g in groups:
            yield from labels_of(g)
        for w in windows:
            first, size = plan.q_spans[w]
            keys = [
                jnp.where(lane == info[g * n : (g + 1) * n, 3 + w : 4 + w], lab_keys[g] + 1.0, 0.0)
                for g in sorted(lab_keys)
            ]
            keys = jnp.sum(add_all(keys), axis=0, keepdims=True) - 1.0
            seen = jnp.where(lab_cols[0][first : first + size] == keys, 1.0, 0.0)
            mask[at_of[w] : at_of[w] + size] = seen
            yield

    def allowed_of(w):
        return mask[at_of[w] : at_of[w] + plan.q_spans[w][1]]

    def ask():
        normed = own_normed[...]
        asked = mm(normed, b_qkv[:, :width])
        yield
        queries[...] = asked * inv_root
        keys = mm(normed, b_qkv[:, width : 2 * width])
        values = mm(normed, b_qkv[:, 2 * width :])
        yield
        put(0, halves[0], keys, values)

    def halo():
        yield from head(2)
        yield from tail(2, halves[0])

    found = {}
    units = [(g, 1) for g in range(width // LANES)]
    mixers = {}
    half = -(-latents // 2)
    halves = [list(range(latents))]
    for move in direct:
        if move[1] == 0:
            copies[move].wait_recv()
    for (dm, da, do), relay in relays.items():
        if dm and not da:
            pl.when(inner[do])(relay.start)
    for move in direct:
        if move[1]:
            copies[move].wait_recv()
    for (_, da, do), relay in relays.items():
        if da:
            pl.when(inner[do])(relay.start)
    for load in loads[15:]:
        load.start()
    run([head(0)])
    run([tail(0, picked) for picked in halves])
    def mate():
        yield from head(1)
        yield from tail(1, halves[0])

    run([mate(), ask(), view([0, 1], [1])])
    run([attention(plan, latents, queries, kw, vw, allowed_of, units, found)])
    for (dm, _, do), relay in relays.items():
        pl.when(inner[-do])(relay.wait_recv)
    run([halo(), view([2], [0, 2])])
    for (p, g, _), piece in found.items():
        early[p, :, g * LANES : (g + 1) * LANES] = piece

    for copy in copies.values():
        copy.wait_send()
    for (_, _, do), relay in relays.items():
        pl.when(inner[do])(relay.wait_send)
    for load in loads[15:]:
        load.wait()


def back_kernel(plan, start, queries, kw, vw, mask, early, gain, b_so, b_up, b_down, out, obuf, sems):
    width = b_so.shape[0]
    n = plan.own
    latents = start.shape[0] // n
    masks, at = [], 0
    for first, size in plan.q_spans:
        masks.append(mask[at : at + size])
        at += size
    found = {}
    row = lax.broadcasted_iota(jnp.int32, (8, 1), 0)

    def merged(p, g):
        tiles = []
        for r in range(0, n, 8):
            tile = None
            for w, (first, size) in enumerate(plan.q_spans):
                if plan.bounds[w] < r + 8 and plan.bounds[w + 1] > r:
                    here = found[p, g, w][r - first : r - first + 8]
                    tile = here if tile is None else jnp.where(row + r < plan.bounds[w], tile, here)
            tiles.append(tile)
        return jnp.concatenate(tiles, axis=0)

    whole = {}
    middle = n // 16 * 8 + 8
    parts = [(0, middle), (middle, n)] if middle < n else [(0, n)]
    runs, k = [], 0
    while k < n:
        i, j, w = plan.own_cells[k]
        size = 1
        while (
            k + size < n
            and plan.own_cells[k + size] == (i, j + size, w)
            and not any(k + size == low for low, _ in parts)
        ):
            size += 1
        runs.append((k, size, i * plan.cols + j))
        k += size
    writes = [
        pltpu.make_async_copy(
            obuf.at[pl.ds(first, size)], out.at[pl.ds(target, size)], sems.at[k]
        )
        for k, (first, size, target) in enumerate(runs)
    ]
    step = 512

    def finish():
        mix = jnp.concatenate([whole[p] for p in range(latents)], axis=0).astype(BF16)
        result = start[...] + mm(mix, b_so[...])
        mlp_in = layer_norm(result, gain[...]).astype(BF16)
        chunks = list(range(0, b_up.shape[1], step))
        ahead = mm(mlp_in, b_up[:, :step])
        for c in chunks:
            up = ahead
            if c + step < b_up.shape[1]:
                ahead = mm(mlp_in, b_up[:, c + step : c + 2 * step])
            act = up * (1.0 + lax.erf(up * math.sqrt(0.5))) * 0.5
            if c != chunks[-1]:
                result = result + mm(act.astype(BF16), b_down[c : c + step, :])
        for low, high in parts:
            cuts = [slice(p * n + low, p * n + high) for p in range(latents)]
            done = jnp.concatenate([act[cut] for cut in cuts], axis=0).astype(BF16)
            done = jnp.concatenate([result[cut] for cut in cuts], axis=0) + mm(done, b_down[c:, :])
            for p in range(latents):
                obuf[low:high, p, :] = done[p * (high - low) : (p + 1) * (high - low)]
            for write, (first, _, _) in zip(writes, runs):
                if low <= first < high:
                    write.start()

    groups = range(width // LANES)
    for p in range(latents):
        for g in groups:
            found[p, g, 1] = early[p, :, g * LANES : (g + 1) * LANES]
    units = [(g, w) for g in groups for w in (0, 2)]
    run([attention(plan, latents, queries, kw, vw, masks.__getitem__, units, found, 3)])
    for p in range(latents):
        whole[p] = jnp.concatenate([merged(p, g) for g in groups], axis=1)
    finish()
    for write in writes:
        write.wait()


def shards(
    sizes, names,
    patches, level_embed, embed_weight, block_ids, latent_queries, cross_gain, cross_query, cross_kv,
    cross_out, region_ids, swin_gain, swin_qkv, swin_out, mlp_gain, mlp_up, mlp_down,
):
    levels = sizes[0]
    _, bands, rows, cols, features = patches.shape
    assert bands == levels
    width = embed_weight.shape[1]
    latents = latent_queries.shape[0]
    plan = Plan(rows, cols, block_ids.shape[-1], levels)
    n = plan.own
    head_mask = np.arange(width)[None, :] // (width // HEADS) == np.arange(HEADS)[:, None]
    vmem = pl.BlockSpec(memory_space=pltpu.VMEM)
    hbm = pl.BlockSpec(memory_space=pl.ANY)
    moves = 6 * levels - 1
    q_rows = sum(size for _, size in plan.q_spans)
    handed = [
        ((latents * n, width), F32), ((latents * n, width), F32),
        ((3, latents, LANES, width), BF16), ((3, latents, LANES, width), BF16),
        ((q_rows, LANES), F32), ((latents, plan.q_spans[1][1], width), F32),
        (swin_out.shape, BF16), (mlp_up.shape, BF16), (mlp_down.shape, BF16),
    ]
    room = int(sum(math.prod(shape) * np.dtype(kind).itemsize for shape, kind in handed))
    inputs = (
        patches[0].transpose(1, 2, 0, 3), embed_weight, level_embed, block_ids, region_ids,
        cross_gain.reshape(1, -1), latent_queries, swin_gain.reshape(1, -1),
        jnp.asarray(plan.info), jnp.asarray(plan.row_code), jnp.asarray(head_mask, BF16),
    )
    weights = (cross_query, cross_kv, cross_out, swin_qkv)
    later = (swin_out, mlp_up, mlp_down)
    held = [pltpu.VMEM(x.shape, x.dtype) for x in inputs]
    held[3] = pltpu.SMEM(block_ids.shape, jnp.int32)
    outs = pl.pallas_call(
        functools.partial(front_kernel, plan, names, sizes),
        out_shape=[pltpu.VMEM(shape, kind) for shape, kind in handed],
        in_specs=[hbm] * 18,
        out_specs=[vmem] * len(handed),
        scratch_shapes=held
        + [pltpu.VMEM(w.shape, BF16) for w in weights]
        + [
            pltpu.VMEM((bands, plan.tile_rows, width), BF16),
            pltpu.VMEM((levels, plan.wide_rows, width), BF16),
            pltpu.VMEM((width, latents * HEADS), BF16),
            pltpu.VMEM((latents * n, width), BF16),
            pltpu.SemaphoreType.DMA((18,)),
            pltpu.SemaphoreType.DMA((-(-features // KCUT),)),
            pltpu.SemaphoreType.DMA((moves,)),
            pltpu.SemaphoreType.DMA((moves,)),
        ],
        compiler_params=pltpu.CompilerParams(
            collective_id=0, has_side_effects=True, vmem_limit_bytes=VMEM - room
        ),
        name="front",
    )(*inputs, *weights, *later)
    outs = [pltpu.with_memory_space_constraint(x, pltpu.VMEM) for x in outs]
    tokens = pl.pallas_call(
        functools.partial(back_kernel, plan),
        out_shape=jax.ShapeDtypeStruct((n, latents, width), F32),
        in_specs=[vmem] * 10,
        out_specs=hbm,
        scratch_shapes=[
            pltpu.VMEM((n, latents, width), F32),
            pltpu.SemaphoreType.DMA((4 * rows,)),
        ],
        compiler_params=pltpu.CompilerParams(vmem_limit_bytes=40 << 20),
        name="back",
    )(*outs[:6], mlp_gain.reshape(1, -1), *outs[6:])
    return tokens.reshape(rows, cols, latents, width).transpose(2, 0, 1, 3)


def solution(mesh):
    names = ("lvl", "lat", "lon")
    sizes = tuple(mesh.shape[name] for name in names)
    tiled = P("lvl", None, "lat", "lon", None)
    return jax.shard_map(
        functools.partial(shards, sizes, names),
        mesh=mesh,
        in_specs=(
            tiled, P("lvl", None), P(), tiled, P(), P(), P(), P(), P(), P(("lvl", "lat"), "lon"),
            P(), P(), P(), P(), P(), P(),
        ),
        out_specs=P(None, ("lvl", "lat"), "lon", None),
        check_vma=False,
    )
```
